32 devices in a mesh: dp: 8 (over y, x, core), ctx: 4 (over z).
Axes of the slice: x: 2, y: 2, z: 4, core: 2. Of those that a mesh axis runs over, the one named last changes fastest.
Arguments:
- layer_in: bfloat16 [8, 2, 1, 1024, 896], P('dp', None, None, 'ctx'), may hold values from -6 to 6
- doc_ids: int32 [8, 2, 1, 1024], P('dp'), may hold values from 0 to 7, never falling along the last dimension, each value on 1 to 512 neighbouring positions
- cotangent: bfloat16 [8, 2, 1, 1024, 896], P('dp', None, None, 'ctx'), may hold values from -6 to 6
- first_gain: bfloat16 [896], P(('dp', 'ctx')), may hold values from 0.099609375 to 1.8984375
- query_weight: bfloat16 [896, 896], P(('dp', 'ctx')), may hold values from -0.1875 to 0.1875
- query_bias: bfloat16 [896], P(('dp', 'ctx')), may hold values from -3 to 3
- key_weight: bfloat16 [896, 128], P(('dp', 'ctx')), may hold values from -0.1875 to 0.1875
- key_bias: bfloat16 [128], P(('dp', 'ctx')), may hold values from -3 to 3
- value_weight: bfloat16 [896, 128], P(('dp', 'ctx')), may hold values from -0.1875 to 0.1875
- value_bias: bfloat16 [128], P(('dp', 'ctx')), may hold values from -3 to 3
- out_weight: bfloat16 [896, 896], P(('dp', 'ctx')), may hold values from -1 to 1
- second_gain: bfloat16 [896], P(('dp', 'ctx')), may hold values from 0.099609375 to 1.8984375
- gate_weight: bfloat16 [896, 4864], P('dp', 'ctx'), may hold values from -0.1875 to 0.1875
- up_weight: bfloat16 [896, 4864], P('dp', 'ctx'), may hold values from -0.1875 to 0.1875
- down_weight: bfloat16 [4864, 896], P('ctx', 'dp'), may hold values from -0.078125 to 0.078125
Outputs:
- layer_out: bfloat16 [8, 2, 1, 1024, 896], P('dp', None, None, 'ctx')
- input_grad: float32 [8, 2, 1, 1024, 896], P('dp', None, None, 'ctx')
- first_gain_grad: float32 [896], P(('dp', 'ctx'))
- query_weight_grad: float32 [896, 896], P(('dp', 'ctx'))
- query_bias_grad: float32 [896], P(('dp', 'ctx'))
- key_weight_grad: float32 [896, 128], P(('dp', 'ctx'))
- key_bias_grad: float32 [128], P(('dp', 'ctx'))
- value_weight_grad: float32 [896, 128], P(('dp', 'ctx'))
- value_bias_grad: float32 [128], P(('dp', 'ctx'))
- out_weight_grad: float32 [896, 896], P(('dp', 'ctx'))
- second_gain_grad: float32 [896], P(('dp', 'ctx'))
- gate_weight_grad: float32 [896, 4864], P('dp', 'ctx')
- up_weight_grad: float32 [896, 4864], P('dp', 'ctx')
- down_weight_grad: float32 [4864, 896], P('ctx', 'dp')
The draws below stay inside these ranges and needn't reach their ends.
Inputs may be any that keep to these rules, and one draw needn't show every extreme that they name: `doc_ids`: along each sequence the document numbers never fall, every number from 0 to 7 occurs, and no document holds more than 512 tokens; some document holds exactly that many.
All inputs are finite; a program needn't handle non-finite values.
Results may differ from the reference program's by a relative error of at most 0.017.
Values may be sent and summed in bfloat16 or wider, within the bound.
No kernel may reach another device: no remote copies, remote signals or barrier semaphores. Data moves between devices by JAX's collectives and lax.ppermute only.
A program may use at most 192 MiB of HBM per device.

```python
import math
import jax
import jax.numpy as jnp
import numpy as np
from jax import lax

D = 896
HEADS = 14
KV_HEADS = 2
HEAD = 64
FF = 4864
SEQ = 1024
DOCS = 8
MICRO = 2
SEQS = 1
QD = 896
KVD = 128
N_DP = 8


def with_spikes(values, stream_key, source, target, parts, factor):
    def block_of(position):
        return (jnp.arange(values.shape[position]) // (values.shape[position] // parts)).reshape((-1,) + (1,) * (values.ndim - 1 - position))

    first = jax.random.permutation(stream_key, parts)[block_of(target)]
    far = (block_of(target) + parts // 2) % parts
    return jnp.where((block_of(source) == first) | (block_of(source) == far), factor * values, values)


def block_levels(rng, shape, shards, least, high):
    def one(position, shards_of):
        heights = jax.random.uniform(jax.random.fold_in(jax.random.fold_in(rng, 6), position), (shards_of,), jnp.float32, least / len(shards), high / len(shards))
        return jnp.repeat(jnp.exp(heights), shape[position] // shards_of).reshape((-1,) + (1,) * (len(shape) - position - 1))

    gain = one(*shards[0])
    for cut in shards[1:]:
        gain = gain * one(*cut)
    return gain


def split_up(amount, total, limit, lean):
    loads = [(1 << 20) // math.isqrt(grade ** lean) + 1 for grade in range(2, amount + 1)]
    rest, holding = total - limit - (amount - 1), [1] * (amount - 1)
    while rest > 0:
        free = [i for i in range(amount - 1) if holding[i] < limit]
        mass, left = sum([loads[i] for i in free]), rest
        for i in free:
            addition = min(limit - holding[i], max(1, left * loads[i] // mass), rest)
            holding[i] = holding[i] + addition
            rest = rest - addition
    return np.array([limit] + holding)


def uneven_parts(rng, count, total, reach, lean):
    if count == 2:
        one = jax.random.randint(rng, (), max(1, total - reach), min(reach, total - 1) + 1)
        return jnp.stack([one, total - one])
    sizes = jnp.asarray(split_up(count, total, reach, lean), jnp.int32)
    couples = (count - 1) // 2
    donor, receiver = sizes[1:1 + 2 * couples:2], sizes[2:2 + 2 * couples:2]
    margin = jnp.minimum(donor - 1, reach - receiver)
    passed = jax.random.randint(jax.random.fold_in(rng, 1), (couples,), 0, 1 << 20) % (margin + 1)
    sizes = sizes.at[1:1 + 2 * couples:2].set(donor - passed).at[2:2 + 2 * couples:2].set(receiver + passed)
    return sizes[jax.random.permutation(jax.random.fold_in(rng, 2), count)]


def scatter_about(own_key, dims, width, bound, pieces=(), held_as=jnp.bfloat16):
    entries = width * jax.random.normal(own_key, dims, jnp.float32)
    if pieces:
        entries = entries * block_levels(own_key, dims, pieces, -0.22, 0.18)
    return jnp.clip(entries, -bound, bound).astype(held_as)


def bell_draw_with(key, shape, width, limit, cuts, heavy, held_as=jnp.bfloat16):
    values = width * jax.random.normal(key, shape, jnp.float32)
    if cuts:
        values = values * block_levels(key, shape, cuts, -0.22, 0.18)
    return jnp.clip(with_spikes(values, jax.random.fold_in(key, 3), *heavy), -limit, limit).astype(held_as)


def setup_inputs(seed: int = 0) -> dict:
    key_of = jax.random.split(jax.random.key(seed), 16)
    return {
        "layer_in": scatter_about(key_of[0], (N_DP, MICRO, SEQS, SEQ, D), 1.0, 6.0, ((0, 8), (3, 4))),
        "doc_ids": jax.vmap(lambda own: jnp.searchsorted(jnp.cumsum(uneven_parts(own, DOCS, SEQ, SEQ // 2, 2)), jnp.arange(SEQ), side="right"))(jax.random.split(key_of[1], N_DP * MICRO * SEQS)).reshape((N_DP, MICRO, SEQS, SEQ)).astype(jnp.int32),
        "cotangent": bell_draw_with(key_of[2], (N_DP, MICRO, SEQS, SEQ, D), 1.0, 6.0, ((0, 8), (3, 4)), (0, 4, 8, 2.0)),
        "first_gain": jnp.clip(1.0 + 0.18 * jax.random.normal(key_of[3], (D,), jnp.float32), 0.099609375, 1.8984375).astype(jnp.bfloat16),
        "query_weight": scatter_about(key_of[4], (D, QD), D ** -0.5, 0.1875, ((0, 32),)),
        "query_bias": scatter_about(key_of[5], (QD,), 0.5, 3.0, ((0, 32),)),
        "key_weight": scatter_about(key_of[6], (D, KVD), D ** -0.5, 0.1875, ((0, 32),)),
        "key_bias": scatter_about(key_of[7], (KVD,), 0.5, 3.0, ((0, 32),)),
        "value_weight": scatter_about(key_of[8], (D, KVD), D ** -0.5, 0.1875, ((0, 32),)),
        "value_bias": scatter_about(key_of[9], (KVD,), 0.5, 3.0, ((0, 32),)),
        "out_weight": scatter_about(key_of[10], (QD, D), (QD // 32) ** -0.5, 1.0, ((0, 32),)),
        "second_gain": jnp.clip(1.0 + 0.18 * jax.random.normal(key_of[11], (D,), jnp.float32), 0.099609375, 1.8984375).astype(jnp.bfloat16),
        "gate_weight": scatter_about(key_of[12], (D, FF), D ** -0.5, 0.1875, ((0, 8), (1, 4))),
        "up_weight": scatter_about(key_of[13], (D, FF), D ** -0.5, 0.1875, ((0, 8), (1, 4))),
        "down_weight": scatter_about(key_of[14], (FF, D), FF ** -0.5, 0.078125, ((0, 4), (1, 8))),
    }


@jax.custom_vjp
def low(v):
    return lax.optimization_barrier(v.astype(jnp.bfloat16)).astype(jnp.float32)

@jax.custom_vjp
def low_back(v):
    return v

def low_keep(v):
    return (low(v), None)

def low_pass(kept, grad):
    return (grad,)

def back_keep(v):
    return (v, None)

def back_low(kept, grad):
    return (low(grad),)
low.defvjp(low_keep, low_pass)
low_back.defvjp(back_keep, back_low)
epsilon = 1e-06
theta = 10000.0
masked = -1e+30

def rotation(positions, head_size):
    exponent = jnp.arange(head_size // 2, dtype=jnp.float32) * (2.0 / head_size)
    frequency = jnp.power(jnp.float32(theta), -exponent)
    angle = positions.astype(jnp.float32)[:, None] * frequency[None, :]
    angle = jnp.concatenate([angle, angle], axis=-1)
    return (jnp.cos(angle)[:, None, :], jnp.sin(angle)[:, None, :])

def turned(values_in):
    half_width = values_in.shape[-1] // 2
    return jnp.concatenate([-values_in[..., half_width:], values_in[..., :half_width]], axis=-1)

def rotate(values_in, cosines, sines):
    return values_in * cosines + turned(values_in) * sines

def scaled(values_in):
    return lax.rsqrt(lax.optimization_barrier(jnp.mean(values_in * values_in, axis=-1, keepdims=True)) + epsilon)

def product(left, right):
    return jnp.dot(left, right, precision=lax.Precision.HIGHEST)

def one_sequence(tokens, documents, params):
    gain_one, w_query, b_query, w_key, b_key, w_value, b_value, w_out, gain_two, w_gate, w_up, w_down = params
    key_count = tokens.shape[0]
    index_rows = jnp.arange(key_count, dtype=jnp.int32)
    earlier = lax.optimization_barrier(jnp.sum((documents[None, :] < documents[:, None]).astype(jnp.int32), axis=1))
    cosines, sines = rotation(index_rows - earlier, HEAD)
    allowed = (documents[:, None] == documents[None, :]) & (index_rows[None, :] <= index_rows[:, None])
    normed_one = low(tokens * scaled(tokens) * gain_one)
    queries = low_back(product(normed_one, w_query) + b_query)
    keys_pre = low_back(product(normed_one, w_key) + b_key)
    values_low = low(low_back(product(normed_one, w_value) + b_value)).reshape(key_count, KV_HEADS, HEAD)
    rot_query = low(rotate(queries.reshape(key_count, HEADS, HEAD), cosines, sines))
    rot_query = rot_query.reshape(key_count, KV_HEADS, HEADS // KV_HEADS, HEAD)
    rot_keys = low(rotate(keys_pre.reshape(key_count, KV_HEADS, HEAD), cosines, sines))
    scores = jnp.einsum('qkgd,skd->kgqs', rot_query, rot_keys, precision=lax.Precision.HIGHEST) * HEAD ** (-0.5)
    scores = jnp.where(allowed, low_back(scores), masked)
    largest = lax.optimization_barrier(jnp.max(scores, axis=-1, keepdims=True))
    exponent = jnp.exp(scores - largest)
    soft_weights = low(exponent / lax.optimization_barrier(jnp.sum(exponent, axis=-1, keepdims=True)))
    mixed_heads = jnp.einsum('kgqs,skd->qkgd', soft_weights, values_low, precision=lax.Precision.HIGHEST)
    mixed_heads = low(low_back(mixed_heads.reshape(key_count, HEADS * HEAD)))
    middle = tokens + low_back(product(mixed_heads, w_out))
    normed_two = low(middle * scaled(middle) * gain_two)
    gate_pre = low_back(product(normed_two, w_gate))
    up_pre = low_back(product(normed_two, w_up))
    activated = low(gate_pre * jax.nn.sigmoid(gate_pre) * up_pre)
    return middle + low_back(product(activated, w_down))

def reference(layer_in, doc_ids, cotangent, first_gain, query_weight, query_bias, key_weight, key_bias, value_weight, value_bias, out_weight, second_gain, gate_weight, up_weight, down_weight):
    params = tuple((weight_arg.astype(jnp.float32) for weight_arg in (first_gain, query_weight, query_bias, key_weight, key_bias, value_weight, value_bias, out_weight, second_gain, gate_weight, up_weight, down_weight)))
    tokens = layer_in.astype(jnp.float32).reshape(-1, SEQ, D)
    documents = doc_ids.reshape(-1, SEQ)
    upstream = cotangent.astype(jnp.float32).reshape(-1, SEQ, D)

    def forward(tokens_in, params_in):
        seq_step = jax.checkpoint(one_sequence)
        return lax.map(lambda item_pair: seq_step(item_pair[0], item_pair[1], params_in), (tokens_in, documents))
    result, pullback = jax.vjp(forward, tokens, params)
    token_grad, weight_grads = pullback(upstream)
    return (result.astype(jnp.bfloat16).reshape(layer_in.shape), token_grad.reshape(layer_in.shape), weight_grads[0], weight_grads[1], weight_grads[2], weight_grads[3], weight_grads[4], weight_grads[5], weight_grads[6], weight_grads[7], weight_grads[8], weight_grads[9], weight_grads[10], weight_grads[11])
```

```python
import jax
import jax.numpy as jnp
from jax import lax
from jax.sharding import PartitionSpec as P

D = 896
HEADS = 14
KV_HEADS = 2
HEAD = 64
LONGEST = 512
LANES = 128

epsilon = 1e-06
theta = 10000.0
masked = -1e30
bf16 = jnp.bfloat16
f32 = jnp.float32


def turned(values_in):
    half_width = values_in.shape[-1] // 2
    return jnp.concatenate([-values_in[..., half_width:], values_in[..., :half_width]], axis=-1)


def turned_back(values_in):
    half_width = values_in.shape[-1] // 2
    return jnp.concatenate([values_in[..., half_width:], -values_in[..., :half_width]], axis=-1)


def rotate(values_in, cosines, sines):
    return values_in * cosines + turned(values_in) * sines


def rotate_back(values_in, cosines, sines):
    return values_in * cosines + turned_back(values_in * sines)


def scaled(values_in):
    return lax.rsqrt(jnp.mean(values_in * values_in, axis=-1, keepdims=True) + epsilon)


def norm_back(grad_in, values_in, inverse, gain_full):
    weighted = grad_in * gain_full
    return inverse * weighted - values_in * (inverse * inverse * inverse) * jnp.mean(
        weighted * values_in, axis=-1, keepdims=True
    )


def dot(left, right, left_dim, right_dim):
    return lax.dot_general(
        left, right, (((left_dim,), (right_dim,)), ((), ())), preferred_element_type=f32
    )


def raw_scores(queries, keys_in, allowed):
    scores = jnp.einsum("qkgd,skd->kgqs", queries, keys_in, preferred_element_type=f32)
    return jnp.where(allowed, scores * HEAD**-0.5, masked)


def attend(queries, keys_in, values_in, allowed):
    scores = raw_scores(queries, keys_in, allowed)
    largest = jnp.max(scores, axis=-1, keepdims=True)
    exponent = jnp.exp(scores - largest)
    totals = jnp.sum(exponent, axis=-1, keepdims=True)
    soft_low = (exponent / totals).astype(bf16)
    mixed_heads = jnp.einsum("kgqs,skd->qkgd", soft_low, values_in, preferred_element_type=f32)
    return mixed_heads, largest, totals


def attend_back(queries, keys_in, values_in, allowed, largest, totals, grad_mixed):
    scores = raw_scores(queries, keys_in, allowed)
    soft_weights = jnp.exp(scores - largest) / totals
    soft_low = soft_weights.astype(bf16)
    grad_soft = jnp.einsum("qkgd,skd->kgqs", grad_mixed, values_in, preferred_element_type=f32)
    row_delta = jnp.sum(soft_weights * grad_soft, axis=-1, keepdims=True)
    grad_scores = (soft_weights * (grad_soft - row_delta)).astype(bf16)
    scale = HEAD**-0.5
    grad_queries = (
        jnp.einsum("kgqs,skd->qkgd", grad_scores, keys_in, preferred_element_type=f32) * scale
    )
    grad_keys = (
        jnp.einsum("kgqs,qkgd->skd", grad_scores, queries, preferred_element_type=f32) * scale
    )
    grad_values = jnp.einsum("kgqs,qkgd->skd", soft_low, grad_mixed, preferred_element_type=f32)
    return grad_queries, grad_keys, grad_values


def body(
    layer_in,
    doc_ids,
    cotangent,
    first_gain,
    query_weight,
    query_bias,
    key_weight,
    key_bias,
    value_weight,
    value_bias,
    out_weight,
    second_gain,
    gate_weight,
    up_weight,
    down_weight,
):
    parts = lax.axis_size("ctx")
    groups = lax.axis_size("dp")
    rank = lax.axis_index("ctx")
    micro_count = layer_in.shape[1]
    shard_rows = layer_in.shape[3]
    key_count = doc_ids.shape[3]
    group_size = HEADS // KV_HEADS
    query_width = HEADS * HEAD
    pair_width = KV_HEADS * HEAD
    hidden = gate_weight.shape[1]
    hidden_pad = -(-hidden // LANES) * LANES
    weight_rows = query_weight.shape[0]
    bias_rows = key_bias.shape[0]
    earlier_parts = min(parts - 1, -(-(LONGEST - 1) // shard_rows))

    def around(values_in, steps):
        return lax.ppermute(
            values_in, "ctx", [(s, (s + steps) % parts) for s in range(parts)]
        )

    def pieces_of(values_in):
        return [values_in] + [around(values_in, d) for d in range(1, parts)]

    def collected(values_in):
        pieces = pieces_of(values_in)
        ordered = [pieces[d] for d in range(parts - 1, -1, -1)]
        ordered = jnp.stack(ordered + ordered[:-1])
        taken = lax.dynamic_slice_in_dim(ordered, parts - 1 - rank, parts, 0)
        return taken.reshape((-1,) + values_in.shape[1:])

    def returned(pieces):
        total = pieces[0]
        for d in range(1, parts):
            total = total + around(pieces[d].astype(bf16), parts - d).astype(f32)
        return total

    def column(values_in):
        return jnp.pad(values_in, (0, weight_rows - values_in.shape[0]))[:, None]

    def wide(values_in):
        return jnp.pad(values_in, ((0, 0), (0, hidden_pad - hidden)))

    small = jnp.concatenate(
        [column(v) for v in (first_gain, second_gain, query_bias, key_bias, value_bias)], axis=1
    )
    small = jnp.pad(small, ((0, 0), (0, LANES - small.shape[1])))
    own_attention = jnp.concatenate(
        [query_weight, key_weight, value_weight, small, out_weight], axis=1
    )
    block_attention = collected(own_attention)
    first_width = query_width + 2 * pair_width + LANES
    first_set = lax.all_gather(block_attention[:, :first_width], "dp", axis=0, tiled=True)
    rest_block = jnp.concatenate(
        [wide(gate_weight), wide(up_weight), wide(down_weight.T), block_attention[:, first_width:]],
        axis=1,
    )
    rest_block = lax.optimization_barrier((rest_block, first_set[0, 0]))[0]
    rest_set = lax.all_gather(rest_block, "dp", axis=0, tiled=True)

    w_qkv = first_set[:, : query_width + 2 * pair_width]
    smalls = first_set[:, query_width + 2 * pair_width :]
    gain_one = smalls[:, 0].astype(f32)
    gain_two = smalls[:, 1].astype(f32)
    bias_all = jnp.concatenate(
        [smalls[:, 2]]
        + [smalls[:, k].reshape(-1, weight_rows)[:, :bias_rows].reshape(-1) for k in (3, 4)]
    ).astype(f32)
    w_gate = rest_set[:, :hidden_pad]
    w_up = rest_set[:, hidden_pad : 2 * hidden_pad]
    w_down = rest_set[:, 2 * hidden_pad : 3 * hidden_pad]
    w_out = rest_set[:, 3 * hidden_pad :]

    exponent = jnp.arange(HEAD // 2, dtype=f32) * (2.0 / HEAD)
    frequency = jnp.power(f32(theta), -exponent)

    upstreams = [cotangent[0, m, 0] for m in range(micro_count)]
    upstream_pieces = [pieces_of(u) for u in upstreams]

    kept = []
    for m in range(micro_count):
        tokens = layer_in[0, m, 0].astype(f32)
        docs_all = doc_ids[0, m, 0]
        own_docs = lax.dynamic_slice_in_dim(docs_all, rank * shard_rows, shard_rows, 0)
        row_index = rank * shard_rows + jnp.arange(shard_rows, dtype=jnp.int32)
        begins = jnp.sum((docs_all[None, :] < own_docs[:, None]).astype(jnp.int32), axis=1)
        positions = row_index - begins
        angle = positions.astype(f32)[:, None] * frequency[None, :]
        angle = jnp.concatenate([angle, angle], axis=-1)
        cosines, sines = jnp.cos(angle)[:, None, :], jnp.sin(angle)[:, None, :]
        key_index = (rank - earlier_parts) * shard_rows + jnp.arange(
            (earlier_parts + 1) * shard_rows, dtype=jnp.int32
        )
        allowed = (key_index[None, :] >= begins[:, None]) & (
            key_index[None, :] <= row_index[:, None]
        )
        inverse_one = scaled(tokens)
        normed_one = (tokens * inverse_one * gain_one).astype(bf16)
        qkv = dot(normed_one, w_qkv, 1, 0) + bias_all
        rot_query = rotate(
            qkv[:, :query_width].reshape(-1, HEADS, HEAD), cosines, sines
        ).astype(bf16)
        rot_keys = rotate(
            qkv[:, query_width : query_width + pair_width].reshape(-1, KV_HEADS, HEAD),
            cosines,
            sines,
        ).astype(bf16)
        own_pair = jnp.concatenate(
            [rot_keys.reshape(-1, pair_width), qkv[:, query_width + pair_width :].astype(bf16)],
            axis=1,
        )
        pair = [
            lax.ppermute(own_pair, "ctx", [(s, s + d) for s in range(parts - d)])
            for d in range(earlier_parts, 0, -1)
        ] + [own_pair]
        pair = jnp.concatenate(pair, axis=0)
        keys_in = pair[:, :pair_width].reshape(-1, KV_HEADS, HEAD)
        values_in = pair[:, pair_width:].reshape(-1, KV_HEADS, HEAD)
        queries = rot_query.reshape(-1, KV_HEADS, group_size, HEAD)
        mixed_heads, largest, totals = attend(queries, keys_in, values_in, allowed)
        mixed_low = mixed_heads.reshape(-1, query_width).astype(bf16)
        middle = tokens + dot(mixed_low, w_out, 1, 0)
        inverse_two = scaled(middle)
        normed_two = (middle * inverse_two * gain_two).astype(bf16)
        rows_all = jnp.concatenate(pieces_of(normed_two), axis=0)
        kept.append(
            dict(
                tokens=tokens, cosines=cosines, sines=sines, allowed=allowed,
                inverse_one=inverse_one, normed_one=normed_one, queries=queries,
                keys_in=keys_in, values_in=values_in, largest=largest, totals=totals,
                mixed_low=mixed_low, middle=middle, inverse_two=inverse_two, rows_all=rows_all,
            )
        )

    outs = []
    for m in range(micro_count):
        k = kept[m]
        rows_all = k["rows_all"]
        gate_pre = dot(rows_all, w_gate, 1, 0)
        up_pre = dot(rows_all, w_up, 1, 0)
        sigmoid_gate = jax.nn.sigmoid(gate_pre)
        activated = (gate_pre * sigmoid_gate * up_pre).astype(bf16)
        partial_out = dot(activated, w_down, 1, 1).reshape(parts, shard_rows, D)
        feed_out = returned([partial_out[d] for d in range(parts)])
        outs.append((k["middle"] + feed_out).astype(bf16))
        upstream_all = jnp.concatenate(upstream_pieces[m], axis=0)
        grad_act = dot(upstream_all, w_down, 1, 0)
        grad_gate = (
            grad_act * up_pre * sigmoid_gate * (1.0 + gate_pre * (1.0 - sigmoid_gate))
        ).astype(bf16)
        grad_up = (grad_act * gate_pre * sigmoid_gate).astype(bf16)
        normed_part = dot(grad_gate, w_gate, 1, 1) + dot(grad_up, w_up, 1, 1)
        normed_part = normed_part.reshape(parts, shard_rows, D)
        k["grad_normed_two"] = returned([normed_part[d] for d in range(parts)])
        k.update(
            activated=activated, grad_gate=grad_gate, grad_up=grad_up, upstream_all=upstream_all
        )

    def both(name):
        return jnp.concatenate([k[name] for k in kept], axis=0)

    rows_both = both("rows_all")
    feed_local = jnp.concatenate(
        [
            dot(rows_both, both("grad_gate"), 0, 0).astype(bf16),
            dot(rows_both, both("grad_up"), 0, 0).astype(bf16),
            dot(both("upstream_all"), both("activated"), 0, 0).astype(bf16),
        ],
        axis=1,
    )
    feed_sum = lax.psum_scatter(feed_local, "dp", scatter_dimension=0, tiled=True).astype(f32)

    inputs_grad = []
    gain_one_sum = gain_two_sum = 0.0
    for m in range(micro_count):
        k = kept[m]
        upstream = upstreams[m].astype(f32)
        grad_middle = upstream + norm_back(
            k["grad_normed_two"], k["middle"], k["inverse_two"], gain_two
        )
        gain_two_sum += jnp.sum(k["grad_normed_two"] * (k["middle"] * k["inverse_two"]), axis=0)
        branch_low = grad_middle.astype(bf16)
        grad_mixed = dot(branch_low, w_out, 1, 1).astype(bf16)
        grad_queries, grad_keys, grad_values = attend_back(
            k["queries"], k["keys_in"], k["values_in"], k["allowed"], k["largest"], k["totals"],
            grad_mixed.reshape(-1, KV_HEADS, group_size, HEAD),
        )
        grad_pair = jnp.concatenate(
            [grad_keys.reshape(-1, pair_width), grad_values.reshape(-1, pair_width)], axis=1
        ).reshape(earlier_parts + 1, shard_rows, 2 * pair_width)
        own_grad = grad_pair[earlier_parts]
        for d in range(1, earlier_parts + 1):
            own_grad = own_grad + lax.ppermute(
                grad_pair[earlier_parts - d].astype(bf16),
                "ctx",
                [(s, s - d) for s in range(d, parts)],
            ).astype(f32)
        query_grad = rotate_back(
            grad_queries.reshape(-1, HEADS, HEAD), k["cosines"], k["sines"]
        ).reshape(-1, query_width)
        key_grad = rotate_back(
            own_grad[:, :pair_width].reshape(-1, KV_HEADS, HEAD), k["cosines"], k["sines"]
        ).reshape(-1, pair_width)
        low = jnp.concatenate([query_grad, key_grad, own_grad[:, pair_width:]], axis=1).astype(bf16)
        grad_normed_one = dot(low, w_qkv, 1, 1)
        gain_one_sum += jnp.sum(grad_normed_one * (k["tokens"] * k["inverse_one"]), axis=0)
        inputs_grad.append(
            grad_middle + norm_back(grad_normed_one, k["tokens"], k["inverse_one"], gain_one)
        )
        k.update(low=low, branch_low=branch_low)

    low = both("low")
    bias_sum = jnp.sum(low.astype(f32), axis=0)

    def spread(values_in):
        values_in = values_in.reshape(-1, bias_rows)
        return jnp.pad(values_in, ((0, 0), (0, weight_rows - bias_rows))).reshape(-1)

    small_sums = jnp.stack(
        [
            gain_one_sum,
            gain_two_sum,
            bias_sum[:query_width],
            spread(bias_sum[query_width : query_width + pair_width]),
            spread(bias_sum[query_width + pair_width :]),
        ],
        axis=1,
    )
    small_sums = jnp.pad(small_sums, ((0, 0), (0, LANES - small_sums.shape[1])))
    attention_local = jnp.concatenate(
        [
            dot(both("normed_one"), low, 0, 0).astype(bf16),
            small_sums.astype(bf16),
            dot(both("mixed_low"), both("branch_low"), 0, 0).astype(bf16),
        ],
        axis=1,
    )
    attention_block = lax.psum_scatter(attention_local, "dp", scatter_dimension=0, tiled=True)
    attention_block = attention_block.reshape(parts, weight_rows, -1)

    def block_for(steps):
        return lax.dynamic_index_in_dim(
            attention_block, (rank + steps) % parts, 0, keepdims=False
        )

    attention_sum = block_for(0).astype(f32)
    for d in range(1, parts):
        attention_sum = attention_sum + around(block_for(d), d).astype(f32)

    edge = query_width + 2 * pair_width
    return (
        jnp.stack(outs)[None, :, None],
        jnp.stack(inputs_grad)[None, :, None],
        attention_sum[:, edge],
        attention_sum[:, :query_width],
        attention_sum[:, edge + 2],
        attention_sum[:, query_width : query_width + pair_width],
        attention_sum[:bias_rows, edge + 3],
        attention_sum[:, query_width + pair_width : edge],
        attention_sum[:bias_rows, edge + 4],
        attention_sum[:, edge + LANES :],
        attention_sum[:, edge + 1],
        feed_sum[:, :hidden],
        feed_sum[:, hidden_pad : hidden_pad + hidden],
        feed_sum[:, 2 * hidden_pad : 2 * hidden_pad + hidden].T,
    )


def solution(mesh):
    both = ("dp", "ctx")
    rows = P(both, None)
    line = P(both)
    tokens = P("dp", None, None, "ctx", None)
    return jax.shard_map(
        body,
        mesh=mesh,
        in_specs=(
            tokens, P("dp", None, None, None), tokens, line, rows, line, rows, line, rows, line,
            rows, line, P("dp", "ctx"), P("dp", "ctx"), P("ctx", "dp"),
        ),
        out_specs=(
            tokens, tokens, line, rows, line, rows, line, rows, line, rows, line,
            P("dp", "ctx"), P("dp", "ctx"), P("ctx", "dp"),
        ),
        check_vma=False,
    )
```

```python
import functools
import jax, jax.numpy as jnp
from jax import lax
from jax.sharding import PartitionSpec as P
from jax.experimental import pallas as pl
from jax.experimental.pallas import tpu as pltpu
D=896; HEADS=14; KV_HEADS=2; HEAD=64; LANES=128
QW=896; KW=128
epsilon=1e-6
bf16=jnp.bfloat16; f32=jnp.float32
LIMIT=56*1024*1024
COST=pl.CostEstimate(flops=1, bytes_accessed=1, transcendentals=0)

def dot(left, right, left_dim, right_dim):
    return lax.dot_general(left, right, (((left_dim,), (right_dim,)), ((), ())), preferred_element_type=f32)

def half_turn(v, back):
    lane = lax.broadcasted_iota(jnp.int32, v.shape, 1) & (HEAD-1)
    width=v.shape[1]
    up = pltpu.roll(v, width-HEAD//2, 1)
    down = pltpu.roll(v, HEAD//2, 1)
    return jnp.where(lane < HEAD//2, up, down)

def scaled(v):
    return lax.rsqrt(jnp.mean(v*v, axis=-1, keepdims=True)+epsilon)

def project_kernel(x_ref, wq_ref, wkv_ref, ws_ref, spread_ref, cos_ref, sin_ref, rq_ref, kv_ref, n1_ref, rows_ref, bias_ref):
    @pl.when(pl.program_id(0)==0)
    def _():
        table = ws_ref[...].astype(f32).T[:8]
        rows_ref[...] = table
        close = dot(table.astype(bf16), spread_ref[...],1,0)
        bias_ref[:, :QW] = table[2:3]
        bias_ref[:, QW:QW+KW] = close[3:4]
        bias_ref[:, QW+KW:] = close[4:5]
    x = x_ref[0].astype(f32)
    n1 = (x*scaled(x)*rows_ref[0:1]).astype(bf16)
    n1_ref[0] = n1
    cos = cos_ref[0]; sin = sin_ref[0]
    q = dot(n1, wq_ref[...],1,0) + bias_ref[:, :QW]
    for b in range(QW//LANES):
        v = q[:, b*LANES:(b+1)*LANES]
        r = (v*cos + half_turn(v,False)*sin).astype(bf16)
        rq_ref[0,:, b*LANES:(b+1)*LANES] = (r.astype(f32)*HEAD**-0.5).astype(bf16)
    kv = dot(n1, wkv_ref[...],1,0) + bias_ref[:, QW:]
    v = kv[:, :KW]
    kv_ref[0,:, :KW] = (v*cos + half_turn(v,False)*sin).astype(bf16)
    kv_ref[0,:, KW:] = kv[:, KW:].astype(bf16)

def project(x, first_set, spread, cos, sin):
    m, rows, _ = x.shape
    full=lambda shape,idx: pl.BlockSpec(shape, lambda i: idx)
    blk=lambda w: pl.BlockSpec((1,rows,w), lambda i:(i,0,0))
    return pl.pallas_call(
        project_kernel, grid=(m,),
        in_specs=[blk(D), full((D,QW),(0,1)), full((D,2*KW),(0,7)), full((D,LANES),(0,16)), full((D,LANES),(0,0)), blk(LANES), blk(LANES)],
        out_specs=[blk(QW), blk(2*KW), blk(D), full((8,D),(0,0))],
        out_shape=[jax.ShapeDtypeStruct((m,rows,QW),bf16), jax.ShapeDtypeStruct((m,rows,2*KW),bf16), jax.ShapeDtypeStruct((m,rows,D),bf16), jax.ShapeDtypeStruct((8,D),f32)],
        scratch_shapes=[pltpu.VMEM((1,QW+2*KW),f32)],
        compiler_params=pltpu.CompilerParams(vmem_limit_bytes=LIMIT), cost_estimate=COST,
        name="project",
    )(x, first_set, first_set, first_set, spread, cos, sin)

BLOCK=128
def units():
    group=HEADS//KV_HEADS
    out=[]
    for g in range(KV_HEADS):
        for parity in range(2):
            blocks=[h//2 for h in range(g*group,(g+1)*group) if h%2==parity]
            out.append((g,parity,blocks))
    return out

def padded(v, g, parity, lane):
    if g != parity:
        v = pltpu.roll(v.astype(f32), HEAD, 1).astype(bf16)
    keep = (lane >= HEAD) if parity else (lane < HEAD)
    return jnp.where(keep, v, jnp.zeros_like(v))

def mask_bias(begins, rank_base, q0, window, reach):
    key = lax.broadcasted_iota(jnp.int32,(window,BLOCK),0) + (rank_base + q0 - reach)
    query = lax.broadcasted_iota(jnp.int32,(window,BLOCK),1) + (rank_base + q0)
    ok = (key >= begins) & (key <= query)
    return jnp.where(ok, 0.0, -1e30).astype(f32)

def fill_padded(kv_refs, k_ref, v_ref):
    rows = kv_refs[0].shape[0]
    lane = lax.broadcasted_iota(jnp.int32,(rows,LANES),1)
    for p,ref in enumerate(kv_refs):
        kv=ref[...]
        for g,parity,_ in units():
            u=2*g+parity
            k_ref[u, p*rows:(p+1)*rows] = padded(kv[:, :KW], g, parity, lane)
            v_ref[u, p*rows:(p+1)*rows] = padded(kv[:, KW:], g, parity, lane)

def attend_kernel(base_ref, rq_ref, kv0_ref, kv1_ref, kv2_ref, begin_ref, wo_ref, x_ref, rows_ref, *refs):
    n2_ref, mixed_ref, middle_ref, lse_ref, k_ref, v_ref = refs[-6:]
    qb = pl.program_id(0)
    rows = kv0_ref.shape[0]
    reach=512; window=reach+BLOCK
    @pl.when(qb==0)
    def _():
        fill_padded((kv2_ref,kv1_ref,kv0_ref), k_ref, v_ref)
    q0 = qb*BLOCK
    bias = mask_bias(begin_ref[...], base_ref[0], q0, window, reach)
    parts=[None]*7
    start = pl.multiple_of(q0 + (2*rows - reach), BLOCK)
    for g,parity,blocks in units():
        u=2*g+parity
        qs = jnp.concatenate([rq_ref[:, b*LANES:(b+1)*LANES] for b in blocks], axis=0)
        keys = k_ref[u, pl.ds(start,window)]
        vals = v_ref[u, pl.ds(start,window)]
        s = dot(keys, qs, 1, 1) + jnp.concatenate([bias]*len(blocks),axis=1)
        top = jnp.max(s, axis=0, keepdims=True)
        e = jnp.exp(s-top)
        total = jnp.sum(e, axis=0, keepdims=True)
        p = (e*(1.0/total)).astype(bf16)
        o = dot(vals, p, 0, 0)
        lse = top+jnp.log(total)
        for i,b in enumerate(blocks):
            piece=o[:, i*BLOCK:(i+1)*BLOCK]
            parts[b] = piece if parts[b] is None else parts[b]+piece
            lse_ref[0, 2*b+parity:2*b+parity+1, :] = lse[:, i*BLOCK:(i+1)*BLOCK]
    for b in range(7):
        mixed_ref[:, b*LANES:(b+1)*LANES] = parts[b].T.astype(bf16)
    middle = x_ref[...].astype(f32) + dot(mixed_ref[...], wo_ref[...],1,0)
    middle_ref[...] = middle
    n2_ref[...] = (middle*scaled(middle)*rows_ref[1:2]).astype(bf16)

def attend(m, base, rq, kvs, begins, first_set, x, rows_table, before):
    micros, rows, _ = rq.shape; nq=rows//BLOCK
    full=lambda shape: pl.BlockSpec(shape, lambda i: (0,)*len(shape))
    blk=lambda w: pl.BlockSpec((None,BLOCK,w), lambda i:(m,i,0))
    sd=jax.ShapeDtypeStruct
    return pl.pallas_call(
        attend_kernel, grid=(nq,),
        in_specs=[pl.BlockSpec(memory_space=pltpu.SMEM), blk(QW)]+[pl.BlockSpec((None,rows,2*KW),lambda i:(m,0,0))]*3+[pl.BlockSpec((None,1,BLOCK),lambda i:(m,0,i)), full((D,QW)), blk(D), full((8,D))]+[pl.BlockSpec(memory_space=pl.ANY)]*len(before),
        out_specs=[pl.BlockSpec((BLOCK,D),lambda i:(i,0)), blk(QW), blk(D), pl.BlockSpec((None,1,16,BLOCK),lambda i:(m,i,0,0))],
        out_shape=[sd((rows,D),bf16), sd((micros,rows,QW),bf16), sd((micros,rows,D),f32), sd((micros,nq,16,BLOCK),f32)],
        scratch_shapes=[pltpu.VMEM((4,3*rows,LANES),bf16), pltpu.VMEM((4,3*rows,LANES),bf16)],
        input_output_aliases={9+k:1+k for k in range(len(before))},
        compiler_params=pltpu.CompilerParams(vmem_limit_bytes=LIMIT), cost_estimate=COST,
        name="attend",
    )(base, rq, *kvs, begins, first_set, x, rows_table, *before)

def attend_back_kernel(base_ref, rq_ref, kv0_ref, kv1_ref, kv2_ref, begin_ref, wo_ref, rows_ref, lse_ref, middle_ref, dy_ref, cos_ref, sin_ref, *refs, count):
    gs=refs[:count]
    far1_ref, far2_ref, dmid_ref, dmb_ref, dq_ref, own_ref, gain_ref, k_ref, v_ref, dk_ref, dv_ref = refs[-11:]
    qb = pl.program_id(0); nq=pl.num_programs(0)
    rows = kv0_ref.shape[0]
    reach=512; window=reach+BLOCK
    @pl.when(qb==0)
    def _():
        fill_padded((kv2_ref,kv1_ref,kv0_ref), k_ref, v_ref)
        dk_ref[...] = jnp.zeros_like(dk_ref)
        dv_ref[...] = jnp.zeros_like(dv_ref)
        gain_ref[...] = jnp.zeros_like(gain_ref)
    dn2 = gs[0][...].astype(f32)
    for g_ref in gs[1:]:
        dn2 = dn2+g_ref[...].astype(f32)
    middle = middle_ref[...]
    inv = scaled(middle)
    gain_ref[...] += jnp.broadcast_to(jnp.sum(dn2*(middle*inv),axis=0,keepdims=True), gain_ref.shape)
    w2 = dn2*rows_ref[1:2]
    dmid = dy_ref[...].astype(f32) + inv*w2 - middle*(inv*inv*inv)*jnp.mean(w2*middle,axis=-1,keepdims=True)
    dmid_ref[...] = dmid
    dmb = dmid.astype(bf16)
    dmb_ref[...] = dmb
    dmixed = dot(dmb, wo_ref[...],1,1).astype(bf16)
    q0 = qb*BLOCK
    bias = mask_bias(begin_ref[...], base_ref[0], q0, window, reach)
    start = pl.multiple_of(q0 + (2*rows - reach), BLOCK)
    parts=[None]*7
    for g,parity,blocks in units():
        u=2*g+parity
        n=len(blocks)
        qs = jnp.concatenate([rq_ref[:, b*LANES:(b+1)*LANES] for b in blocks], axis=0)
        ds_ = jnp.concatenate([dmixed[:, b*LANES:(b+1)*LANES] for b in blocks], axis=0)
        keys = k_ref[u, pl.ds(start,window)]
        vals = v_ref[u, pl.ds(start,window)]
        lse = jnp.concatenate([lse_ref[0, 2*b+parity:2*b+parity+1, :] for b in blocks],axis=1)
        p = jnp.exp(dot(keys,qs,1,1) + jnp.concatenate([bias]*n,axis=1) - lse)
        dp = dot(vals, ds_, 1, 1)
        t = p*dp
        ds = (t-p*jnp.sum(t,axis=0,keepdims=True)).astype(bf16)
        pb = p.astype(bf16)
        o = dot(keys, ds, 0, 0)
        for i,b in enumerate(blocks):
            piece=o[:, i*BLOCK:(i+1)*BLOCK]
            parts[b] = piece if parts[b] is None else parts[b]+piece
        dk = dot(ds, qs, 1, 0); dv = dot(pb, ds_, 1, 0)
        keep = lax.broadcasted_iota(jnp.int32,(window,LANES),1)
        keep = (keep>=HEAD) if parity else (keep<HEAD)
        dk = jnp.where(keep, dk, 0.0); dv=jnp.where(keep,dv,0.0)
        if g!=parity:
            dk = pltpu.roll(dk,HEAD,1); dv=pltpu.roll(dv,HEAD,1)
        dk_ref[pl.ds(start,window)] += dk
        dv_ref[pl.ds(start,window)] += dv
    cos=cos_ref[...]; sin=sin_ref[...]
    for b in range(7):
        gq = parts[b].T*HEAD**-0.5
        dq_ref[:, b*LANES:(b+1)*LANES] = (gq*cos + half_turn(gq*sin,True)).astype(bf16)
    @pl.when(qb==nq-1)
    def _():
        own_ref[:, :KW] = dk_ref[2*rows:]; own_ref[:, KW:] = dv_ref[2*rows:]
        far1_ref[:, :KW] = dk_ref[rows:2*rows].astype(bf16); far1_ref[:, KW:] = dv_ref[rows:2*rows].astype(bf16)
        far2_ref[:, :KW] = dk_ref[:rows].astype(bf16); far2_ref[:, KW:] = dv_ref[:rows].astype(bf16)

def attend_back(m, base, rq, kvs, begins, first_set, rows_table, lse, middle, dy, gs, cos, sin, before):
    micros, rows, _ = rq.shape; nq=rows//BLOCK
    full=lambda shape: pl.BlockSpec(shape, lambda i: (0,)*len(shape))
    blk=lambda w: pl.BlockSpec((None,BLOCK,w), lambda i:(m,i,0))
    one=lambda h,w: pl.BlockSpec((None,h,w), lambda i:(m,0,0))
    sd=jax.ShapeDtypeStruct
    at=12+len(gs)
    return pl.pallas_call(
        functools.partial(attend_back_kernel,count=len(gs)), grid=(nq,),
        in_specs=[pl.BlockSpec(memory_space=pltpu.SMEM), blk(QW)]+[one(rows,2*KW)]*3+[pl.BlockSpec((None,1,BLOCK),lambda i:(m,0,i)), full((D,QW)), full((8,D)),
            pl.BlockSpec((None,1,16,BLOCK),lambda i:(m,i,0,0)), blk(D), blk(D)]+[blk(LANES)]*2+[pl.BlockSpec((BLOCK,D),lambda i:(i,0))]*len(gs)+[pl.BlockSpec(memory_space=pl.ANY)]*len(before),
        out_specs=[full((rows,2*KW)), full((rows,2*KW)), blk(D), blk(D), blk(QW), one(rows,2*KW), one(8,D)],
        out_shape=[sd((rows,2*KW),bf16), sd((rows,2*KW),bf16), sd((micros,rows,D),f32), sd((micros,rows,D),bf16), sd((micros,rows,QW),bf16), sd((micros,rows,2*KW),f32), sd((micros,8,D),f32)],
        scratch_shapes=[pltpu.VMEM((4,3*rows,LANES),bf16)]*2+[pltpu.VMEM((3*rows,LANES),f32)]*2,
        input_output_aliases={at+1+k:2+k for k in range(len(before))},
        compiler_params=pltpu.CompilerParams(vmem_limit_bytes=LIMIT), cost_estimate=COST,
        name="attend_back",
    )(base, rq, *kvs, begins, first_set, rows_table, lse, middle, dy, cos, sin, *gs, *before)

CHUNK=256

class Tokens:
    def __init__(self, kind, arrays, micro=None):
        self.kind, self.arrays, self.micro = kind, tuple(arrays), micro
    def specs(self, rows):
        if self.kind=="whole":
            return [pl.BlockSpec((rows,D), lambda i: (i,0))]
        if self.micro is None:
            return [pl.BlockSpec((rows,D), lambda i: (0,0), pipeline_mode=pl.Buffered(1))]*len(self.arrays)
        return [pl.BlockSpec((None,rows,D), lambda i: (self.micro,0,0), pipeline_mode=pl.Buffered(1))]*len(self.arrays)
    def take(self, refs, i, rank, parts, into):
        if self.kind=="whole":
            into[...]=refs[0][...]
        elif self.kind=="around":
            for k in range(parts):
                @pl.when(lax.rem(rank-i+parts,parts)==k)
                def _(k=k): into[...]=refs[k][...]
        else:
            for k in range(-(parts-1),parts):
                ref = refs[0] if k==0 else refs[2*k-1] if k>0 else refs[-2*k]
                @pl.when(rank-i==k)
                def _(ref=ref): into[...]=ref[...]

def feed_kernel(rank_ref, *refs, parts, kept, toks, grads):
    n_t=len(toks.arrays); n_g=len(grads.arrays)
    ts=refs[:n_t]; gs=refs[n_t:n_t+n_g]; refs=refs[n_t+n_g:]
    wg_ref,wu_ref,wd_ref=refs[:3]
    refs=refs[3+kept:]
    backs=refs[:parts]; outs=refs[parts:2*parts]
    x_ref,y_ref,pair_ref,act_ref=refs[2*parts:]
    i=pl.program_id(0); rank=rank_ref[0]
    toks.take(ts,i,rank,parts,x_ref); grads.take(gs,i,rank,parts,y_ref)
    x=x_ref[...]; y=y_ref[...]
    width=wg_ref.shape[1]
    for j in range(width//CHUNK):
        c=slice(j*CHUNK,(j+1)*CHUNK); c2=slice(width+j*CHUNK,width+(j+1)*CHUNK)
        g=dot(x,wg_ref[:,c],1,0); u=dot(x,wu_ref[:,c],1,0); da=dot(y,wd_ref[:,c],1,0)
        s=jax.nn.sigmoid(g)
        gs_=g*s
        act_ref[:,c]=(gs_*u).astype(bf16)
        pair_ref[:,c]=(da*u*s*(1.0+g*(1.0-s))).astype(bf16)
        pair_ref[:,c2]=(da*gs_).astype(bf16)
    out=dot(act_ref[...],wd_ref[...],1,1)
    res=dot(pair_ref[:,:width],wg_ref[...],1,1)+dot(pair_ref[:,width:],wu_ref[...],1,1)
    for value,places in ((out,outs),(res,backs)):
        for k in range(parts):
            @pl.when(lax.rem(rank-i+parts,parts)==k)
            def _(k=k,value=value,places=places):
                places[k][...]=value.astype(places[k].dtype)

def feed(rank, toks, grads, rest_set, hidden_pad, micro, micros, parts, rows, before):
    full=lambda shape,idx=(0,0): pl.BlockSpec(shape, lambda i: idx)
    blk=lambda w,first=0: pl.BlockSpec((rows,w), lambda i:(first+i,0))
    sd=jax.ShapeDtypeStruct
    everything=rows*parts*micros
    kept=len(before)
    specs=[full((rows,D))]*parts+[pl.BlockSpec((None,rows,D),lambda i:(micro,0,0))]*parts
    shapes=[sd((rows,D),f32)]+[sd((rows,D),bf16)]*(parts-1)+[sd((micros,rows,D),f32)]+[sd((micros,rows,D),bf16)]*(parts-1)
    n_in=1+len(toks.arrays)+len(grads.arrays)+3
    out=pl.pallas_call(
        functools.partial(feed_kernel,parts=parts,kept=kept,toks=toks,grads=grads), grid=(parts,),
        in_specs=[pl.BlockSpec(memory_space=pltpu.SMEM)]+toks.specs(rows)+grads.specs(rows)+[pl.BlockSpec((D,hidden_pad),lambda i,k=k:(0,k),pipeline_mode=pl.Buffered(1)) for k in range(3)]+[pl.BlockSpec(memory_space=pl.ANY)]*kept,
        out_specs=specs+[blk(w,micro*parts) for w in (D,D,2*hidden_pad,hidden_pad)],
        out_shape=shapes+[sd((everything,w),bf16) for w in (D,D,2*hidden_pad,hidden_pad)],
        input_output_aliases={n_in+k:parts+k for k in range(kept)},
        compiler_params=pltpu.CompilerParams(vmem_limit_bytes=LIMIT), cost_estimate=COST,
        name="feed",
    )(rank,*toks.arrays,*grads.arrays,rest_set,rest_set,rest_set,*before)
    return out[:parts], out[parts:]

def finish_kernel(bit_ref, dq_ref, own_ref, cos_ref, sin_ref, wq_ref, wkv_ref, rows_ref, x_ref, n1_ref, dmid_ref, mixed_ref, dmb_ref, spread_ref, gain2_ref, *refs, near, block):
    far=refs[:-6]
    ig_ref, keep_ref, send_ref, acc_ref, small_ref, sum_ref = refs[-6:]
    i=pl.program_id(0)
    @pl.when(i==0)
    def _():
        acc_ref[...]=jnp.zeros_like(acc_ref)
        small_ref[...]=jnp.zeros_like(small_ref)
    for m in range(len(far)//near):
        @pl.when(i==m)
        def _(m=m):
            own=own_ref[...]
            for ref in far[m*near:(m+1)*near]:
                own=own+ref[...].astype(f32)
            sum_ref[...]=own
    own=sum_ref[...]
    k=own[:, :KW]
    cos=cos_ref[...]; sin=sin_ref[...]
    dk=(k*cos+half_turn(k*sin,True)).astype(bf16)
    dv=own[:, KW:].astype(bf16)
    dkv=jnp.concatenate([dk,dv],axis=1)
    dq=dq_ref[...]
    dn1=dot(dq,wq_ref[...],1,1)+dot(dkv,wkv_ref[...],1,1)
    x=x_ref[...].astype(f32); inv=scaled(x)
    small_ref[0:1]+=jnp.sum(dn1*(x*inv),axis=0,keepdims=True)
    small_ref[1:2]+=gain2_ref[0:1]
    small_ref[2:3]+=jnp.sum(dq.astype(f32),axis=0,keepdims=True)
    small_ref[3:4,:2*KW]+=jnp.sum(dkv.astype(f32),axis=0,keepdims=True)
    w1=dn1*rows_ref[0:1]
    ig_ref[...]=dmid_ref[...]+inv*w1-x*(inv*inv*inv)*jnp.mean(w1*x,axis=-1,keepdims=True)
    n1=n1_ref[...]
    acc_ref[:, :QW]+=dot(mixed_ref[...],dmb_ref[...],0,0)
    acc_ref[:, QW:2*QW]+=dot(n1,dq,0,0)
    acc_ref[:, 2*QW:2*QW+2*KW]+=dot(n1,dkv,0,0)
    @pl.when(i==pl.num_programs(0)-1)
    def _():
        pair=jnp.concatenate([small_ref[3:4,:KW],small_ref[3:4,KW:2*KW],jnp.zeros((6,KW),f32)],axis=0).astype(bf16)
        table=jnp.concatenate([small_ref[0:3],dot(pair,spread_ref[...],1,1)[0:2],jnp.zeros((LANES-5,D),f32)],axis=0)
        acc_ref[:, 2*QW+2*KW:]=table.T
        if block:
            for j in range(D//block//2):
                at=pl.multiple_of((2*j+bit_ref[0])*block,16)
                keep_ref[j*block:(j+1)*block]=acc_ref[pl.ds(at,block)].astype(bf16)
                at=pl.multiple_of((2*j+1-bit_ref[0])*block,16)
                send_ref[j*block:(j+1)*block]=acc_ref[pl.ds(at,block)].astype(bf16)
        else:
            keep_ref[...]=acc_ref[:D//2].astype(bf16)
            send_ref[...]=acc_ref[D//2:].astype(bf16)

def finish(bit,dq,own,far,cos,sin,first_set,rows_table,x,n1,dmid,mixed,dmb,spread,gain2,block):
    m,rows,_=x.shape
    full=lambda shape,idx=(0,0): pl.BlockSpec(shape, lambda i: idx)
    blk=lambda w,h=rows: pl.BlockSpec((None,h,w), lambda i:(i,0,0))
    sd=jax.ShapeDtypeStruct
    width=2*QW+2*KW+LANES
    near=len(far[0])
    far=[f for pieces in far for f in pieces]
    return pl.pallas_call(
        functools.partial(finish_kernel,near=near,block=block), grid=(m,),
        in_specs=[pl.BlockSpec(memory_space=pltpu.SMEM),blk(QW),blk(2*KW),blk(LANES),blk(LANES),full((D,QW),(0,1)),full((D,2*KW),(0,7)),full((8,D)),blk(D),blk(D),blk(D),blk(QW),blk(D),full((D,LANES)),blk(D,8)]+[full((rows,2*KW))]*len(far),
        out_specs=[blk(D),full((D//2,width)),full((D//2,width))],
        out_shape=[sd((m,rows,D),f32),sd((D//2,width),bf16),sd((D//2,width),bf16)],
        scratch_shapes=[pltpu.VMEM((D,width),f32),pltpu.VMEM((8,D),f32),pltpu.VMEM((rows,2*KW),f32)],
        compiler_params=pltpu.CompilerParams(vmem_limit_bytes=LIMIT), cost_estimate=COST,
        name="finish",
    )(bit,dq,own,cos,sin,first_set,first_set,rows_table,x,n1,dmid,mixed,dmb,spread,gain2,*far)

def weights_kernel(x_ref, y_ref, pair_ref, act_ref, out_ref, left_ref, *, split):
    j=pl.program_id(0)
    @pl.when(j==0)
    def _(): left_ref[...]=x_ref[...].T
    @pl.when(j==split)
    def _(): left_ref[...]=y_ref[...].T
    @pl.when(j<split)
    def _(): out_ref[...]=dot(left_ref[...],pair_ref[...],1,0).astype(bf16)
    @pl.when(j>=split)
    def _(): out_ref[...]=dot(left_ref[...],act_ref[...],1,0).astype(bf16)

def weights(x,y,pair,act,chunk=256):
    rows=x.shape[0]; width=pair.shape[1]+act.shape[1]; split=pair.shape[1]//chunk
    one=pl.BlockSpec((rows,D),lambda j:(0,0),pipeline_mode=pl.Buffered(1))
    return pl.pallas_call(
        functools.partial(weights_kernel,split=split), grid=(width//chunk,),
        in_specs=[one,one,pl.BlockSpec((rows,chunk),lambda j:(0,jnp.minimum(j,split-1))),pl.BlockSpec((rows,chunk),lambda j:(0,jnp.maximum(j-split,0)))],
        out_specs=pl.BlockSpec((D,chunk),lambda j:(0,j)), out_shape=jax.ShapeDtypeStruct((D,width),bf16),
        scratch_shapes=[pltpu.VMEM((D,rows),bf16)],
        compiler_params=pltpu.CompilerParams(vmem_limit_bytes=LIMIT), cost_estimate=COST,
        name="weights",
    )(x,y,pair,act)


LONGEST = 512


def after(values_in, *needed):
    return lax.optimization_barrier((values_in, needed))[0]


theta = 10000.0


def body(
    layer_in,
    doc_ids,
    cotangent,
    first_gain,
    query_weight,
    query_bias,
    key_weight,
    key_bias,
    value_weight,
    value_bias,
    out_weight,
    second_gain,
    gate_weight,
    up_weight,
    down_weight,
):
    parts = lax.axis_size("ctx")
    rank = lax.axis_index("ctx")
    micros = layer_in.shape[1]
    shard_rows = layer_in.shape[3]
    hidden = gate_weight.shape[1]
    hidden_pad = -(-hidden // (2 * LANES)) * 2 * LANES
    weight_rows = query_weight.shape[0]
    bias_rows = key_bias.shape[0]
    reach_parts = -(-LONGEST // shard_rows)

    def around(values_in, steps):
        return lax.ppermute(values_in, "ctx", [(s, (s + steps) % parts) for s in range(parts)])

    def pieces_of(values_in):
        return [values_in] + [around(values_in, d) for d in range(1, parts)]

    def collected(values_in):
        pieces = pieces_of(values_in)
        ordered = [pieces[d] for d in range(parts - 1, -1, -1)]
        ordered = jnp.stack(ordered + ordered[:-1])
        taken = lax.dynamic_slice_in_dim(ordered, parts - 1 - rank, parts, 0)
        return taken.reshape((-1,) + values_in.shape[1:])

    def ahead(values_in):
        return lax.ppermute(values_in, "ctx", [(s, s + 1) for s in range(parts - 1)])

    def behind(values_in):
        return lax.ppermute(values_in, "ctx", [(s + 1, s) for s in range(parts - 1)])

    def column(values_in):
        return jnp.pad(values_in, (0, weight_rows - values_in.shape[0]))[:, None]

    def wide(values_in):
        return jnp.pad(values_in, ((0, 0), (0, hidden_pad - hidden)))

    small = jnp.concatenate(
        [column(v) for v in (first_gain, second_gain, query_bias, key_bias, value_bias)], axis=1
    )
    small = jnp.pad(small, ((0, 0), (0, LANES - small.shape[1])))
    own_attention = jnp.concatenate(
        [out_weight, query_weight, key_weight, value_weight, small], axis=1
    )
    first_set = lax.all_gather(collected(own_attention), "dp", axis=0, tiled=True)
    rest_block = jnp.concatenate([wide(gate_weight), wide(up_weight), wide(down_weight.T)], axis=1)
    rest_block = lax.optimization_barrier((rest_block, first_set[0, 0]))[0]
    rest_set = lax.all_gather(rest_block, "dp", axis=0, tiled=True)

    row = jnp.arange(D, dtype=jnp.int32)[:, None]
    place = row // weight_rows * bias_rows + row % weight_rows
    spread = (
        (place == jnp.arange(LANES, dtype=jnp.int32)[None, :]) & (row % weight_rows < bias_rows)
    ).astype(bf16)

    docs = doc_ids[0, :, 0]
    own_docs = lax.dynamic_slice_in_dim(docs, rank * shard_rows, shard_rows, 1)
    begins = jnp.sum((docs[:, None, :] < own_docs[:, :, None]).astype(jnp.int32), axis=2)
    row_index = rank * shard_rows + jnp.arange(shard_rows, dtype=jnp.int32)
    positions = row_index[None, :] - begins
    frequency = jnp.power(f32(theta), -(jnp.arange(HEAD // 2, dtype=f32) * (2.0 / HEAD)))
    angle = positions.astype(f32)[:, :, None] * frequency
    cosines, sines = jnp.cos(angle), jnp.sin(angle)
    cosines = jnp.concatenate([cosines] * (2 * LANES // HEAD), axis=2)
    sines = jnp.concatenate([-sines, sines] * (LANES // HEAD), axis=2)
    base = (rank * shard_rows).reshape(1)

    tokens = layer_in[0, :, 0]
    upstream = cotangent[0, :, 0]
    chains = [[upstream[m]] for m in range(micros)]
    moving = [(upstream[m], upstream[m]) for m in range(micros)]

    def next_round(m):
        moving[m] = (ahead(moving[m][0]), behind(moving[m][1]))
        chains[m] += list(moving[m])

    for m in range(micros):
        next_round(m)
    next_round(0)
    first_set = after(first_set, moving)
    for m in range(1, micros):
        next_round(m)

    rot_query, pairs, normed_one, rows_table = project(tokens, first_set, spread, cosines, sines)
    pairs = after(pairs, moving)
    kvs = [pairs] + [
        lax.ppermute(pairs, "ctx", [(s, s + d) for s in range(parts - d)])
        for d in range(1, reach_parts + 1)
    ]
    moving = after(moving, kvs[1:])
    while len(chains[0]) < 2 * parts - 1:
        for m in range(micros):
            next_round(m)

    begins = begins[:, None, :]
    exchanged = []
    held = ()
    for m in range(micros):
        if m == 1:
            kvs = after(kvs, moving)
        normed_two, *held = attend(
            m, base, rot_query, kvs, begins, first_set, tokens, rows_table, held
        )
        exchanged.append(Tokens("around", pieces_of(normed_two)))
    mixed, middle, log_sums = held

    backs = []
    before = ()
    rank_one = rank.reshape(1)
    for m in range(micros):
        back, before = feed(
            rank_one, exchanged[m], Tokens("chain", chains[m]), rest_set, hidden_pad, m, micros,
            parts, shard_rows, before,
        )
        backs.append([back[0]] + [around(back[d], parts - d) for d in range(1, parts)])
    partials = before[:parts]

    feed_local = weights(*before[parts:])
    backs[0] = after(backs[0], feed_local)
    far = []
    ended = ()
    arrived = {}
    for m in range(micros):
        if m == micros - 1:
            backs[m], feed_local, ended, far = after((backs[m], feed_local, ended, far))
            arrived[1] = around(after(partials[1], backs[m]), parts - 1)
        far1, far2, *ended = attend_back(
            m, base, rot_query, kvs, begins, first_set, rows_table, log_sums, middle, upstream,
            backs[m], cosines, sines, ended,
        )
        if m == micros - 1:
            far1, far2, arrived[1] = after((far1, far2, arrived[1]))
        far.append(
            [
                lax.ppermute(part, "ctx", [(s, s - d) for s in range(d, parts)])
                for d, part in ((1, far1), (2, far2))
            ]
        )
    feed_sum = lax.psum_scatter(feed_local, "dp", scatter_dimension=0, tiled=True).astype(f32)

    group_rank = lax.axis_index("dp")
    groups = lax.axis_size("dp")
    bits = [1 << k for k in range(groups.bit_length() - 1)]
    block_rows = parts * weight_rows
    even = block_rows % 16 == 0
    grad_middle, branch_low, query_grad, own_pair, gain_sum = ended
    input_grad, keep, send = finish(
        (group_rank % 2).reshape(1), query_grad, own_pair, far, cosines, sines, first_set,
        rows_table, tokens, normed_one, grad_middle, mixed, branch_low, spread, gain_sum,
        block_rows if even else 0,
    )
    if not even:
        both = jnp.concatenate([keep, send]).reshape(groups // 2, 2, block_rows, -1)
        keep, send = (
            lax.dynamic_index_in_dim(both, v, 1, keepdims=False)
            for v in (group_rank % 2, 1 - group_rank % 2)
        )

    arrived[3] = around(after(partials[3], far), parts - 3)

    def swapped(values_in, bit):
        return lax.ppermute(values_in, "dp", [(s, s ^ bit) for s in range(groups)])

    def halved(blocks, order):
        for k, bit in enumerate(order):
            size = blocks.shape[0]
            at = sorted(order[k:]).index(bit)
            view = blocks.reshape((size >> (at + 1), 2, 1 << at) + blocks.shape[1:])
            own = (group_rank // bit) % 2
            kept = lax.dynamic_index_in_dim(view, own, 1, keepdims=False)
            sent = lax.dynamic_index_in_dim(view, 1 - own, 1, keepdims=False)
            got = swapped(sent.astype(bf16), bit)
            blocks = (kept.astype(f32) + got.astype(f32)).reshape((size // 2,) + blocks.shape[1:])
        return blocks

    blocks = keep.astype(f32) + swapped(send, 1).astype(f32)
    blocks, arrived[3] = after((blocks, arrived[3]))
    arrived[2] = around(after(partials[2], blocks), parts - 2)
    blocks = blocks.reshape(groups // 2, block_rows, -1)
    cut = QW + 2 * LANES
    attention_block = jnp.concatenate(
        [halved(blocks[:, :, :cut], bits[1:])[0], halved(blocks[:, :, cut:], bits[:0:-1])[0]], axis=1
    ).astype(bf16)
    attention_block, arrived[2] = after((attention_block, arrived[2]))
    attention_block = attention_block.reshape(parts, weight_rows, -1)

    def block_for(steps):
        return lax.dynamic_index_in_dim(
            attention_block, (rank + steps) % parts, 0, keepdims=False
        )

    sums = block_for(0).astype(f32)
    for d in range(1, parts):
        sums = sums + around(block_for(d), d).astype(f32)

    total = middle + partials[0]
    for d in range(1, parts):
        total = total + arrived[d].astype(f32)

    edge = 2 * QW + 2 * KW
    return (
        total.astype(bf16)[None, :, None],
        input_grad[None, :, None],
        sums[:, edge],
        sums[:, QW : 2 * QW],
        sums[:, edge + 2],
        sums[:, 2 * QW : 2 * QW + KW],
        sums[:bias_rows, edge + 3],
        sums[:, 2 * QW + KW : edge],
        sums[:bias_rows, edge + 4],
        sums[:, :QW],
        sums[:, edge + 1],
        feed_sum[:, :hidden],
        feed_sum[:, hidden_pad : hidden_pad + hidden],
        feed_sum[:, 2 * hidden_pad : 2 * hidden_pad + hidden].T,
    )


def solution(mesh):
    both = ("dp", "ctx")
    rows = P(both, None)
    line = P(both)
    tokens = P("dp", None, None, "ctx", None)
    return jax.shard_map(
        body,
        mesh=mesh,
        in_specs=(
            tokens, P("dp", None, None, None), tokens, line, rows, line, rows, line, rows, line,
            rows, line, P("dp", "ctx"), P("dp", "ctx"), P("ctx", "dp"),
        ),
        out_specs=(
            tokens, tokens, line, rows, line, rows, line, rows, line, rows, line,
            P("dp", "ctx"), P("dp", "ctx"), P("ctx", "dp"),
        ),
        check_vma=False,
    )
```

```python
import functools
import jax, jax.numpy as jnp
from jax import lax
from jax.sharding import PartitionSpec as P
from jax.experimental import pallas as pl
from jax.experimental.pallas import tpu as pltpu
D=896; HEADS=14; KV_HEADS=2; HEAD=64; LANES=128
QW=896; KW=128
epsilon=1e-6
bf16=jnp.bfloat16; f32=jnp.float32
LIMIT=56*1024*1024
COST=pl.CostEstimate(flops=1, bytes_accessed=1, transcendentals=0)

def dot(left, right, left_dim, right_dim):
    return lax.dot_general(left, right, (((left_dim,), (right_dim,)), ((), ())), preferred_element_type=f32)

def half_turn(v, back):
    lane = lax.broadcasted_iota(jnp.int32, v.shape, 1) & (HEAD-1)
    width=v.shape[1]
    up = pltpu.roll(v, width-HEAD//2, 1)
    down = pltpu.roll(v, HEAD//2, 1)
    return jnp.where(lane < HEAD//2, up, down)

def scaled(v):
    return lax.rsqrt(jnp.mean(v*v, axis=-1, keepdims=True)+epsilon)

def pairs_kernel(x_ref, wkv_ref, ws_ref, spread_ref, cos_ref, sin_ref, kv_ref, n1_ref, rows_ref, bias_ref):
    @pl.when(pl.program_id(0)==0)
    def _():
        table = ws_ref[...].astype(f32).T[:8]
        rows_ref[...] = table
        close = dot(table.astype(bf16), spread_ref[...],1,0)
        bias_ref[:, :KW] = close[3:4]
        bias_ref[:, KW:] = close[4:5]
    x = x_ref[...].astype(f32)
    n1 = (x*scaled(x)*rows_ref[0:1]).astype(bf16)
    n1_ref[...] = n1
    kv = dot(n1, wkv_ref[...],1,0) + bias_ref[...]
    v = kv[:, :KW]
    kv_ref[:, :KW] = (v*cos_ref[...] + half_turn(v,False)*sin_ref[...]).astype(bf16)
    kv_ref[:, KW:] = kv[:, KW:].astype(bf16)

def queries_kernel(n1_ref, wq_ref, rows_ref, cos_ref, sin_ref, rq_ref):
    q = dot(n1_ref[...], wq_ref[...],1,0) + rows_ref[2:3]
    cos = cos_ref[...]; sin = sin_ref[...]
    for b in range(QW//LANES):
        v = q[:, b*LANES:(b+1)*LANES]
        r = (v*cos + half_turn(v,False)*sin).astype(bf16)
        rq_ref[:, b*LANES:(b+1)*LANES] = (r.astype(f32)*HEAD**-0.5).astype(bf16)

def project(x, first_set, spread, cos, sin):
    m, rows, _ = x.shape
    full=lambda shape,idx: pl.BlockSpec(shape, lambda i: idx)
    blk=lambda w: pl.BlockSpec((None,rows,w), lambda i:(i,0,0))
    sd=jax.ShapeDtypeStruct
    params=dict(compiler_params=pltpu.CompilerParams(vmem_limit_bytes=LIMIT), cost_estimate=COST)
    pair, n1, table = pl.pallas_call(
        pairs_kernel, grid=(m,),
        in_specs=[blk(D), full((D,2*KW),(0,7)), full((D,LANES),(0,16)), full((D,LANES),(0,0)), blk(LANES), blk(LANES)],
        out_specs=[blk(2*KW), blk(D), full((8,D),(0,0))],
        out_shape=[sd((m,rows,2*KW),bf16), sd((m,rows,D),bf16), sd((8,D),f32)],
        scratch_shapes=[pltpu.VMEM((1,2*KW),f32)],
        name="pairs", **params,
    )(x, first_set, first_set, spread, cos, sin)
    rq = pl.pallas_call(
        queries_kernel, grid=(m,),
        in_specs=[blk(D), full((D,QW),(0,1)), full((8,D),(0,0)), blk(LANES), blk(LANES)],
        out_specs=blk(QW), out_shape=sd((m,rows,QW),bf16),
        name="queries", **params,
    )(n1, first_set, table, cos, sin)
    return rq, pair, n1, table

BLOCK=128
def units():
    group=HEADS//KV_HEADS
    out=[]
    for g in range(KV_HEADS):
        for parity in range(2):
            blocks=[h//2 for h in range(g*group,(g+1)*group) if h%2==parity]
            out.append((g,parity,blocks))
    return out

def padded(v, g, parity, lane):
    if g != parity:
        v = pltpu.roll(v.astype(f32), HEAD, 1).astype(bf16)
    keep = (lane >= HEAD) if parity else (lane < HEAD)
    return jnp.where(keep, v, jnp.zeros_like(v))

def mask_bias(begins, rank_base, q0, window, reach):
    key = lax.broadcasted_iota(jnp.int32,(window,BLOCK),0) + (rank_base + q0 - reach)
    query = lax.broadcasted_iota(jnp.int32,(window,BLOCK),1) + (rank_base + q0)
    ok = (key >= begins) & (key <= query)
    return jnp.where(ok, 0.0, -1e30).astype(f32)

def fill_padded(kv_refs, k_ref, v_ref):
    rows = kv_refs[0].shape[0]
    lane = lax.broadcasted_iota(jnp.int32,(rows,LANES),1)
    for p,ref in enumerate(kv_refs):
        kv=ref[...]
        for g,parity,_ in units():
            u=2*g+parity
            k_ref[u, p*rows:(p+1)*rows] = padded(kv[:, :KW], g, parity, lane)
            v_ref[u, p*rows:(p+1)*rows] = padded(kv[:, KW:], g, parity, lane)

def attend_kernel(base_ref, rq_ref, kv0_ref, kv1_ref, kv2_ref, begin_ref, wo_ref, x_ref, rows_ref, *refs):
    n2_ref, mixed_ref, middle_ref, lse_ref, k_ref, v_ref = refs[-6:]
    qb = pl.program_id(0)
    rows = kv0_ref.shape[0]
    reach=512; window=reach+BLOCK
    @pl.when(qb==0)
    def _():
        fill_padded((kv2_ref,kv1_ref,kv0_ref), k_ref, v_ref)
    q0 = qb*BLOCK
    bias = mask_bias(begin_ref[...], base_ref[0], q0, window, reach)
    parts=[None]*7
    start = pl.multiple_of(q0 + (2*rows - reach), BLOCK)
    for g,parity,blocks in units():
        u=2*g+parity
        qs = jnp.concatenate([rq_ref[:, b*LANES:(b+1)*LANES] for b in blocks], axis=0)
        keys = k_ref[u, pl.ds(start,window)]
        vals = v_ref[u, pl.ds(start,window)]
        s = dot(keys, qs, 1, 1) + jnp.concatenate([bias]*len(blocks),axis=1)
        top = jnp.max(s, axis=0, keepdims=True)
        e = jnp.exp(s-top)
        total = jnp.sum(e, axis=0, keepdims=True)
        p = (e*(1.0/total)).astype(bf16)
        o = dot(vals, p, 0, 0)
        lse = top+jnp.log(total)
        for i,b in enumerate(blocks):
            piece=o[:, i*BLOCK:(i+1)*BLOCK]
            parts[b] = piece if parts[b] is None else parts[b]+piece
            lse_ref[0, 2*b+parity:2*b+parity+1, :] = lse[:, i*BLOCK:(i+1)*BLOCK]
    for b in range(7):
        mixed_ref[:, b*LANES:(b+1)*LANES] = parts[b].T.astype(bf16)
    middle = x_ref[...].astype(f32) + dot(mixed_ref[...], wo_ref[...],1,0)
    middle_ref[...] = middle
    n2_ref[...] = (middle*scaled(middle)*rows_ref[1:2]).astype(bf16)

def attend(m, base, rq, kvs, begins, first_set, x, rows_table, before):
    micros, rows, _ = rq.shape; nq=rows//BLOCK
    full=lambda shape: pl.BlockSpec(shape, lambda i: (0,)*len(shape))
    blk=lambda w: pl.BlockSpec((None,BLOCK,w), lambda i:(m,i,0))
    sd=jax.ShapeDtypeStruct
    return pl.pallas_call(
        attend_kernel, grid=(nq,),
        in_specs=[pl.BlockSpec(memory_space=pltpu.SMEM), blk(QW)]+[pl.BlockSpec((None,rows,2*KW),lambda i:(m,0,0))]*3+[pl.BlockSpec((None,1,BLOCK),lambda i:(m,0,i)), full((D,QW)), blk(D), full((8,D))]+[pl.BlockSpec(memory_space=pl.ANY)]*len(before),
        out_specs=[pl.BlockSpec((BLOCK,D),lambda i:(i,0)), blk(QW), blk(D), pl.BlockSpec((None,1,16,BLOCK),lambda i:(m,i,0,0))],
        out_shape=[sd((rows,D),bf16), sd((micros,rows,QW),bf16), sd((micros,rows,D),f32), sd((micros,nq,16,BLOCK),f32)],
        scratch_shapes=[pltpu.VMEM((4,3*rows,LANES),bf16), pltpu.VMEM((4,3*rows,LANES),bf16)],
        input_output_aliases={9+k:1+k for k in range(len(before))},
        compiler_params=pltpu.CompilerParams(vmem_limit_bytes=LIMIT), cost_estimate=COST,
        name="attend",
    )(base, rq, *kvs, begins, first_set, x, rows_table, *before)

def attend_back_kernel(base_ref, rq_ref, kv0_ref, kv1_ref, kv2_ref, begin_ref, wo_ref, rows_ref, lse_ref, middle_ref, dy_ref, cos_ref, sin_ref, *refs, count):
    gs=refs[:count]
    far1_ref, far2_ref, dmid_ref, dmb_ref, dq_ref, own_ref, gain_ref, k_ref, v_ref, dk_ref, dv_ref = refs[-11:]
    qb = pl.program_id(0); nq=pl.num_programs(0)
    rows = kv0_ref.shape[0]
    reach=512; window=reach+BLOCK
    @pl.when(qb==0)
    def _():
        fill_padded((kv2_ref,kv1_ref,kv0_ref), k_ref, v_ref)
        dk_ref[...] = jnp.zeros_like(dk_ref)
        dv_ref[...] = jnp.zeros_like(dv_ref)
        gain_ref[...] = jnp.zeros_like(gain_ref)
    dn2 = gs[0][...].astype(f32)
    for g_ref in gs[1:]:
        dn2 = dn2+g_ref[...].astype(f32)
    middle = middle_ref[...]
    inv = scaled(middle)
    gain_ref[...] += jnp.broadcast_to(jnp.sum(dn2*(middle*inv),axis=0,keepdims=True), gain_ref.shape)
    w2 = dn2*rows_ref[1:2]
    dmid = dy_ref[...].astype(f32) + inv*w2 - middle*(inv*inv*inv)*jnp.mean(w2*middle,axis=-1,keepdims=True)
    dmid_ref[...] = dmid
    dmb = dmid.astype(bf16)
    dmb_ref[...] = dmb
    dmixed = dot(dmb, wo_ref[...],1,1).astype(bf16)
    q0 = qb*BLOCK
    bias = mask_bias(begin_ref[...], base_ref[0], q0, window, reach)
    start = pl.multiple_of(q0 + (2*rows - reach), BLOCK)
    parts=[None]*7
    for g,parity,blocks in units():
        u=2*g+parity
        n=len(blocks)
        qs = jnp.concatenate([rq_ref[:, b*LANES:(b+1)*LANES] for b in blocks], axis=0)
        ds_ = jnp.concatenate([dmixed[:, b*LANES:(b+1)*LANES] for b in blocks], axis=0)
        keys = k_ref[u, pl.ds(start,window)]
        vals = v_ref[u, pl.ds(start,window)]
        lse = jnp.concatenate([lse_ref[0, 2*b+parity:2*b+parity+1, :] for b in blocks],axis=1)
        p = jnp.exp(dot(keys,qs,1,1) + jnp.concatenate([bias]*n,axis=1) - lse)
        dp = dot(vals, ds_, 1, 1)
        t = p*dp
        ds = (t-p*jnp.sum(t,axis=0,keepdims=True)).astype(bf16)
        pb = p.astype(bf16)
        o = dot(keys, ds, 0, 0)
        for i,b in enumerate(blocks):
            piece=o[:, i*BLOCK:(i+1)*BLOCK]
            parts[b] = piece if parts[b] is None else parts[b]+piece
        dk = dot(ds, qs, 1, 0); dv = dot(pb, ds_, 1, 0)
        keep = lax.broadcasted_iota(jnp.int32,(window,LANES),1)
        keep = (keep>=HEAD) if parity else (keep<HEAD)
        dk = jnp.where(keep, dk, 0.0); dv=jnp.where(keep,dv,0.0)
        if g!=parity:
            dk = pltpu.roll(dk,HEAD,1); dv=pltpu.roll(dv,HEAD,1)
        dk_ref[pl.ds(start,window)] += dk
        dv_ref[pl.ds(start,window)] += dv
    cos=cos_ref[...]; sin=sin_ref[...]
    for b in range(7):
        gq = parts[b].T*HEAD**-0.5
        dq_ref[:, b*LANES:(b+1)*LANES] = (gq*cos + half_turn(gq*sin,True)).astype(bf16)
    @pl.when(qb==nq-1)
    def _():
        own_ref[:, :KW] = dk_ref[2*rows:]; own_ref[:, KW:] = dv_ref[2*rows:]
        far1_ref[:, :KW] = dk_ref[rows:2*rows].astype(bf16); far1_ref[:, KW:] = dv_ref[rows:2*rows].astype(bf16)
        far2_ref[:, :KW] = dk_ref[:rows].astype(bf16); far2_ref[:, KW:] = dv_ref[:rows].astype(bf16)

def attend_back(m, base, rq, kvs, begins, first_set, rows_table, lse, middle, dy, gs, cos, sin, before):
    micros, rows, _ = rq.shape; nq=rows//BLOCK
    full=lambda shape: pl.BlockSpec(shape, lambda i: (0,)*len(shape))
    blk=lambda w: pl.BlockSpec((None,BLOCK,w), lambda i:(m,i,0))
    one=lambda h,w: pl.BlockSpec((None,h,w), lambda i:(m,0,0))
    sd=jax.ShapeDtypeStruct
    at=12+len(gs)
    return pl.pallas_call(
        functools.partial(attend_back_kernel,count=len(gs)), grid=(nq,),
        in_specs=[pl.BlockSpec(memory_space=pltpu.SMEM), blk(QW)]+[pl.BlockSpec((None,rows,2*KW),lambda i:(m,0,0))]*3+[pl.BlockSpec((None,1,BLOCK),lambda i:(m,0,i)), full((D,QW)), full((8,D)),
            pl.BlockSpec((None,1,16,BLOCK),lambda i:(m,i,0,0)), blk(D), blk(D)]+[blk(LANES)]*2+[pl.BlockSpec((BLOCK,D),lambda i:(i,0))]*len(gs)+[pl.BlockSpec(memory_space=pl.ANY)]*len(before),
        out_specs=[full((rows,2*KW)), full((rows,2*KW)), blk(D), blk(D), blk(QW), one(rows,2*KW), one(8,D)],
        out_shape=[sd((rows,2*KW),bf16), sd((rows,2*KW),bf16), sd((micros,rows,D),f32), sd((micros,rows,D),bf16), sd((micros,rows,QW),bf16), sd((micros,rows,2*KW),f32), sd((micros,8,D),f32)],
        scratch_shapes=[pltpu.VMEM((4,3*rows,LANES),bf16)]*2+[pltpu.VMEM((3*rows,LANES),f32)]*2,
        input_output_aliases={at+1+k:2+k for k in range(len(before))},
        compiler_params=pltpu.CompilerParams(vmem_limit_bytes=LIMIT), cost_estimate=COST,
        name="attend_back",
    )(base, rq, *kvs, begins, first_set, rows_table, lse, middle, dy, cos, sin, *gs, *before)

CHUNK=256

def feed_kernel(own_ref, *refs, parts, micro, kept):
    ts=refs[:parts]; gs=refs[parts:2*parts]; sets=refs[2*parts:2*parts+2]
    refs=refs[2*parts+2+kept:]
    backs=refs[:parts]; outs=refs[parts:2*parts]
    left_ref,pair_ref,act_ref,x_ref,y_ref,w_ref,own_buf,far_buf,w_sem,in_sem,out_sem=refs[2*parts:]
    i=pl.program_id(0)
    width=w_ref.shape[1]//3
    chunks=width//CHUNK
    def tokens(k):
        return (pltpu.make_async_copy(ts[k],x_ref.at[k],in_sem.at[0,k]),
                pltpu.make_async_copy(gs[k].at[micro],y_ref.at[k],in_sem.at[1,k]))
    def columns(which,j,p):
        c=slice(p*width+j*CHUNK,p*width+(j+1)*CHUNK)
        return pltpu.make_async_copy(sets[which].at[:,c],w_ref.at[:,c],w_sem.at[p,j])
    def results(k):
        if k==0:
            return (pltpu.make_async_copy(own_buf.at[0],outs[0].at[micro],out_sem.at[0,0]),
                    pltpu.make_async_copy(own_buf.at[1],backs[0],out_sem.at[1,0]))
        return (pltpu.make_async_copy(far_buf.at[0,k-1],outs[k].at[micro],out_sem.at[0,k]),
                pltpu.make_async_copy(far_buf.at[1,k-1],backs[k],out_sem.at[1,k]))
    @pl.when(i==0)
    def _():
        for copy in tokens(0): copy.start()
        for which in range(2):
            @pl.when(own_ref[0]==1-which)
            def _(which=which):
                for j in range(chunks):
                    for p in range(3): columns(which,j,p).start()
        for k in range(1,parts):
            for copy in tokens(k): copy.start()
    for k in range(parts):
        @pl.when(i==k)
        def _(k=k):
            for copy in tokens(k): copy.wait()
    @pl.when(i==0)
    def _():
        for j in range(chunks):
            for p in range(3): columns(0,j,p).wait()
    x=x_ref[i]; y=y_ref[i]
    left_ref[0]=x; left_ref[1]=y
    for j in range(chunks):
        c=slice(j*CHUNK,(j+1)*CHUNK); c2=slice(width+j*CHUNK,width+(j+1)*CHUNK); c3=slice(2*width+j*CHUNK,2*width+(j+1)*CHUNK)
        g=dot(x,w_ref[:,c],1,0); u=dot(x,w_ref[:,c2],1,0); da=dot(y,w_ref[:,c3],1,0)
        s=jax.nn.sigmoid(g)
        gs_=g*s
        act_ref[:,c]=(gs_*u).astype(bf16)
        pair_ref[:,c]=(da*u*s*(1.0+g*(1.0-s))).astype(bf16)
        pair_ref[:,c2]=(da*gs_).astype(bf16)
    out=dot(act_ref[...],w_ref[:,2*width:],1,1)
    res=dot(pair_ref[...],w_ref[:,:2*width],1,1)
    for k in range(parts):
        @pl.when(i==k)
        def _(k=k):
            if k==0:
                own_buf[0]=out; own_buf[1]=res
            else:
                far_buf[0,k-1]=out.astype(bf16); far_buf[1,k-1]=res.astype(bf16)
            for copy in results(k): copy.start()
    @pl.when(i==parts-1)
    def _():
        for k in range(parts):
            for copy in results(k): copy.wait()

def feed(own, toks, grads, sets, micro, micros, before):
    parts=len(toks); rows=toks[0].shape[0]; hidden_pad=sets[0].shape[1]//3
    blk=lambda w: pl.BlockSpec((rows,w), lambda i:(micro*parts+i,0))
    sd=jax.ShapeDtypeStruct
    everything=rows*parts*micros
    kept=len(before)
    hold=pl.BlockSpec(memory_space=pl.ANY)
    shapes=[sd((rows,D),f32)]+[sd((rows,D),bf16)]*(parts-1)+[sd((micros,rows,D),f32)]+[sd((micros,rows,D),bf16)]*(parts-1)
    n_in=1+2*parts+2
    dma=pltpu.SemaphoreType.DMA
    out=pl.pallas_call(
        functools.partial(feed_kernel,parts=parts,micro=micro,kept=kept), grid=(parts,),
        in_specs=[pl.BlockSpec(memory_space=pltpu.SMEM)]+[hold]*(2*parts+2+kept),
        out_specs=[hold]*(2*parts)+[pl.BlockSpec((2,rows,D), lambda i:(0,micro*parts+i,0)),blk(2*hidden_pad),blk(hidden_pad)],
        out_shape=shapes+[sd((2,everything,D),bf16)]+[sd((everything,w),bf16) for w in (2*hidden_pad,hidden_pad)],
        scratch_shapes=[pltpu.VMEM((parts,rows,D),bf16)]*2+[pltpu.VMEM(sets[0].shape,bf16),pltpu.VMEM((2,rows,D),f32),pltpu.VMEM((2,parts-1,rows,D),bf16),
            dma((3,hidden_pad//CHUNK)),dma((2,parts)),dma((2,parts))],
        input_output_aliases={n_in+k:parts+k for k in range(kept)},
        compiler_params=pltpu.CompilerParams(vmem_limit_bytes=LIMIT), cost_estimate=COST,
        name="feed",
    )(own,*toks,*grads,*sets,*before)
    return out[:parts], out[parts:]

def finish_kernel(bit_ref, dq_ref, own_ref, cos_ref, sin_ref, wq_ref, wkv_ref, rows_ref, x_ref, n1_ref, dmid_ref, mixed_ref, dmb_ref, spread_ref, gain2_ref, *refs, near, block):
    far=refs[:-6]
    ig_ref, keep_ref, send_ref, acc_ref, small_ref, sum_ref = refs[-6:]
    i=pl.program_id(0)
    @pl.when(i==0)
    def _():
        acc_ref[...]=jnp.zeros_like(acc_ref)
        small_ref[...]=jnp.zeros_like(small_ref)
    for m in range(len(far)//near):
        @pl.when(i==m)
        def _(m=m):
            own=own_ref[...]
            for ref in far[m*near:(m+1)*near]:
                own=own+ref[...].astype(f32)
            sum_ref[...]=own
    own=sum_ref[...]
    k=own[:, :KW]
    cos=cos_ref[...]; sin=sin_ref[...]
    dk=(k*cos+half_turn(k*sin,True)).astype(bf16)
    dv=own[:, KW:].astype(bf16)
    dkv=jnp.concatenate([dk,dv],axis=1)
    dq=dq_ref[...]
    dn1=dot(dq,wq_ref[...],1,1)+dot(dkv,wkv_ref[...],1,1)
    x=x_ref[...].astype(f32); inv=scaled(x)
    small_ref[0:1]+=jnp.sum(dn1*(x*inv),axis=0,keepdims=True)
    small_ref[1:2]+=gain2_ref[0:1]
    small_ref[2:3]+=jnp.sum(dq.astype(f32),axis=0,keepdims=True)
    small_ref[3:4,:2*KW]+=jnp.sum(dkv.astype(f32),axis=0,keepdims=True)
    w1=dn1*rows_ref[0:1]
    ig_ref[...]=dmid_ref[...]+inv*w1-x*(inv*inv*inv)*jnp.mean(w1*x,axis=-1,keepdims=True)
    n1=n1_ref[...]
    acc_ref[:, :QW]+=dot(mixed_ref[...],dmb_ref[...],0,0)
    acc_ref[:, QW:2*QW]+=dot(n1,dq,0,0)
    acc_ref[:, 2*QW:2*QW+2*KW]+=dot(n1,dkv,0,0)
    @pl.when(i==pl.num_programs(0)-1)
    def _():
        pair=jnp.concatenate([small_ref[3:4,:KW],small_ref[3:4,KW:2*KW],jnp.zeros((6,KW),f32)],axis=0).astype(bf16)
        table=jnp.concatenate([small_ref[0:3],dot(pair,spread_ref[...],1,1)[0:2],jnp.zeros((LANES-5,D),f32)],axis=0)
        acc_ref[:, 2*QW+2*KW:]=table.T
        if block:
            for j in range(D//block//2):
                at=pl.multiple_of((2*j+bit_ref[0])*block,16)
                keep_ref[j*block:(j+1)*block]=acc_ref[pl.ds(at,block)].astype(bf16)
                at=pl.multiple_of((2*j+1-bit_ref[0])*block,16)
                send_ref[j*block:(j+1)*block]=acc_ref[pl.ds(at,block)].astype(bf16)
        else:
            keep_ref[...]=acc_ref[:D//2].astype(bf16)
            send_ref[...]=acc_ref[D//2:].astype(bf16)

def finish(bit,dq,own,far,cos,sin,first_set,rows_table,x,n1,dmid,mixed,dmb,spread,gain2,block):
    m,rows,_=x.shape
    full=lambda shape,idx=(0,0): pl.BlockSpec(shape, lambda i: idx)
    blk=lambda w,h=rows: pl.BlockSpec((None,h,w), lambda i:(i,0,0))
    sd=jax.ShapeDtypeStruct
    width=2*QW+2*KW+LANES
    near=len(far[0])
    far=[f for pieces in far for f in pieces]
    return pl.pallas_call(
        functools.partial(finish_kernel,near=near,block=block), grid=(m,),
        in_specs=[pl.BlockSpec(memory_space=pltpu.SMEM),blk(QW),blk(2*KW),blk(LANES),blk(LANES),full((D,QW),(0,1)),full((D,2*KW),(0,7)),full((8,D)),blk(D),blk(D),blk(D),blk(QW),blk(D),full((D,LANES)),blk(D,8)]+[full((rows,2*KW))]*len(far),
        out_specs=[blk(D),full((D//2,width)),full((D//2,width))],
        out_shape=[sd((m,rows,D),f32),sd((D//2,width),bf16),sd((D//2,width),bf16)],
        scratch_shapes=[pltpu.VMEM((D,width),f32),pltpu.VMEM((8,D),f32),pltpu.VMEM((rows,2*KW),f32)],
        compiler_params=pltpu.CompilerParams(vmem_limit_bytes=LIMIT), cost_estimate=COST,
        name="finish",
    )(bit,dq,own,cos,sin,first_set,first_set,rows_table,x,n1,dmid,mixed,dmb,spread,gain2,*far)

def weights_kernel(left_ref, pair_ref, act_ref, out_ref, turned_ref, *, split):
    j=pl.program_id(0)
    @pl.when((j==0)|(j==split))
    def _(): turned_ref[...]=left_ref[...].T
    @pl.when(j<split)
    def _(): out_ref[...]=dot(turned_ref[...],pair_ref[...],1,0).astype(bf16)
    @pl.when(j>=split)
    def _(): out_ref[...]=dot(turned_ref[...],act_ref[...],1,0).astype(bf16)

def weights(left,pair,act,chunk=256):
    rows=left.shape[1]; width=pair.shape[1]+act.shape[1]; split=pair.shape[1]//chunk
    return pl.pallas_call(
        functools.partial(weights_kernel,split=split), grid=(width//chunk,),
        in_specs=[pl.BlockSpec((None,rows,D),lambda j:(jnp.where(j<split,0,1),0,0)),pl.BlockSpec((rows,chunk),lambda j:(0,jnp.minimum(j,split-1))),pl.BlockSpec((rows,chunk),lambda j:(0,jnp.maximum(j-split,0)))],
        out_specs=pl.BlockSpec((D,chunk),lambda j:(0,j)), out_shape=jax.ShapeDtypeStruct((D,width),bf16),
        scratch_shapes=[pltpu.VMEM((D,rows),bf16)],
        compiler_params=pltpu.CompilerParams(vmem_limit_bytes=LIMIT), cost_estimate=COST,
        name="weights",
    )(left,pair,act)


LONGEST = 512


def after(values_in, *needed):
    return lax.optimization_barrier((values_in, needed))[0]


theta = 10000.0


def body(
    layer_in,
    doc_ids,
    cotangent,
    first_gain,
    query_weight,
    query_bias,
    key_weight,
    key_bias,
    value_weight,
    value_bias,
    out_weight,
    second_gain,
    gate_weight,
    up_weight,
    down_weight,
):
    ctx = ("zh", "zb")
    dp = ("grp", "core")
    parts = lax.axis_size(ctx)
    rank = lax.axis_index(ctx)
    micros = layer_in.shape[1]
    shard_rows = layer_in.shape[3]
    hidden = gate_weight.shape[1]
    hidden_pad = -(-hidden // (2 * LANES)) * 2 * LANES
    weight_rows = query_weight.shape[0]
    bias_rows = key_bias.shape[0]
    reach_parts = -(-LONGEST // shard_rows)
    core = lax.axis_index("core")
    far_half = lax.axis_index("zh")

    def around(values_in, steps):
        return lax.ppermute(values_in, ctx, [(s, (s + steps) % parts) for s in range(parts)])

    def other(values_in, axis):
        return lax.ppermute(values_in, axis, [(0, 1), (1, 0)])

    def corner(values_in):
        return lax.ppermute(values_in, ("core", "zb"), [(s, 3 - s) for s in range(4)])

    def shared(values_in):
        beside = other(values_in, "zb")
        return [values_in, other(values_in, "core"), beside, other(beside, "core")]

    def collected(values_in):
        pieces = [values_in] + [around(values_in, d) for d in range(1, parts)]
        ordered = [pieces[d] for d in range(parts - 1, -1, -1)]
        ordered = jnp.stack(ordered + ordered[:-1])
        taken = lax.dynamic_slice_in_dim(ordered, parts - 1 - rank, parts, 0)
        return taken.reshape((-1,) + values_in.shape[1:])

    def column(values_in):
        return jnp.pad(values_in, (0, weight_rows - values_in.shape[0]))[:, None]

    def wide(values_in):
        return jnp.pad(values_in, ((0, 0), (0, hidden_pad - hidden)))

    own_block = jnp.concatenate([wide(gate_weight), wide(up_weight), wide(down_weight.T)], axis=1)
    own_set = lax.all_gather(own_block, dp, axis=0, tiled=True)
    small = jnp.concatenate(
        [column(v) for v in (first_gain, second_gain, query_bias, key_bias, value_bias)], axis=1
    )
    small = jnp.pad(small, ((0, 0), (0, LANES - small.shape[1])))
    own_attention = jnp.concatenate(
        [out_weight, query_weight, key_weight, value_weight, small], axis=1
    )
    first_block = collected(own_attention)
    own_block, first_block = after((own_block, first_block))
    other_block = other(own_block, "zh")
    first_block, other_block, own_set, upstream = after(
        (first_block, other_block, own_set, cotangent[0, :, 0])
    )
    first_set = lax.all_gather(first_block, dp, axis=0, tiled=True)
    upstream_pieces = shared(upstream)
    own_quarter = (core == far_half).astype(jnp.int32).reshape(1)

    row = jnp.arange(D, dtype=jnp.int32)[:, None]
    place = row // weight_rows * bias_rows + row % weight_rows
    spread = (
        (place == jnp.arange(LANES, dtype=jnp.int32)[None, :]) & (row % weight_rows < bias_rows)
    ).astype(bf16)

    docs = doc_ids[0, :, 0]
    own_docs = lax.dynamic_slice_in_dim(docs, rank * shard_rows, shard_rows, 1)
    begins = jnp.sum((docs[:, None, :] < own_docs[:, :, None]).astype(jnp.int32), axis=2)
    row_index = rank * shard_rows + jnp.arange(shard_rows, dtype=jnp.int32)
    positions = row_index[None, :] - begins
    frequency = jnp.power(f32(theta), -(jnp.arange(HEAD // 2, dtype=f32) * (2.0 / HEAD)))
    angle = positions.astype(f32)[:, :, None] * frequency
    cosines, sines = jnp.cos(angle), jnp.sin(angle)
    cosines = jnp.concatenate([cosines] * (2 * LANES // HEAD), axis=2)
    sines = jnp.concatenate([-sines, sines] * (LANES // HEAD), axis=2)
    base = (rank * shard_rows).reshape(1)

    tokens = layer_in[0, :, 0]
    first_set, other_block, upstream_pieces, spread, cosines, sines, begins = after(
        (first_set, other_block, upstream_pieces, spread, cosines, sines, begins)
    )
    other_set = lax.all_gather(other_block, dp, axis=0, tiled=True)
    sets = (own_set, other_set)

    rot_query, pairs, normed_one, rows_table = project(tokens, first_set, spread, cosines, sines)
    kvs = [pairs] + [
        lax.ppermute(pairs, ctx, [(s, s + d) for s in range(parts - d)])
        for d in range(1, reach_parts + 1)
    ]

    begins = begins[:, None, :]
    exchanged = []
    held = ()
    for m in range(micros):
        normed_two, *held = attend(
            m, base, rot_query, kvs, begins, first_set, tokens, rows_table, held
        )
        pieces = [normed_two, other(normed_two, "core"), other(normed_two, "zb")]
        if m < micros - 1:
            exchanged.append(pieces)
        else:
            exchanged.append(pieces + [corner(normed_two)])
            exchanged[:-1], normed_two = after((exchanged[:-1], normed_two))
            exchanged[-1][0] = normed_two
            for early in exchanged[:-1]:
                early.append(other(early[2], "core"))
    mixed, middle, log_sums = held

    backs = []
    before = ()
    for m in range(micros):
        back, before = feed(
            own_quarter, exchanged[m], upstream_pieces, sets, m, micros, before
        )
        backs.append([back[0], other(back[1], "core"), other(back[2], "zb"), corner(back[3])])
    partials = before[:4]
    out_near = other(partials[1], "core")
    out_far = other(partials[3], "core")

    feed_local = weights(*after(before[4:], backs[0]))
    backs, feed_local, out_near, out_far = after((backs, feed_local, out_near, out_far))
    far = []
    ended = ()
    out_beside = []
    for m in range(micros):
        out_sum = (partials[2][m].astype(f32) + out_far[m].astype(f32)).astype(bf16)
        out_beside.append(other(out_sum, "zb"))
        far1, far2, *ended = attend_back(
            m, base, rot_query, kvs, begins, first_set, rows_table, log_sums, middle, upstream,
            backs[m], cosines, sines, ended,
        )
        far1, far2, ended, out_beside = after((far1, far2, ended, out_beside))
        far.append(
            [
                lax.ppermute(part, ctx, [(s, s - d) for s in range(d, parts)])
                for d, part in ((1, far1), (2, far2))
            ]
        )
        if m < micros - 1:
            out_far, ended = after((out_far, ended))
    feed_half = lax.psum_scatter(feed_local, "grp", scatter_dimension=0, tiled=True)

    group_rank = lax.axis_index(dp)
    groups = lax.axis_size(dp)
    bits = [1 << k for k in range(groups.bit_length() - 1)]
    block_rows = parts * weight_rows
    even = block_rows % 16 == 0
    grad_middle, branch_low, query_grad, own_pair, gain_sum = ended
    input_grad, keep, send = finish(
        (group_rank % 2).reshape(1), query_grad, own_pair, far, cosines, sines, first_set,
        rows_table, tokens, normed_one, grad_middle, mixed, branch_low, spread, gain_sum,
        block_rows if even else 0,
    )
    if not even:
        both = jnp.concatenate([keep, send]).reshape(groups // 2, 2, block_rows, -1)
        keep, send = (
            lax.dynamic_index_in_dim(both, v, 1, keepdims=False)
            for v in (group_rank % 2, 1 - group_rank % 2)
        )

    def swapped(values_in, bit):
        return lax.ppermute(values_in, dp, [(s, s ^ bit) for s in range(groups)])

    def halved(blocks, order, k):
        bit = order[k]
        size = blocks.shape[0]
        at = sorted(order[k:]).index(bit)
        view = blocks.reshape((size >> (at + 1), 2, 1 << at) + blocks.shape[1:])
        own = (group_rank // bit) % 2
        kept = lax.dynamic_index_in_dim(view, own, 1, keepdims=False)
        sent = lax.dynamic_index_in_dim(view, 1 - own, 1, keepdims=False)
        got = swapped(sent.astype(bf16), bit)
        return (kept.astype(f32) + got.astype(f32)).reshape((size // 2,) + blocks.shape[1:])

    def delivered(k):
        part = lax.dynamic_index_in_dim(
            feed_half, (core + far_half + k) % 2, 0, keepdims=False
        )
        return lax.ppermute(
            part, ("core", "zh"), [(2 * s + a, 2 * (s ^ a ^ k) + s) for s in range(2) for a in range(2)]
        )

    feed_half = feed_half.reshape((2, -1) + feed_half.shape[1:])
    blocks = keep.astype(f32) + swapped(send, 1).astype(f32)
    blocks = blocks.reshape(groups // 2, block_rows, -1)
    cut = QW + 2 * LANES
    sides = [blocks[:, :, :cut], blocks[:, :, cut:]]
    orders = [bits[1:], bits[:0:-1]]
    for k in range(len(bits) - 1):
        sides = [halved(side, order, k) for side, order in zip(sides, orders)]
        if k == len(bits) - 3:
            sides, feed_half = after((sides, feed_half))
            feed_first = delivered(0)
    sides, feed_first = after((sides, feed_first))
    attention_block = jnp.concatenate([side[0] for side in sides], axis=1).astype(bf16)
    feed_last = delivered(1)
    attention_block = attention_block.reshape(parts, weight_rows, -1)

    def block_for(steps):
        return lax.dynamic_index_in_dim(
            attention_block, (rank + steps) % parts, 0, keepdims=False
        )

    sums = block_for(0).astype(f32)
    for d in range(1, parts):
        sums = sums + around(block_for(d), d).astype(f32)

    feed_sum = feed_first.astype(f32) + feed_last.astype(f32)

    total = middle + partials[0] + out_near.astype(f32) + jnp.stack(out_beside).astype(f32)

    edge = 2 * QW + 2 * KW
    return (
        total.astype(bf16)[None, :, None],
        input_grad[None, :, None],
        sums[:, edge],
        sums[:, QW : 2 * QW],
        sums[:, edge + 2],
        sums[:, 2 * QW : 2 * QW + KW],
        sums[:bias_rows, edge + 3],
        sums[:, 2 * QW + KW : edge],
        sums[:bias_rows, edge + 4],
        sums[:, :QW],
        sums[:, edge + 1],
        feed_sum[:, :hidden],
        feed_sum[:, hidden_pad : hidden_pad + hidden],
        feed_sum[:, 2 * hidden_pad : 2 * hidden_pad + hidden].T,
    )


def solution(mesh):
    groups, parts = mesh.devices.shape
    split = jax.sharding.Mesh(
        mesh.devices.reshape(groups // 2, 2, parts // 2, 2), ("grp", "core", "zh", "zb")
    )
    dp = ("grp", "core")
    ctx = ("zh", "zb")
    rows = P(dp + ctx, None)
    line = P(dp + ctx)
    tokens = P(dp, None, None, ctx, None)
    up = P(dp, ctx)
    return jax.shard_map(
        body,
        mesh=split,
        in_specs=(
            tokens, P(dp, None, None, None), tokens, line, rows, line, rows, line, rows, line,
            rows, line, up, up, P(ctx, dp),
        ),
        out_specs=(
            tokens, tokens, line, rows, line, rows, line, rows, line, rows, line,
            up, up, P(ctx, dp),
        ),
        check_vma=False,
    )
```

```python
import functools
import jax, jax.numpy as jnp
from jax import lax
from jax.sharding import PartitionSpec as P
from jax.experimental import pallas as pl
from jax.experimental.pallas import tpu as pltpu
D=896; HEADS=14; KV_HEADS=2; HEAD=64; LANES=128
QW=896; KW=128
epsilon=1e-6
bf16=jnp.bfloat16; f32=jnp.float32
LIMIT=56*1024*1024
COST=pl.CostEstimate(flops=1, bytes_accessed=1, transcendentals=0)

def dot(left, right, left_dim, right_dim):
    return lax.dot_general(left, right, (((left_dim,), (right_dim,)), ((), ())), preferred_element_type=f32)

def half_turn(v, back):
    lane = lax.broadcasted_iota(jnp.int32, v.shape, 1) & (HEAD-1)
    width=v.shape[1]
    up = pltpu.roll(v, width-HEAD//2, 1)
    down = pltpu.roll(v, HEAD//2, 1)
    return jnp.where(lane < HEAD//2, up, down)

def scaled(v):
    return lax.rsqrt(jnp.mean(v*v, axis=-1, keepdims=True)+epsilon)

def pairs_kernel(x_ref, wkv_ref, ws_ref, spread_ref, cos_ref, sin_ref, kv_ref, n1_ref, rows_ref, bias_ref):
    @pl.when(pl.program_id(0)==0)
    def _():
        table = ws_ref[...].astype(f32).T[:8]
        rows_ref[...] = table
        close = dot(table.astype(bf16), spread_ref[...],1,0)
        bias_ref[:, :KW] = close[3:4]
        bias_ref[:, KW:] = close[4:5]
    x = x_ref[...].astype(f32)
    n1 = (x*scaled(x)*rows_ref[0:1]).astype(bf16)
    n1_ref[...] = n1
    kv = dot(n1, wkv_ref[...],1,0) + bias_ref[...]
    v = kv[:, :KW]
    kv_ref[:, :KW] = (v*cos_ref[...] + half_turn(v,False)*sin_ref[...]).astype(bf16)
    kv_ref[:, KW:] = kv[:, KW:].astype(bf16)

def queries_kernel(n1_ref, wq_ref, rows_ref, cos_ref, sin_ref, rq_ref):
    q = dot(n1_ref[...], wq_ref[:, 2*KW:],1,0) + rows_ref[2:3]
    cos = cos_ref[...]; sin = sin_ref[...]
    for b in range(QW//LANES):
        v = q[:, b*LANES:(b+1)*LANES]
        r = (v*cos + half_turn(v,False)*sin).astype(bf16)
        rq_ref[:, b*LANES:(b+1)*LANES] = (r.astype(f32)*HEAD**-0.5).astype(bf16)

def project(x, out_set, in_set, spread, cos, sin):
    m, rows, _ = x.shape
    full=lambda shape,idx: pl.BlockSpec(shape, lambda i: idx)
    blk=lambda w: pl.BlockSpec((None,rows,w), lambda i:(i,0,0))
    sd=jax.ShapeDtypeStruct
    params=dict(compiler_params=pltpu.CompilerParams(vmem_limit_bytes=LIMIT), cost_estimate=COST)
    pair, n1, table = pl.pallas_call(
        pairs_kernel, grid=(m,),
        in_specs=[blk(D), full((D,2*KW),(0,0)), full((D,LANES),(0,QW//LANES)), full((D,LANES),(0,0)), blk(LANES), blk(LANES)],
        out_specs=[blk(2*KW), blk(D), full((8,D),(0,0))],
        out_shape=[sd((m,rows,2*KW),bf16), sd((m,rows,D),bf16), sd((8,D),f32)],
        scratch_shapes=[pltpu.VMEM((1,2*KW),f32)],
        name="pairs", **params,
    )(x, in_set, out_set, spread, cos, sin)
    rq = pl.pallas_call(
        queries_kernel, grid=(m,),
        in_specs=[blk(D), full((D,2*KW+QW),(0,0)), full((8,D),(0,0)), blk(LANES), blk(LANES)],
        out_specs=blk(QW), out_shape=sd((m,rows,QW),bf16),
        name="queries", **params,
    )(n1, in_set, table, cos, sin)
    return rq, pair, n1, table

BLOCK=128
def units():
    group=HEADS//KV_HEADS
    out=[]
    for g in range(KV_HEADS):
        for parity in range(2):
            blocks=[h//2 for h in range(g*group,(g+1)*group) if h%2==parity]
            out.append((g,parity,blocks))
    return out

def padded(v, g, parity, lane):
    if g != parity:
        v = pltpu.roll(v.astype(f32), HEAD, 1).astype(bf16)
    keep = (lane >= HEAD) if parity else (lane < HEAD)
    return jnp.where(keep, v, jnp.zeros_like(v))

def mask_bias(begins, rank_base, q0, window, reach):
    key = lax.broadcasted_iota(jnp.int32,(window,BLOCK),0) + (rank_base + q0 - reach)
    query = lax.broadcasted_iota(jnp.int32,(window,BLOCK),1) + (rank_base + q0)
    ok = (key >= begins) & (key <= query)
    return jnp.where(ok, 0.0, -1e30).astype(f32)

def fill_padded(kv_refs, k_ref, v_ref):
    rows = kv_refs[0].shape[0]
    lane = lax.broadcasted_iota(jnp.int32,(rows,LANES),1)
    for p,ref in enumerate(kv_refs):
        kv=ref[...]
        for g,parity,_ in units():
            u=2*g+parity
            k_ref[u, p*rows:(p+1)*rows] = padded(kv[:, :KW], g, parity, lane)
            v_ref[u, p*rows:(p+1)*rows] = padded(kv[:, KW:], g, parity, lane)

def attend_kernel(base_ref, rq_ref, kv0_ref, kv1_ref, kv2_ref, begin_ref, wo_ref, x_ref, rows_ref, *refs):
    n2_ref, mixed_ref, middle_ref, lse_ref, k_ref, v_ref = refs[-6:]
    qb = pl.program_id(0)
    rows = kv0_ref.shape[0]
    reach=512; window=reach+BLOCK
    @pl.when(qb==0)
    def _():
        fill_padded((kv2_ref,kv1_ref,kv0_ref), k_ref, v_ref)
    q0 = qb*BLOCK
    bias = mask_bias(begin_ref[...], base_ref[0], q0, window, reach)
    parts=[None]*7
    start = pl.multiple_of(q0 + (2*rows - reach), BLOCK)
    for g,parity,blocks in units():
        u=2*g+parity
        qs = jnp.concatenate([rq_ref[:, b*LANES:(b+1)*LANES] for b in blocks], axis=0)
        keys = k_ref[u, pl.ds(start,window)]
        vals = v_ref[u, pl.ds(start,window)]
        s = dot(keys, qs, 1, 1) + jnp.concatenate([bias]*len(blocks),axis=1)
        top = jnp.max(s, axis=0, keepdims=True)
        e = jnp.exp(s-top)
        total = jnp.sum(e, axis=0, keepdims=True)
        p = (e*(1.0/total)).astype(bf16)
        o = dot(vals, p, 0, 0)
        lse = top+jnp.log(total)
        for i,b in enumerate(blocks):
            piece=o[:, i*BLOCK:(i+1)*BLOCK]
            parts[b] = piece if parts[b] is None else parts[b]+piece
            lse_ref[0, 2*b+parity:2*b+parity+1, :] = lse[:, i*BLOCK:(i+1)*BLOCK]
    for b in range(7):
        mixed_ref[:, b*LANES:(b+1)*LANES] = parts[b].T.astype(bf16)
    middle = x_ref[...].astype(f32) + dot(mixed_ref[...], wo_ref[...],1,0)
    middle_ref[...] = middle
    n2_ref[...] = (middle*scaled(middle)*rows_ref[1:2]).astype(bf16)

def attend(m, base, rq, kvs, begins, out_set, x, rows_table, before):
    micros, rows, _ = rq.shape; nq=rows//BLOCK
    full=lambda shape: pl.BlockSpec(shape, lambda i: (0,)*len(shape))
    blk=lambda w: pl.BlockSpec((None,BLOCK,w), lambda i:(m,i,0))
    sd=jax.ShapeDtypeStruct
    return pl.pallas_call(
        attend_kernel, grid=(nq,),
        in_specs=[pl.BlockSpec(memory_space=pltpu.SMEM), blk(QW)]+[pl.BlockSpec((None,rows,2*KW),lambda i:(m,0,0))]*3+[pl.BlockSpec((None,1,BLOCK),lambda i:(m,0,i)), full((D,QW)), blk(D), full((8,D))]+[pl.BlockSpec(memory_space=pl.ANY)]*len(before),
        out_specs=[pl.BlockSpec((BLOCK,D),lambda i:(i,0)), blk(QW), blk(D), pl.BlockSpec((None,1,16,BLOCK),lambda i:(m,i,0,0))],
        out_shape=[sd((rows,D),bf16), sd((micros,rows,QW),bf16), sd((micros,rows,D),f32), sd((micros,nq,16,BLOCK),f32)],
        scratch_shapes=[pltpu.VMEM((4,3*rows,LANES),bf16), pltpu.VMEM((4,3*rows,LANES),bf16)],
        input_output_aliases={9+k:1+k for k in range(len(before))},
        compiler_params=pltpu.CompilerParams(vmem_limit_bytes=LIMIT), cost_estimate=COST,
        name="attend",
    )(base, rq, *kvs, begins, out_set, x, rows_table, *before)

def attend_back_kernel(base_ref, rq_ref, kv0_ref, kv1_ref, kv2_ref, begin_ref, wo_ref, rows_ref, lse_ref, middle_ref, dy_ref, cos_ref, sin_ref, *refs, count):
    gs=refs[:count]
    far1_ref, far2_ref, dmid_ref, dmb_ref, dq_ref, own_ref, gain_ref, k_ref, v_ref, dk_ref, dv_ref = refs[-11:]
    qb = pl.program_id(0); nq=pl.num_programs(0)
    rows = kv0_ref.shape[0]
    reach=512; window=reach+BLOCK
    @pl.when(qb==0)
    def _():
        fill_padded((kv2_ref,kv1_ref,kv0_ref), k_ref, v_ref)
        dk_ref[...] = jnp.zeros_like(dk_ref)
        dv_ref[...] = jnp.zeros_like(dv_ref)
        gain_ref[...] = jnp.zeros_like(gain_ref)
    dn2 = gs[0][...].astype(f32)
    for g_ref in gs[1:]:
        dn2 = dn2+g_ref[...].astype(f32)
    middle = middle_ref[...]
    inv = scaled(middle)
    gain_ref[...] += jnp.broadcast_to(jnp.sum(dn2*(middle*inv),axis=0,keepdims=True), gain_ref.shape)
    w2 = dn2*rows_ref[1:2]
    dmid = dy_ref[...].astype(f32) + inv*w2 - middle*(inv*inv*inv)*jnp.mean(w2*middle,axis=-1,keepdims=True)
    dmid_ref[...] = dmid
    dmb = dmid.astype(bf16)
    dmb_ref[...] = dmb
    dmixed = dot(dmb, wo_ref[...],1,1).astype(bf16)
    q0 = qb*BLOCK
    bias = mask_bias(begin_ref[...], base_ref[0], q0, window, reach)
    start = pl.multiple_of(q0 + (2*rows - reach), BLOCK)
    parts=[None]*7
    for g,parity,blocks in units():
        u=2*g+parity
        n=len(blocks)
        qs = jnp.concatenate([rq_ref[:, b*LANES:(b+1)*LANES] for b in blocks], axis=0)
        ds_ = jnp.concatenate([dmixed[:, b*LANES:(b+1)*LANES] for b in blocks], axis=0)
        keys = k_ref[u, pl.ds(start,window)]
        vals = v_ref[u, pl.ds(start,window)]
        lse = jnp.concatenate([lse_ref[0, 2*b+parity:2*b+parity+1, :] for b in blocks],axis=1)
        p = jnp.exp(dot(keys,qs,1,1) + jnp.concatenate([bias]*n,axis=1) - lse)
        dp = dot(vals, ds_, 1, 1)
        t = p*dp
        ds = (t-p*jnp.sum(t,axis=0,keepdims=True)).astype(bf16)
        pb = p.astype(bf16)
        o = dot(keys, ds, 0, 0)
        for i,b in enumerate(blocks):
            piece=o[:, i*BLOCK:(i+1)*BLOCK]
            parts[b] = piece if parts[b] is None else parts[b]+piece
        dk = dot(ds, qs, 1, 0); dv = dot(pb, ds_, 1, 0)
        keep = lax.broadcasted_iota(jnp.int32,(window,LANES),1)
        keep = (keep>=HEAD) if parity else (keep<HEAD)
        dk = jnp.where(keep, dk, 0.0); dv=jnp.where(keep,dv,0.0)
        if g!=parity:
            dk = pltpu.roll(dk,HEAD,1); dv=pltpu.roll(dv,HEAD,1)
        dk_ref[pl.ds(start,window)] += dk
        dv_ref[pl.ds(start,window)] += dv
    cos=cos_ref[...]; sin=sin_ref[...]
    for b in range(7):
        gq = parts[b].T*HEAD**-0.5
        dq_ref[:, b*LANES:(b+1)*LANES] = (gq*cos + half_turn(gq*sin,True)).astype(bf16)
    @pl.when(qb==nq-1)
    def _():
        own_ref[:, :KW] = dk_ref[2*rows:]; own_ref[:, KW:] = dv_ref[2*rows:]
        far1_ref[:, :KW] = dk_ref[rows:2*rows].astype(bf16); far1_ref[:, KW:] = dv_ref[rows:2*rows].astype(bf16)
        far2_ref[:, :KW] = dk_ref[:rows].astype(bf16); far2_ref[:, KW:] = dv_ref[:rows].astype(bf16)

def attend_back(m, base, rq, kvs, begins, out_set, rows_table, lse, middle, dy, gs, cos, sin, before):
    micros, rows, _ = rq.shape; nq=rows//BLOCK
    full=lambda shape: pl.BlockSpec(shape, lambda i: (0,)*len(shape))
    blk=lambda w: pl.BlockSpec((None,BLOCK,w), lambda i:(m,i,0))
    one=lambda h,w: pl.BlockSpec((None,h,w), lambda i:(m,0,0))
    sd=jax.ShapeDtypeStruct
    at=12+len(gs)
    return pl.pallas_call(
        functools.partial(attend_back_kernel,count=len(gs)), grid=(nq,),
        in_specs=[pl.BlockSpec(memory_space=pltpu.SMEM), blk(QW)]+[pl.BlockSpec((None,rows,2*KW),lambda i:(m,0,0))]*3+[pl.BlockSpec((None,1,BLOCK),lambda i:(m,0,i)), full((D,QW)), full((8,D)),
            pl.BlockSpec((None,1,16,BLOCK),lambda i:(m,i,0,0)), blk(D), blk(D)]+[blk(LANES)]*2+[pl.BlockSpec((BLOCK,D),lambda i:(i,0))]*len(gs)+[pl.BlockSpec(memory_space=pl.ANY)]*len(before),
        out_specs=[full((rows,2*KW)), full((rows,2*KW)), blk(D), blk(D), blk(QW), one(rows,2*KW), one(8,D)],
        out_shape=[sd((rows,2*KW),bf16), sd((rows,2*KW),bf16), sd((micros,rows,D),f32), sd((micros,rows,D),bf16), sd((micros,rows,QW),bf16), sd((micros,rows,2*KW),f32), sd((micros,8,D),f32)],
        scratch_shapes=[pltpu.VMEM((4,3*rows,LANES),bf16)]*2+[pltpu.VMEM((3*rows,LANES),f32)]*2,
        input_output_aliases={at+1+k:2+k for k in range(len(before))},
        compiler_params=pltpu.CompilerParams(vmem_limit_bytes=LIMIT), cost_estimate=COST,
        name="attend_back",
    )(base, rq, *kvs, begins, out_set, rows_table, lse, middle, dy, cos, sin, *gs, *before)

CHUNK=256

def feed_kernel(own_ref, *refs, parts, micro, kept):
    ts=refs[:parts]; gs=refs[parts:2*parts]; sets=refs[2*parts:2*parts+2]
    refs=refs[2*parts+2+kept:]
    backs=refs[:parts]; outs=refs[parts:2*parts]
    left_ref,pair_ref,act_ref,x_ref,y_ref,w_ref,own_buf,far_buf,w_sem,in_sem,out_sem=refs[2*parts:]
    i=pl.program_id(0)
    width=w_ref.shape[1]//3
    chunks=width//CHUNK
    def tokens(k):
        return (pltpu.make_async_copy(ts[k],x_ref.at[k],in_sem.at[0,k]),
                pltpu.make_async_copy(gs[k],y_ref.at[k],in_sem.at[1,k]))
    def columns(which,j,p):
        c=slice(p*width+j*CHUNK,p*width+(j+1)*CHUNK)
        return pltpu.make_async_copy(sets[which].at[:,c],w_ref.at[:,c],w_sem.at[p,j])
    def results(k):
        if k==0:
            return (pltpu.make_async_copy(own_buf.at[0],outs[0].at[micro],out_sem.at[0,0]),
                    pltpu.make_async_copy(own_buf.at[1],backs[0],out_sem.at[1,0]))
        return (pltpu.make_async_copy(far_buf.at[0,k-1],outs[k].at[micro],out_sem.at[0,k]),
                pltpu.make_async_copy(far_buf.at[1,k-1],backs[k],out_sem.at[1,k]))
    @pl.when(i==0)
    def _():
        for copy in tokens(0): copy.start()
        for which in range(2):
            @pl.when(own_ref[0]==1-which)
            def _(which=which):
                for j in range(chunks):
                    for p in range(3): columns(which,j,p).start()
        for k in range(1,parts):
            for copy in tokens(k): copy.start()
    for k in range(parts):
        @pl.when(i==k)
        def _(k=k):
            for copy in tokens(k): copy.wait()
    @pl.when(i==0)
    def _():
        for j in range(chunks):
            for p in range(3): columns(0,j,p).wait()
    x=x_ref[i]; y=y_ref[i]
    left_ref[0]=x; left_ref[1]=y
    for j in range(chunks):
        c=slice(j*CHUNK,(j+1)*CHUNK); c2=slice(width+j*CHUNK,width+(j+1)*CHUNK); c3=slice(2*width+j*CHUNK,2*width+(j+1)*CHUNK)
        g=dot(x,w_ref[:,c],1,0); u=dot(x,w_ref[:,c2],1,0); da=dot(y,w_ref[:,c3],1,0)
        s=jax.nn.sigmoid(g)
        gs_=g*s
        act_ref[:,c]=(gs_*u).astype(bf16)
        pair_ref[:,c]=(da*u*s*(1.0+g*(1.0-s))).astype(bf16)
        pair_ref[:,c2]=(da*gs_).astype(bf16)
    out=dot(act_ref[...],w_ref[:,2*width:],1,1)
    res=dot(pair_ref[...],w_ref[:,:2*width],1,1)
    for k in range(parts):
        @pl.when(i==k)
        def _(k=k):
            if k==0:
                own_buf[0]=out; own_buf[1]=res
            else:
                far_buf[0,k-1]=out.astype(bf16); far_buf[1,k-1]=res.astype(bf16)
            for copy in results(k): copy.start()
    @pl.when(i==parts-1)
    def _():
        for k in range(parts):
            for copy in results(k): copy.wait()

def feed(own, toks, grads, sets, micro, micros, before):
    parts=len(toks); rows=toks[0].shape[0]; hidden_pad=sets[0].shape[1]//3
    blk=lambda w: pl.BlockSpec((rows,w), lambda i:(micro*parts+i,0))
    sd=jax.ShapeDtypeStruct
    everything=rows*parts*micros
    kept=len(before)
    hold=pl.BlockSpec(memory_space=pl.ANY)
    shapes=[sd((rows,D),f32)]+[sd((rows,D),bf16)]*(parts-1)+[sd((micros,rows,D),f32)]+[sd((micros,rows,D),bf16)]*(parts-1)
    n_in=1+2*parts+2
    dma=pltpu.SemaphoreType.DMA
    out=pl.pallas_call(
        functools.partial(feed_kernel,parts=parts,micro=micro,kept=kept), grid=(parts,),
        in_specs=[pl.BlockSpec(memory_space=pltpu.SMEM)]+[hold]*(2*parts+2+kept),
        out_specs=[hold]*(2*parts)+[pl.BlockSpec((2,rows,D), lambda i:(0,micro*parts+i,0)),blk(2*hidden_pad),blk(hidden_pad)],
        out_shape=shapes+[sd((2,everything,D),bf16)]+[sd((everything,w),bf16) for w in (2*hidden_pad,hidden_pad)],
        scratch_shapes=[pltpu.VMEM((parts,rows,D),bf16)]*2+[pltpu.VMEM(sets[0].shape,bf16),pltpu.VMEM((2,rows,D),f32),pltpu.VMEM((2,parts-1,rows,D),bf16),
            dma((3,hidden_pad//CHUNK)),dma((2,parts)),dma((2,parts))],
        input_output_aliases={n_in+k:parts+k for k in range(kept)},
        compiler_params=pltpu.CompilerParams(vmem_limit_bytes=LIMIT), cost_estimate=COST,
        name="feed",
    )(own,*toks,*grads,*sets,*before)
    return out[:parts], out[parts:]

def finish_kernel(bit_ref, dq_ref, own_ref, cos_ref, sin_ref, wq_ref, wkv_ref, rows_ref, x_ref, n1_ref, dmid_ref, mixed_ref, dmb_ref, spread_ref, gain2_ref, *refs, near, block):
    far=refs[:-6]
    ig_ref, keep_ref, send_ref, acc_ref, small_ref, sum_ref = refs[-6:]
    i=pl.program_id(0)
    @pl.when(i==0)
    def _():
        acc_ref[...]=jnp.zeros_like(acc_ref)
        small_ref[...]=jnp.zeros_like(small_ref)
    for m in range(len(far)//near):
        @pl.when(i==m)
        def _(m=m):
            own=own_ref[...]
            for ref in far[m*near:(m+1)*near]:
                own=own+ref[...].astype(f32)
            sum_ref[...]=own
    own=sum_ref[...]
    k=own[:, :KW]
    cos=cos_ref[...]; sin=sin_ref[...]
    dk=(k*cos+half_turn(k*sin,True)).astype(bf16)
    dv=own[:, KW:].astype(bf16)
    dkv=jnp.concatenate([dk,dv],axis=1)
    dq=dq_ref[...]
    dn1=dot(dq,wq_ref[:, 2*KW:],1,1)+dot(dkv,wkv_ref[...],1,1)
    x=x_ref[...].astype(f32); inv=scaled(x)
    small_ref[0:1]+=jnp.sum(dn1*(x*inv),axis=0,keepdims=True)
    small_ref[1:2]+=gain2_ref[0:1]
    small_ref[2:3]+=jnp.sum(dq.astype(f32),axis=0,keepdims=True)
    small_ref[3:4,:2*KW]+=jnp.sum(dkv.astype(f32),axis=0,keepdims=True)
    w1=dn1*rows_ref[0:1]
    ig_ref[...]=dmid_ref[...]+inv*w1-x*(inv*inv*inv)*jnp.mean(w1*x,axis=-1,keepdims=True)
    n1=n1_ref[...]
    acc_ref[:, :QW]+=dot(mixed_ref[...],dmb_ref[...],0,0)
    acc_ref[:, QW:2*QW]+=dot(n1,dq,0,0)
    acc_ref[:, 2*QW:2*QW+2*KW]+=dot(n1,dkv,0,0)
    @pl.when(i==pl.num_programs(0)-1)
    def _():
        pair=jnp.concatenate([small_ref[3:4,:KW],small_ref[3:4,KW:2*KW],jnp.zeros((6,KW),f32)],axis=0).astype(bf16)
        table=jnp.concatenate([small_ref[0:3],dot(pair,spread_ref[...],1,1)[0:2],jnp.zeros((LANES-5,D),f32)],axis=0)
        acc_ref[:, 2*QW+2*KW:]=table.T
        if block:
            for j in range(D//block//2):
                at=pl.multiple_of((2*j+bit_ref[0])*block,16)
                keep_ref[j*block:(j+1)*block]=acc_ref[pl.ds(at,block)].astype(bf16)
                at=pl.multiple_of((2*j+1-bit_ref[0])*block,16)
                send_ref[j*block:(j+1)*block]=acc_ref[pl.ds(at,block)].astype(bf16)
        else:
            keep_ref[...]=acc_ref[:D//2].astype(bf16)
            send_ref[...]=acc_ref[D//2:].astype(bf16)

def finish(bit,dq,own,far,cos,sin,in_set,rows_table,x,n1,dmid,mixed,dmb,spread,gain2,block):
    m,rows,_=x.shape
    full=lambda shape,idx=(0,0): pl.BlockSpec(shape, lambda i: idx)
    blk=lambda w,h=rows: pl.BlockSpec((None,h,w), lambda i:(i,0,0))
    sd=jax.ShapeDtypeStruct
    width=2*QW+2*KW+LANES
    near=len(far[0])
    far=[f for pieces in far for f in pieces]
    return pl.pallas_call(
        functools.partial(finish_kernel,near=near,block=block), grid=(m,),
        in_specs=[pl.BlockSpec(memory_space=pltpu.SMEM),blk(QW),blk(2*KW),blk(LANES),blk(LANES),full((D,2*KW+QW)),full((D,2*KW)),full((8,D)),blk(D),blk(D),blk(D),blk(QW),blk(D),full((D,LANES)),blk(D,8)]+[full((rows,2*KW))]*len(far),
        out_specs=[blk(D),full((D//2,width)),full((D//2,width))],
        out_shape=[sd((m,rows,D),f32),sd((D//2,width),bf16),sd((D//2,width),bf16)],
        scratch_shapes=[pltpu.VMEM((D,width),f32),pltpu.VMEM((8,D),f32),pltpu.VMEM((rows,2*KW),f32)],
        compiler_params=pltpu.CompilerParams(vmem_limit_bytes=LIMIT), cost_estimate=COST,
        name="finish",
    )(bit,dq,own,cos,sin,in_set,in_set,rows_table,x,n1,dmid,mixed,dmb,spread,gain2,*far)

def weights_kernel(left_ref, right_ref, out_ref, turned_ref):
    @pl.when(pl.program_id(0)==0)
    def _(): turned_ref[...]=left_ref[...].T
    out_ref[...]=dot(turned_ref[...],right_ref[...],1,0).astype(bf16)

def weights(left,which,right,chunk):
    rows=left.shape[1]; width=right.shape[1]
    return pl.pallas_call(
        weights_kernel, grid=(width//chunk,),
        in_specs=[pl.BlockSpec((None,rows,D),lambda j:(which,0,0),pipeline_mode=pl.Buffered(1)),pl.BlockSpec((rows,chunk),lambda j:(0,j))],
        out_specs=pl.BlockSpec((D,chunk),lambda j:(0,j)), out_shape=jax.ShapeDtypeStruct((D,width),bf16),
        scratch_shapes=[pltpu.VMEM((D,rows),bf16)],
        compiler_params=pltpu.CompilerParams(vmem_limit_bytes=LIMIT), cost_estimate=COST,
        name="weights",
    )(left,right)

def woven_kernel(core_ref, *refs):
    n=len(refs)//3
    mine=refs[:n]; got=refs[n:2*n]; outs=refs[2*n:]
    core=core_ref[0]; j=pl.program_id(0)
    for k in range(n):
        rows=mine[k].shape[0]
        outs[k][pl.ds(pl.multiple_of(core*rows,16),rows)]=mine[k][...]
        outs[k][pl.ds(pl.multiple_of((1-core)*rows,16),rows)]=got[k][...]

def woven(core, mine, got):
    n=len(mine); blocks,rows,_=mine[0].shape
    shapes=[jax.ShapeDtypeStruct((2*blocks*rows,v.shape[2]),v.dtype) for v in mine]
    return pl.pallas_call(
        woven_kernel, grid=(blocks,), in_specs=[pl.BlockSpec(memory_space=pltpu.SMEM)]+[pl.BlockSpec((None,)+v.shape[1:],lambda j:(j,0,0)) for v in mine+got],
        out_specs=[pl.BlockSpec((2*rows,v.shape[2]),lambda j:(j,0)) for v in mine], out_shape=shapes,
        compiler_params=pltpu.CompilerParams(vmem_limit_bytes=LIMIT), cost_estimate=COST,
        name="woven",
    )(core,*mine,*got)


LONGEST = 512


def after(values_in, *needed):
    return lax.optimization_barrier((values_in, needed))[0]


theta = 10000.0


def body(
    layer_in,
    doc_ids,
    cotangent,
    first_gain,
    query_weight,
    query_bias,
    key_weight,
    key_bias,
    value_weight,
    value_bias,
    out_weight,
    second_gain,
    gate_weight,
    up_weight,
    down_weight,
):
    ctx = ("zh", "zb")
    dp = ("grp", "core")
    parts = lax.axis_size(ctx)
    rank = lax.axis_index(ctx)
    micros = layer_in.shape[1]
    shard_rows = layer_in.shape[3]
    hidden = gate_weight.shape[1]
    hidden_pad = -(-hidden // (2 * LANES)) * 2 * LANES
    weight_rows = query_weight.shape[0]
    bias_rows = key_bias.shape[0]
    reach_parts = -(-LONGEST // shard_rows)
    core = lax.axis_index("core")
    far_half = lax.axis_index("zh")

    group_rank = lax.axis_index(dp)
    groups = lax.axis_size(dp)
    bits = [1 << k for k in range(groups.bit_length() - 1)]
    block_rows = parts * weight_rows
    even = block_rows % 16 == 0

    def swapped(values_in, bit):
        return lax.ppermute(values_in, dp, [(s, s ^ bit) for s in range(groups)])

    def doubled(blocks, order, k):
        bit = order[k]
        got = swapped(blocks, bit)
        low = (group_rank // bit) % 2 == 0
        at = sum(earlier > bit for earlier in order[:k])
        return jnp.stack([jnp.where(low, blocks, got), jnp.where(low, got, blocks)], axis=at)

    def around(values_in, steps):
        return lax.ppermute(values_in, ctx, [(s, (s + steps) % parts) for s in range(parts)])

    def other(values_in, axis):
        return lax.ppermute(values_in, axis, [(0, 1), (1, 0)])

    def corner(values_in):
        return lax.ppermute(values_in, ("core", "zb"), [(s, 3 - s) for s in range(4)])

    def shared(values_in):
        beside = other(values_in, "zb")
        return [values_in, other(values_in, "core"), beside, other(beside, "core")]

    def collected(values_in):
        pieces = [values_in] + [around(values_in, d) for d in range(1, parts)]
        ordered = [pieces[d] for d in range(parts - 1, -1, -1)]
        ordered = jnp.stack(ordered + ordered[:-1])
        taken = lax.dynamic_slice_in_dim(ordered, parts - 1 - rank, parts, 0)
        return taken.reshape((-1,) + values_in.shape[1:])

    def column(values_in):
        return jnp.pad(values_in, (0, weight_rows - values_in.shape[0]))[:, None]

    def wide(values_in):
        return jnp.pad(values_in, ((0, 0), (0, hidden_pad - hidden)))

    own_block = jnp.concatenate([wide(gate_weight), wide(up_weight), wide(down_weight.T)], axis=1)
    own_set = lax.all_gather(own_block, dp, axis=0, tiled=True)
    small = jnp.concatenate(
        [column(v) for v in (first_gain, second_gain, query_bias, key_bias, value_bias)], axis=1
    )
    small = jnp.pad(small, ((0, 0), (0, LANES - small.shape[1])))
    own_attention = jnp.concatenate(
        [out_weight, small, key_weight, value_weight, query_weight], axis=1
    )
    first_block = collected(own_attention)
    row = jnp.arange(D, dtype=jnp.int32)[:, None]
    place = row // weight_rows * bias_rows + row % weight_rows
    spread = (
        (place == jnp.arange(LANES, dtype=jnp.int32)[None, :]) & (row % weight_rows < bias_rows)
    ).astype(bf16)

    docs = doc_ids[0, :, 0]
    own_docs = lax.dynamic_slice_in_dim(docs, rank * shard_rows, shard_rows, 1)
    begins = jnp.sum((docs[:, None, :] < own_docs[:, :, None]).astype(jnp.int32), axis=2)
    row_index = rank * shard_rows + jnp.arange(shard_rows, dtype=jnp.int32)
    positions = row_index[None, :] - begins
    frequency = jnp.power(f32(theta), -(jnp.arange(HEAD // 2, dtype=f32) * (2.0 / HEAD)))
    angle = positions.astype(f32)[:, :, None] * frequency
    cosines, sines = jnp.cos(angle), jnp.sin(angle)
    cosines = jnp.concatenate([cosines] * (2 * LANES // HEAD), axis=2)
    sines = jnp.concatenate([-sines, sines] * (LANES // HEAD), axis=2)
    base = (rank * shard_rows).reshape(1)

    own_block, first_block = after((own_block, first_block))
    cut = QW + LANES
    firsts = [first_block[:, :cut], first_block[:, cut:]]
    gather_orders = [bits[1:] + bits[:1], bits[:0:-1] + bits[:1]]
    widths = own_block.shape[1] // LANES // 4 * LANES
    edges = [0, widths, own_block.shape[1] - widths, own_block.shape[1]]
    other_block = []
    upstream = [cotangent[0, m, 0] for m in range(micros)]
    crossed = []
    for k in range(len(bits)):
        if k < len(bits) - 1 or not even:
            firsts = [doubled(side, order, k) for side, order in zip(firsts, gather_orders)]
        else:
            gots = [swapped(side, 1) for side in firsts]
            firsts = [firsts, gots]
        if k < 3:
            other_block.append(other(own_block[:, edges[k] : edges[k + 1]], "zh"))
        firsts, other_block, own_block, spread, cosines, sines, begins, upstream, crossed = after(
            (firsts, other_block, own_block, spread, cosines, sines, begins, upstream, crossed)
        )
    other_set = lax.all_gather(jnp.concatenate(other_block, axis=1), dp, axis=0, tiled=True)
    if even:
        firsts, gots = ([v.reshape((-1,) + v.shape[-2:]) for v in part] for part in firsts)
        out_set, in_set = woven(core.reshape(1), firsts, gots)
        crossed.append(other(upstream[0], "zb"))
        out_set, in_set, crossed = after((out_set, in_set, crossed))
    else:
        out_set, in_set = (side.reshape(-1, side.shape[-1]) for side in firsts)
        crossed.append(other(upstream[0], "zb"))
    sets = (own_set, other_set)
    own_quarter = (core == far_half).astype(jnp.int32).reshape(1)

    tokens = layer_in[0, :, 0]
    rot_query, pairs, normed_one, rows_table = project(
        tokens, out_set, in_set, spread, cosines, sines
    )
    kvs = [pairs] + [
        lax.ppermute(pairs, ctx, [(s, s + d) for s in range(parts - d)])
        for d in range(1, reach_parts + 1)
    ]

    kvs, rot_query, upstream = after((kvs, rot_query, upstream))
    crossed += [other(u, "zb") for u in upstream[1:]]
    upstream_pieces = [[u, other(u, "core"), v] for u, v in zip(upstream, crossed)]

    begins = begins[:, None, :]
    exchanged = []
    held = ()
    for m in range(micros):
        normed_two, *held = attend(
            m, base, rot_query, kvs, begins, out_set, tokens, rows_table, held
        )
        exchanged.append([normed_two, other(normed_two, "core"), other(normed_two, "zb")])
    exchanged[-1].append(corner(normed_two))
    exchanged[:-1], upstream_pieces[0], exchanged[-1][0] = after(
        (exchanged[:-1], upstream_pieces[0], normed_two)
    )
    for early in exchanged[:-1] + upstream_pieces[:1]:
        early.append(other(early[2], "core"))
    mixed, middle, log_sums = held

    backs = []
    before = ()
    for m in range(micros):
        back, before = feed(
            own_quarter, exchanged[m], upstream_pieces[m], sets, m, micros, before
        )
        if m < micros - 1:
            back, upstream_pieces[m + 1] = after((back, upstream_pieces[m + 1]))
            upstream_pieces[m + 1].append(other(upstream_pieces[m + 1][2], "core"))
        backs.append([back[0], other(back[1], "core"), other(back[2], "zb"), corner(back[3])])
    partials = before[:4]
    out_near = other(partials[1], "core")
    out_far = other(partials[3], "core")

    left, pair, act = after(before[4:], backs[0])
    feed_pair = weights(left, 0, pair, 512)
    feed_down = weights(left, 1, act, 640)
    backs, feed_pair, feed_down, out_near, out_far = after(
        (backs, feed_pair, feed_down, out_near, out_far)
    )
    feed_pair = lax.psum_scatter(feed_pair, "grp", scatter_dimension=0, tiled=True)

    far = []
    ended = ()
    out_beside = []
    for m in range(micros):
        out_sum = (partials[2][m].astype(f32) + out_far[m].astype(f32)).astype(bf16)
        out_beside.append(other(out_sum, "zb"))
        far1, far2, *ended = attend_back(
            m, base, rot_query, kvs, begins, out_set, rows_table, log_sums, middle, cotangent[0, :, 0],
            backs[m], cosines, sines, ended,
        )
        far1, far2, ended, out_beside = after((far1, far2, ended, out_beside))
        far.append(
            [
                lax.ppermute(part, ctx, [(s, s - d) for s in range(d, parts)])
                for d, part in ((1, far1), (2, far2))
            ]
        )
        if m < micros - 1:
            out_far, ended = after((out_far, ended))
    grad_middle, branch_low, query_grad, own_pair, gain_sum = ended
    input_grad, keep, send = finish(
        (group_rank % 2).reshape(1), query_grad, own_pair, far, cosines, sines, in_set,
        rows_table, tokens, normed_one, grad_middle, mixed, branch_low, spread, gain_sum,
        block_rows if even else 0,
    )
    keep, send, feed_pair, feed_down = after((keep, send, feed_pair, feed_down))
    feed_down = lax.psum_scatter(feed_down, "grp", scatter_dimension=0, tiled=True)
    if not even:
        both = jnp.concatenate([keep, send]).reshape(groups // 2, 2, block_rows, -1)
        keep, send = (
            lax.dynamic_index_in_dim(both, v, 1, keepdims=False)
            for v in (group_rank % 2, 1 - group_rank % 2)
        )

    def halved(blocks, order, k):
        bit = order[k]
        size = blocks.shape[0]
        at = sorted(order[k:]).index(bit)
        view = blocks.reshape((size >> (at + 1), 2, 1 << at) + blocks.shape[1:])
        own = (group_rank // bit) % 2
        kept = lax.dynamic_index_in_dim(view, own, 1, keepdims=False)
        sent = lax.dynamic_index_in_dim(view, 1 - own, 1, keepdims=False)
        got = swapped(sent.astype(bf16), bit)
        return (kept.astype(f32) + got.astype(f32)).reshape((size // 2,) + blocks.shape[1:])

    def delivered(half, k):
        part = lax.dynamic_index_in_dim(
            half.reshape((2, -1) + half.shape[1:]), (core + far_half + k) % 2, 0, keepdims=False
        )
        return lax.ppermute(
            part, ("core", "zh"), [(2 * s + a, 2 * (s ^ a ^ k) + s) for s in range(2) for a in range(2)]
        )

    blocks = keep.astype(f32) + swapped(send, 1).astype(f32)
    blocks = blocks.reshape(groups // 2, block_rows, -1)
    cut = QW + 2 * LANES
    sides = [blocks[:, :, :cut], blocks[:, :, cut:]]
    orders = [bits[1:], bits[:0:-1]]
    pair_parts = []
    for k in range(len(bits) - 1):
        if k < 2:
            pair_parts.append(delivered(feed_pair, k))
        sides = [halved(side, order, k) for side, order in zip(sides, orders)]
        if k == len(bits) - 2:
            sides, feed_down = after((sides, feed_down))
        sides, pair_parts, feed_pair = after((sides, pair_parts, feed_pair))
    down_parts = [delivered(feed_down, k) for k in range(2)]
    attention_block = jnp.concatenate([side[0] for side in sides], axis=1).astype(bf16)
    attention_block = attention_block.reshape(parts, weight_rows, -1)

    def block_for(steps):
        return lax.dynamic_index_in_dim(
            attention_block, (rank + steps) % parts, 0, keepdims=False
        )

    sums = block_for(0).astype(f32)
    for d in range(1, parts):
        sums = sums + around(block_for(d), d).astype(f32)

    pair_sum = pair_parts[0].astype(f32) + pair_parts[1].astype(f32)
    down_sum = down_parts[0].astype(f32) + down_parts[1].astype(f32)

    total = middle + partials[0] + out_near.astype(f32) + jnp.stack(out_beside).astype(f32)

    edge = 2 * QW + 2 * KW
    return (
        total.astype(bf16)[None, :, None],
        input_grad[None, :, None],
        sums[:, edge],
        sums[:, QW : 2 * QW],
        sums[:, edge + 2],
        sums[:, 2 * QW : 2 * QW + KW],
        sums[:bias_rows, edge + 3],
        sums[:, 2 * QW + KW : edge],
        sums[:bias_rows, edge + 4],
        sums[:, :QW],
        sums[:, edge + 1],
        pair_sum[:, :hidden],
        pair_sum[:, hidden_pad : hidden_pad + hidden],
        down_sum[:, :hidden].T,
    )


def solution(mesh):
    groups, parts = mesh.devices.shape
    split = jax.sharding.Mesh(
        mesh.devices.reshape(groups // 2, 2, parts // 2, 2), ("grp", "core", "zh", "zb")
    )
    dp = ("grp", "core")
    ctx = ("zh", "zb")
    rows = P(dp + ctx, None)
    line = P(dp + ctx)
    tokens = P(dp, None, None, ctx, None)
    up = P(dp, ctx)
    return jax.shard_map(
        body,
        mesh=split,
        in_specs=(
            tokens, P(dp, None, None, None), tokens, line, rows, line, rows, line, rows, line,
            rows, line, up, up, P(ctx, dp),
        ),
        out_specs=(
            tokens, tokens, line, rows, line, rows, line, rows, line, rows, line,
            up, up, P(ctx, dp),
        ),
        check_vma=False,
    )
```

```python
import functools
import jax, jax.numpy as jnp
from jax import lax
from jax.sharding import PartitionSpec as P
from jax.experimental import pallas as pl
from jax.experimental.pallas import tpu as pltpu
D=896; HEADS=14; KV_HEADS=2; HEAD=64; LANES=128
QW=896; KW=128
epsilon=1e-6
bf16=jnp.bfloat16; f32=jnp.float32
LIMIT=56*1024*1024
COST=pl.CostEstimate(flops=1, bytes_accessed=1, transcendentals=0)

def dot(left, right, left_dim, right_dim):
    return lax.dot_general(left, right, (((left_dim,), (right_dim,)), ((), ())), preferred_element_type=f32)

def half_turn(v, back):
    lane = lax.broadcasted_iota(jnp.int32, v.shape, 1) & (HEAD-1)
    width=v.shape[1]
    up = pltpu.roll(v, width-HEAD//2, 1)
    down = pltpu.roll(v, HEAD//2, 1)
    return jnp.where(lane < HEAD//2, up, down)

def scaled(v):
    return lax.rsqrt(jnp.mean(v*v, axis=-1, keepdims=True)+epsilon)

def pairs_kernel(x_ref, wkv_ref, ws_ref, spread_ref, cos_ref, sin_ref, kv_ref, n1_ref, rows_ref, bias_ref):
    @pl.when(pl.program_id(0)==0)
    def _():
        table = ws_ref[...].astype(f32).T[:8]
        rows_ref[...] = table
        close = dot(table.astype(bf16), spread_ref[...],1,0)
        bias_ref[:, :KW] = close[3:4]
        bias_ref[:, KW:] = close[4:5]
    x = x_ref[...].astype(f32)
    n1 = (x*scaled(x)*rows_ref[0:1]).astype(bf16)
    n1_ref[...] = n1
    kv = dot(n1, wkv_ref[...],1,0) + bias_ref[...]
    v = kv[:, :KW]
    kv_ref[:, :KW] = (v*cos_ref[...] + half_turn(v,False)*sin_ref[...]).astype(bf16)
    kv_ref[:, KW:] = kv[:, KW:].astype(bf16)

def queries_kernel(n1_ref, wq_ref, rows_ref, cos_ref, sin_ref, rq_ref):
    q = dot(n1_ref[...], wq_ref[:, 2*KW:],1,0) + rows_ref[2:3]
    cos = cos_ref[...]; sin = sin_ref[...]
    for b in range(QW//LANES):
        v = q[:, b*LANES:(b+1)*LANES]
        r = (v*cos + half_turn(v,False)*sin).astype(bf16)
        rq_ref[:, b*LANES:(b+1)*LANES] = (r.astype(f32)*HEAD**-0.5).astype(bf16)

def project(x, out_set, in_set, spread, cos, sin):
    m, rows, _ = x.shape
    full=lambda shape,idx: pl.BlockSpec(shape, lambda i: idx)
    blk=lambda w: pl.BlockSpec((None,rows,w), lambda i:(i,0,0))
    sd=jax.ShapeDtypeStruct
    params=dict(compiler_params=pltpu.CompilerParams(vmem_limit_bytes=LIMIT), cost_estimate=COST)
    pair, n1, table = pl.pallas_call(
        pairs_kernel, grid=(m,),
        in_specs=[blk(D), full((D,2*KW),(0,0)), full((D,LANES),(0,QW//LANES)), full((D,LANES),(0,0)), blk(LANES), blk(LANES)],
        out_specs=[blk(2*KW), blk(D), full((8,D),(0,0))],
        out_shape=[sd((m,rows,2*KW),bf16), sd((m,rows,D),bf16), sd((8,D),f32)],
        scratch_shapes=[pltpu.VMEM((1,2*KW),f32)],
        name="pairs", **params,
    )(x, in_set, out_set, spread, cos, sin)
    rq = pl.pallas_call(
        queries_kernel, grid=(m,),
        in_specs=[blk(D), full((D,2*KW+QW),(0,0)), full((8,D),(0,0)), blk(LANES), blk(LANES)],
        out_specs=blk(QW), out_shape=sd((m,rows,QW),bf16),
        name="queries", **params,
    )(n1, in_set, table, cos, sin)
    return rq, pair, n1, table

BLOCK=128
def units():
    group=HEADS//KV_HEADS
    out=[]
    for g in range(KV_HEADS):
        for parity in range(2):
            blocks=[h//2 for h in range(g*group,(g+1)*group) if h%2==parity]
            out.append((g,parity,blocks))
    return out

def padded(v, g, parity, lane):
    if g != parity:
        v = pltpu.roll(v.astype(f32), HEAD, 1).astype(bf16)
    keep = (lane >= HEAD) if parity else (lane < HEAD)
    return jnp.where(keep, v, jnp.zeros_like(v))

def mask_bias(begins, rank_base, q0, window, reach):
    key = lax.broadcasted_iota(jnp.int32,(window,BLOCK),0) + (rank_base + q0 - reach)
    query = lax.broadcasted_iota(jnp.int32,(window,BLOCK),1) + (rank_base + q0)
    ok = (key >= begins) & (key <= query)
    return jnp.where(ok, 0.0, -1e30).astype(f32)

def fill_padded(kv_refs, k_ref, v_ref):
    rows = kv_refs[0].shape[0]
    lane = lax.broadcasted_iota(jnp.int32,(rows,LANES),1)
    for p,ref in enumerate(kv_refs):
        kv=ref[...]
        for g,parity,_ in units():
            u=2*g+parity
            k_ref[u, p*rows:(p+1)*rows] = padded(kv[:, :KW], g, parity, lane)
            v_ref[u, p*rows:(p+1)*rows] = padded(kv[:, KW:], g, parity, lane)

def attend_kernel(base_ref, rq_ref, kv0_ref, kv1_ref, kv2_ref, begin_ref, wo_ref, x_ref, rows_ref, *refs):
    n2_ref, mixed_ref, middle_ref, lse_ref, k_ref, v_ref = refs[-6:]
    qb = pl.program_id(0)
    rows = kv0_ref.shape[0]
    reach=512; window=reach+BLOCK
    @pl.when(qb==0)
    def _():
        fill_padded((kv2_ref,kv1_ref,kv0_ref), k_ref, v_ref)
    q0 = qb*BLOCK
    bias = mask_bias(begin_ref[...], base_ref[0], q0, window, reach)
    parts=[None]*7
    start = pl.multiple_of(q0 + (2*rows - reach), BLOCK)
    for g,parity,blocks in units():
        u=2*g+parity
        qs = jnp.concatenate([rq_ref[:, b*LANES:(b+1)*LANES] for b in blocks], axis=0)
        keys = k_ref[u, pl.ds(start,window)]
        vals = v_ref[u, pl.ds(start,window)]
        s = dot(keys, qs, 1, 1) + jnp.concatenate([bias]*len(blocks),axis=1)
        top = jnp.max(s, axis=0, keepdims=True)
        e = jnp.exp(s-top)
        total = jnp.sum(e, axis=0, keepdims=True)
        p = (e*(1.0/total)).astype(bf16)
        o = dot(vals, p, 0, 0)
        lse = top+jnp.log(total)
        for i,b in enumerate(blocks):
            piece=o[:, i*BLOCK:(i+1)*BLOCK]
            parts[b] = piece if parts[b] is None else parts[b]+piece
            lse_ref[0, 2*b+parity:2*b+parity+1, :] = lse[:, i*BLOCK:(i+1)*BLOCK]
    for b in range(7):
        mixed_ref[:, b*LANES:(b+1)*LANES] = parts[b].T.astype(bf16)
    middle = x_ref[...].astype(f32) + dot(mixed_ref[...], wo_ref[...],1,0)
    middle_ref[...] = middle
    n2_ref[...] = (middle*scaled(middle)*rows_ref[1:2]).astype(bf16)

def attend(m, base, rq, kvs, begins, out_set, x, rows_table, before):
    micros, rows, _ = rq.shape; nq=rows//BLOCK
    full=lambda shape: pl.BlockSpec(shape, lambda i: (0,)*len(shape))
    blk=lambda w: pl.BlockSpec((None,BLOCK,w), lambda i:(m,i,0))
    sd=jax.ShapeDtypeStruct
    return pl.pallas_call(
        attend_kernel, grid=(nq,),
        in_specs=[pl.BlockSpec(memory_space=pltpu.SMEM), blk(QW)]+[pl.BlockSpec((None,rows,2*KW),lambda i:(m,0,0))]*3+[pl.BlockSpec((None,1,BLOCK),lambda i:(m,0,i)), full((D,QW)), blk(D), full((8,D))]+[pl.BlockSpec(memory_space=pl.ANY)]*len(before),
        out_specs=[pl.BlockSpec((BLOCK,D),lambda i:(i,0)), blk(QW), blk(D), pl.BlockSpec((None,1,16,BLOCK),lambda i:(m,i,0,0))],
        out_shape=[sd((rows,D),bf16), sd((micros,rows,QW),bf16), sd((micros,rows,D),f32), sd((micros,nq,16,BLOCK),f32)],
        scratch_shapes=[pltpu.VMEM((4,3*rows,LANES),bf16), pltpu.VMEM((4,3*rows,LANES),bf16)],
        input_output_aliases={9+k:1+k for k in range(len(before))},
        compiler_params=pltpu.CompilerParams(vmem_limit_bytes=LIMIT), cost_estimate=COST,
        name="attend",
    )(base, rq, *kvs, begins, out_set, x, rows_table, *before)

def attend_back_kernel(base_ref, rq_ref, kv0_ref, kv1_ref, kv2_ref, begin_ref, wo_ref, rows_ref, lse_ref, middle_ref, dy_ref, cos_ref, sin_ref, *refs, count):
    gs=refs[:count]
    far1_ref, far2_ref, dmid_ref, dmb_ref, dq_ref, own_ref, gain_ref, k_ref, v_ref, dk_ref, dv_ref = refs[-11:]
    qb = pl.program_id(0); nq=pl.num_programs(0)
    rows = kv0_ref.shape[0]
    reach=512; window=reach+BLOCK
    @pl.when(qb==0)
    def _():
        fill_padded((kv2_ref,kv1_ref,kv0_ref), k_ref, v_ref)
        dk_ref[...] = jnp.zeros_like(dk_ref)
        dv_ref[...] = jnp.zeros_like(dv_ref)
        gain_ref[...] = jnp.zeros_like(gain_ref)
    dn2 = gs[0][...].astype(f32)
    for g_ref in gs[1:]:
        dn2 = dn2+g_ref[...].astype(f32)
    middle = middle_ref[...]
    inv = scaled(middle)
    gain_ref[...] += jnp.broadcast_to(jnp.sum(dn2*(middle*inv),axis=0,keepdims=True), gain_ref.shape)
    w2 = dn2*rows_ref[1:2]
    dmid = dy_ref[...].astype(f32) + inv*w2 - middle*(inv*inv*inv)*jnp.mean(w2*middle,axis=-1,keepdims=True)
    dmid_ref[...] = dmid
    dmb = dmid.astype(bf16)
    dmb_ref[...] = dmb
    dmixed = dot(dmb, wo_ref[...],1,1).astype(bf16)
    q0 = qb*BLOCK
    bias = mask_bias(begin_ref[...], base_ref[0], q0, window, reach)
    start = pl.multiple_of(q0 + (2*rows - reach), BLOCK)
    parts=[None]*7
    for g,parity,blocks in units():
        u=2*g+parity
        n=len(blocks)
        qs = jnp.concatenate([rq_ref[:, b*LANES:(b+1)*LANES] for b in blocks], axis=0)
        ds_ = jnp.concatenate([dmixed[:, b*LANES:(b+1)*LANES] for b in blocks], axis=0)
        keys = k_ref[u, pl.ds(start,window)]
        vals = v_ref[u, pl.ds(start,window)]
        lse = jnp.concatenate([lse_ref[0, 2*b+parity:2*b+parity+1, :] for b in blocks],axis=1)
        p = jnp.exp(dot(keys,qs,1,1) + jnp.concatenate([bias]*n,axis=1) - lse)
        dp = dot(vals, ds_, 1, 1)
        t = p*dp
        ds = (t-p*jnp.sum(t,axis=0,keepdims=True)).astype(bf16)
        pb = p.astype(bf16)
        o = dot(keys, ds, 0, 0)
        for i,b in enumerate(blocks):
            piece=o[:, i*BLOCK:(i+1)*BLOCK]
            parts[b] = piece if parts[b] is None else parts[b]+piece
        dk = dot(ds, qs, 1, 0); dv = dot(pb, ds_, 1, 0)
        keep = lax.broadcasted_iota(jnp.int32,(window,LANES),1)
        keep = (keep>=HEAD) if parity else (keep<HEAD)
        dk = jnp.where(keep, dk, 0.0); dv=jnp.where(keep,dv,0.0)
        if g!=parity:
            dk = pltpu.roll(dk,HEAD,1); dv=pltpu.roll(dv,HEAD,1)
        dk_ref[pl.ds(start,window)] += dk
        dv_ref[pl.ds(start,window)] += dv
    cos=cos_ref[...]; sin=sin_ref[...]
    for b in range(7):
        gq = parts[b].T*HEAD**-0.5
        dq_ref[:, b*LANES:(b+1)*LANES] = (gq*cos + half_turn(gq*sin,True)).astype(bf16)
    @pl.when(qb==nq-1)
    def _():
        own_ref[:, :KW] = dk_ref[2*rows:]; own_ref[:, KW:] = dv_ref[2*rows:]
        far1_ref[:, :KW] = dk_ref[rows:2*rows].astype(bf16); far1_ref[:, KW:] = dv_ref[rows:2*rows].astype(bf16)
        far2_ref[:, :KW] = dk_ref[:rows].astype(bf16); far2_ref[:, KW:] = dv_ref[:rows].astype(bf16)

def attend_back(m, base, rq, kvs, begins, out_set, rows_table, lse, middle, dy, gs, cos, sin, before):
    micros, rows, _ = rq.shape; nq=rows//BLOCK
    full=lambda shape: pl.BlockSpec(shape, lambda i: (0,)*len(shape))
    blk=lambda w: pl.BlockSpec((None,BLOCK,w), lambda i:(m,i,0))
    one=lambda h,w: pl.BlockSpec((None,h,w), lambda i:(m,0,0))
    sd=jax.ShapeDtypeStruct
    at=12+len(gs)
    return pl.pallas_call(
        functools.partial(attend_back_kernel,count=len(gs)), grid=(nq,),
        in_specs=[pl.BlockSpec(memory_space=pltpu.SMEM), blk(QW)]+[pl.BlockSpec((None,rows,2*KW),lambda i:(m,0,0))]*3+[pl.BlockSpec((None,1,BLOCK),lambda i:(m,0,i)), full((D,QW)), full((8,D)),
            pl.BlockSpec((None,1,16,BLOCK),lambda i:(m,i,0,0)), blk(D), blk(D)]+[blk(LANES)]*2+[pl.BlockSpec((BLOCK,D),lambda i:(i,0))]*len(gs)+[pl.BlockSpec(memory_space=pl.ANY)]*len(before),
        out_specs=[full((rows,2*KW)), full((rows,2*KW)), blk(D), blk(D), blk(QW), one(rows,2*KW), one(8,D)],
        out_shape=[sd((rows,2*KW),bf16), sd((rows,2*KW),bf16), sd((micros,rows,D),f32), sd((micros,rows,D),bf16), sd((micros,rows,QW),bf16), sd((micros,rows,2*KW),f32), sd((micros,8,D),f32)],
        scratch_shapes=[pltpu.VMEM((4,3*rows,LANES),bf16)]*2+[pltpu.VMEM((3*rows,LANES),f32)]*2,
        input_output_aliases={at+1+k:2+k for k in range(len(before))},
        compiler_params=pltpu.CompilerParams(vmem_limit_bytes=LIMIT), cost_estimate=COST,
        name="attend_back",
    )(base, rq, *kvs, begins, out_set, rows_table, lse, middle, dy, cos, sin, *gs, *before)

CHUNK=256

def feed_kernel(own_ref, *refs, parts, micro, kept):
    ts=refs[:parts]; gs=refs[parts:2*parts]; sets=refs[2*parts:2*parts+2]
    refs=refs[2*parts+2+kept:]
    backs=refs[:parts]; outs=refs[parts:2*parts]
    left_ref,pair_ref,act_ref,x_ref,y_ref,w_ref,own_buf,far_buf,w_sem,in_sem,out_sem=refs[2*parts:]
    i=pl.program_id(0)
    width=w_ref.shape[1]//3
    chunks=width//CHUNK
    def tokens(k):
        return (pltpu.make_async_copy(ts[k],x_ref.at[k],in_sem.at[0,k]),
                pltpu.make_async_copy(gs[k],y_ref.at[k],in_sem.at[1,k]))
    def columns(which,j,p):
        c=slice(p*width+j*CHUNK,p*width+(j+1)*CHUNK)
        return pltpu.make_async_copy(sets[which].at[:,c],w_ref.at[:,c],w_sem.at[p,j])
    def results(k):
        if k==0:
            return (pltpu.make_async_copy(own_buf.at[0],outs[0].at[micro],out_sem.at[0,0]),
                    pltpu.make_async_copy(own_buf.at[1],backs[0],out_sem.at[1,0]))
        return (pltpu.make_async_copy(far_buf.at[0,k-1],outs[k].at[micro],out_sem.at[0,k]),
                pltpu.make_async_copy(far_buf.at[1,k-1],backs[k],out_sem.at[1,k]))
    @pl.when(i==0)
    def _():
        for copy in tokens(0): copy.start()
        for which in range(2):
            @pl.when(own_ref[0]==1-which)
            def _(which=which):
                for j in range(chunks):
                    for p in range(3): columns(which,j,p).start()
        for k in range(1,parts):
            for copy in tokens(k): copy.start()
    for k in range(parts):
        @pl.when(i==k)
        def _(k=k):
            for copy in tokens(k): copy.wait()
    @pl.when(i==0)
    def _():
        for j in range(chunks):
            for p in range(3): columns(0,j,p).wait()
    x=x_ref[i]; y=y_ref[i]
    left_ref[0]=x; left_ref[1]=y
    for j in range(chunks):
        c=slice(j*CHUNK,(j+1)*CHUNK); c2=slice(width+j*CHUNK,width+(j+1)*CHUNK); c3=slice(2*width+j*CHUNK,2*width+(j+1)*CHUNK)
        g=dot(x,w_ref[:,c],1,0); u=dot(x,w_ref[:,c2],1,0); da=dot(y,w_ref[:,c3],1,0)
        s=jax.nn.sigmoid(g)
        gs_=g*s
        act_ref[:,c]=(gs_*u).astype(bf16)
        pair_ref[:,c]=(da*u*s*(1.0+g*(1.0-s))).astype(bf16)
        pair_ref[:,c2]=(da*gs_).astype(bf16)
    out=dot(act_ref[...],w_ref[:,2*width:],1,1)
    res=dot(pair_ref[...],w_ref[:,:2*width],1,1)
    for k in range(parts):
        @pl.when(i==k)
        def _(k=k):
            if k==0:
                own_buf[0]=out; own_buf[1]=res
            else:
                far_buf[0,k-1]=out.astype(bf16); far_buf[1,k-1]=res.astype(bf16)
            for copy in results(k): copy.start()
    @pl.when(i==parts-1)
    def _():
        for k in range(parts):
            for copy in results(k): copy.wait()

def feed(own, toks, grads, sets, micro, micros, before):
    parts=len(toks); rows=toks[0].shape[0]; hidden_pad=sets[0].shape[1]//3
    blk=lambda w: pl.BlockSpec((rows,w), lambda i:(micro*parts+i,0))
    sd=jax.ShapeDtypeStruct
    everything=rows*parts*micros
    kept=len(before)
    hold=pl.BlockSpec(memory_space=pl.ANY)
    shapes=[sd((rows,D),f32)]+[sd((rows,D),bf16)]*(parts-1)+[sd((micros,rows,D),f32)]+[sd((micros,rows,D),bf16)]*(parts-1)
    n_in=1+2*parts+2
    dma=pltpu.SemaphoreType.DMA
    out=pl.pallas_call(
        functools.partial(feed_kernel,parts=parts,micro=micro,kept=kept), grid=(parts,),
        in_specs=[pl.BlockSpec(memory_space=pltpu.SMEM)]+[hold]*(2*parts+2+kept),
        out_specs=[hold]*(2*parts)+[pl.BlockSpec((2,rows,D), lambda i:(0,micro*parts+i,0)),blk(2*hidden_pad),blk(hidden_pad)],
        out_shape=shapes+[sd((2,everything,D),bf16)]+[sd((everything,w),bf16) for w in (2*hidden_pad,hidden_pad)],
        scratch_shapes=[pltpu.VMEM((parts,rows,D),bf16)]*2+[pltpu.VMEM(sets[0].shape,bf16),pltpu.VMEM((2,rows,D),f32),pltpu.VMEM((2,parts-1,rows,D),bf16),
            dma((3,hidden_pad//CHUNK)),dma((2,parts)),dma((2,parts))],
        input_output_aliases={n_in+k:parts+k for k in range(kept)},
        compiler_params=pltpu.CompilerParams(vmem_limit_bytes=LIMIT), cost_estimate=COST,
        name="feed",
    )(own,*toks,*grads,*sets,*before)
    return out[:parts], out[parts:]

def finish_kernel(bit_ref, dq_ref, own_ref, cos_ref, sin_ref, wq_ref, wkv_ref, rows_ref, x_ref, n1_ref, dmid_ref, mixed_ref, dmb_ref, spread_ref, gain2_ref, *refs, near, block):
    far=refs[:-6]
    ig_ref, keep_ref, send_ref, acc_ref, small_ref, sum_ref = refs[-6:]
    i=pl.program_id(0)
    @pl.when(i==0)
    def _():
        acc_ref[...]=jnp.zeros_like(acc_ref)
        small_ref[...]=jnp.zeros_like(small_ref)
    for m in range(len(far)//near):
        @pl.when(i==m)
        def _(m=m):
            own=own_ref[...]
            for ref in far[m*near:(m+1)*near]:
                own=own+ref[...].astype(f32)
            sum_ref[...]=own
    own=sum_ref[...]
    k=own[:, :KW]
    cos=cos_ref[...]; sin=sin_ref[...]
    dk=(k*cos+half_turn(k*sin,True)).astype(bf16)
    dv=own[:, KW:].astype(bf16)
    dkv=jnp.concatenate([dk,dv],axis=1)
    dq=dq_ref[...]
    dn1=dot(dq,wq_ref[:, 2*KW:],1,1)+dot(dkv,wkv_ref[...],1,1)
    x=x_ref[...].astype(f32); inv=scaled(x)
    small_ref[0:1]+=jnp.sum(dn1*(x*inv),axis=0,keepdims=True)
    small_ref[1:2]+=gain2_ref[0:1]
    small_ref[2:3]+=jnp.sum(dq.astype(f32),axis=0,keepdims=True)
    small_ref[3:4,:2*KW]+=jnp.sum(dkv.astype(f32),axis=0,keepdims=True)
    w1=dn1*rows_ref[0:1]
    ig_ref[...]=dmid_ref[...]+inv*w1-x*(inv*inv*inv)*jnp.mean(w1*x,axis=-1,keepdims=True)
    n1=n1_ref[...]
    acc_ref[:, :QW]+=dot(mixed_ref[...],dmb_ref[...],0,0)
    acc_ref[:, QW:2*QW]+=dot(n1,dq,0,0)
    acc_ref[:, 2*QW:2*QW+2*KW]+=dot(n1,dkv,0,0)
    @pl.when(i==pl.num_programs(0)-1)
    def _():
        pair=jnp.concatenate([small_ref[3:4,:KW],small_ref[3:4,KW:2*KW],jnp.zeros((6,KW),f32)],axis=0).astype(bf16)
        table=jnp.concatenate([small_ref[0:3],dot(pair,spread_ref[...],1,1)[0:2],jnp.zeros((LANES-5,D),f32)],axis=0)
        acc_ref[:, 2*QW+2*KW:]=table.T
        if block:
            for j in range(D//block//2):
                at=pl.multiple_of((2*j+bit_ref[0])*block,16)
                keep_ref[j*block:(j+1)*block]=acc_ref[pl.ds(at,block)].astype(bf16)
                at=pl.multiple_of((2*j+1-bit_ref[0])*block,16)
                send_ref[j*block:(j+1)*block]=acc_ref[pl.ds(at,block)].astype(bf16)
        else:
            keep_ref[...]=acc_ref[:D//2].astype(bf16)
            send_ref[...]=acc_ref[D//2:].astype(bf16)

def finish(bit,dq,own,far,cos,sin,in_set,rows_table,x,n1,dmid,mixed,dmb,spread,gain2,block):
    m,rows,_=x.shape
    full=lambda shape,idx=(0,0): pl.BlockSpec(shape, lambda i: idx)
    blk=lambda w,h=rows: pl.BlockSpec((None,h,w), lambda i:(i,0,0))
    sd=jax.ShapeDtypeStruct
    width=2*QW+2*KW+LANES
    near=len(far[0])
    far=[f for pieces in far for f in pieces]
    return pl.pallas_call(
        functools.partial(finish_kernel,near=near,block=block), grid=(m,),
        in_specs=[pl.BlockSpec(memory_space=pltpu.SMEM),blk(QW),blk(2*KW),blk(LANES),blk(LANES),full((D,2*KW+QW)),full((D,2*KW)),full((8,D)),blk(D),blk(D),blk(D),blk(QW),blk(D),full((D,LANES)),blk(D,8)]+[full((rows,2*KW))]*len(far),
        out_specs=[blk(D),full((D//2,width)),full((D//2,width))],
        out_shape=[sd((m,rows,D),f32),sd((D//2,width),bf16),sd((D//2,width),bf16)],
        scratch_shapes=[pltpu.VMEM((D,width),f32),pltpu.VMEM((8,D),f32),pltpu.VMEM((rows,2*KW),f32)],
        compiler_params=pltpu.CompilerParams(vmem_limit_bytes=LIMIT), cost_estimate=COST,
        name="finish",
    )(bit,dq,own,cos,sin,in_set,in_set,rows_table,x,n1,dmid,mixed,dmb,spread,gain2,*far)

def weights_kernel(left_ref, right_ref, out_ref, turned_ref):
    @pl.when(pl.program_id(0)==0)
    def _(): turned_ref[...]=left_ref[...].T
    out_ref[...]=dot(turned_ref[...],right_ref[...],1,0).astype(bf16)

def weights(left,which,right,chunk):
    rows=left.shape[1]; width=right.shape[1]
    return pl.pallas_call(
        weights_kernel, grid=(width//chunk,),
        in_specs=[pl.BlockSpec((None,rows,D),lambda j:(which,0,0),pipeline_mode=pl.Buffered(1)),pl.BlockSpec((rows,chunk),lambda j:(0,j))],
        out_specs=pl.BlockSpec((D,chunk),lambda j:(0,j)), out_shape=jax.ShapeDtypeStruct((D,width),bf16),
        scratch_shapes=[pltpu.VMEM((D,rows),bf16)],
        compiler_params=pltpu.CompilerParams(vmem_limit_bytes=LIMIT), cost_estimate=COST,
        name="weights",
    )(left,right)

def woven_kernel(core_ref, *refs):
    n=len(refs)//3
    mine=refs[:n]; got=refs[n:2*n]; outs=refs[2*n:]
    core=core_ref[0]; j=pl.program_id(0)
    for k in range(n):
        rows=mine[k].shape[0]
        outs[k][pl.ds(pl.multiple_of(core*rows,16),rows)]=mine[k][...]
        outs[k][pl.ds(pl.multiple_of((1-core)*rows,16),rows)]=got[k][...]

def woven(core, mine, got):
    n=len(mine); blocks,rows,_=mine[0].shape
    size=blocks.bit_length()-1
    def turned(j):
        return sum(((j>>k)&1)<<(size-1-k) for k in range(size))
    places=[lambda j:(j,0,0), lambda j:(turned(j),0,0)]
    shapes=[jax.ShapeDtypeStruct((2*blocks*rows,v.shape[2]),v.dtype) for v in mine]
    return pl.pallas_call(
        woven_kernel, grid=(blocks,), in_specs=[pl.BlockSpec(memory_space=pltpu.SMEM)]+[pl.BlockSpec((None,)+v.shape[1:],places[k%n]) for k,v in enumerate(mine+got)],
        out_specs=[pl.BlockSpec((2*rows,v.shape[2]),lambda j:(j,0)) for v in mine], out_shape=shapes,
        compiler_params=pltpu.CompilerParams(vmem_limit_bytes=LIMIT), cost_estimate=COST,
        name="woven",
    )(core,*mine,*got)


LONGEST = 512


def after(values_in, *needed):
    return lax.optimization_barrier((values_in, needed))[0]


theta = 10000.0


def body(
    layer_in,
    doc_ids,
    cotangent,
    first_gain,
    query_weight,
    query_bias,
    key_weight,
    key_bias,
    value_weight,
    value_bias,
    out_weight,
    second_gain,
    gate_weight,
    up_weight,
    down_weight,
):
    ctx = ("zh", "zb")
    dp = ("grp", "core")
    parts = lax.axis_size(ctx)
    rank = lax.axis_index(ctx)
    micros = layer_in.shape[1]
    shard_rows = layer_in.shape[3]
    hidden = gate_weight.shape[1]
    hidden_pad = -(-hidden // (2 * LANES)) * 2 * LANES
    weight_rows = query_weight.shape[0]
    bias_rows = key_bias.shape[0]
    reach_parts = -(-LONGEST // shard_rows)
    core = lax.axis_index("core")
    far_half = lax.axis_index("zh")

    group_rank = lax.axis_index(dp)
    groups = lax.axis_size(dp)
    bits = [1 << k for k in range(groups.bit_length() - 1)]
    block_rows = parts * weight_rows
    even = block_rows % 16 == 0

    def swapped(values_in, bit):
        return lax.ppermute(values_in, dp, [(s, s ^ bit) for s in range(groups)])

    def doubled(blocks, order, k):
        bit = order[k]
        got = swapped(blocks, bit)
        low = (group_rank // bit) % 2 == 0
        return jnp.stack([jnp.where(low, blocks, got), jnp.where(low, got, blocks)])

    def around(values_in, steps):
        return lax.ppermute(values_in, ctx, [(s, (s + steps) % parts) for s in range(parts)])

    def other(values_in, axis):
        return lax.ppermute(values_in, axis, [(0, 1), (1, 0)])

    def corner(values_in):
        return lax.ppermute(values_in, ("core", "zb"), [(s, 3 - s) for s in range(4)])

    def shared(values_in):
        beside = other(values_in, "zb")
        return [values_in, other(values_in, "core"), beside, other(beside, "core")]

    def collected(values_in):
        pieces = [values_in] + [around(values_in, d) for d in range(1, parts)]
        ordered = [pieces[d] for d in range(parts - 1, -1, -1)]
        ordered = jnp.stack(ordered + ordered[:-1])
        taken = lax.dynamic_slice_in_dim(ordered, parts - 1 - rank, parts, 0)
        return taken.reshape((-1,) + values_in.shape[1:])

    def column(values_in):
        return jnp.pad(values_in, (0, weight_rows - values_in.shape[0]))[:, None]

    def wide(values_in):
        return jnp.pad(values_in, ((0, 0), (0, hidden_pad - hidden)))

    own_block = jnp.concatenate([wide(gate_weight), wide(up_weight), wide(down_weight.T)], axis=1)
    own_set = lax.all_gather(own_block, dp, axis=0, tiled=True)
    small = jnp.concatenate(
        [column(v) for v in (first_gain, second_gain, query_bias, key_bias, value_bias)], axis=1
    )
    small = jnp.pad(small, ((0, 0), (0, LANES - small.shape[1])))
    own_attention = jnp.concatenate(
        [out_weight, small, key_weight, value_weight, query_weight], axis=1
    )
    first_block = collected(own_attention)
    row = jnp.arange(D, dtype=jnp.int32)[:, None]
    place = row // weight_rows * bias_rows + row % weight_rows
    spread = (
        (place == jnp.arange(LANES, dtype=jnp.int32)[None, :]) & (row % weight_rows < bias_rows)
    ).astype(bf16)

    docs = doc_ids[0, :, 0]
    own_docs = lax.dynamic_slice_in_dim(docs, rank * shard_rows, shard_rows, 1)
    begins = jnp.sum((docs[:, None, :] < own_docs[:, :, None]).astype(jnp.int32), axis=2)
    row_index = rank * shard_rows + jnp.arange(shard_rows, dtype=jnp.int32)
    positions = row_index[None, :] - begins
    frequency = jnp.power(f32(theta), -(jnp.arange(HEAD // 2, dtype=f32) * (2.0 / HEAD)))
    angle = positions.astype(f32)[:, :, None] * frequency
    cosines, sines = jnp.cos(angle), jnp.sin(angle)
    cosines = jnp.concatenate([cosines] * (2 * LANES // HEAD), axis=2)
    sines = jnp.concatenate([-sines, sines] * (LANES // HEAD), axis=2)
    base = (rank * shard_rows).reshape(1)

    own_block, first_block = after((own_block, first_block))
    cut = QW + LANES
    firsts = [first_block[:, :cut], first_block[:, cut:]]
    gather_orders = [bits[1:] + bits[:1], bits[:0:-1] + bits[:1]]
    widths = own_block.shape[1] // LANES // 4 * LANES
    edges = [0, widths, own_block.shape[1] - widths, own_block.shape[1]]
    other_block = []
    upstream = [cotangent[0, m, 0] for m in range(micros)]
    crossed = []
    for k in range(len(bits)):
        if k < len(bits) - 1 or not even:
            firsts = [doubled(side, order, k) for side, order in zip(firsts, gather_orders)]
        else:
            gots = [swapped(side, 1) for side in firsts]
            firsts = [firsts, gots]
        if k < 3:
            other_block.append(other(own_block[:, edges[k] : edges[k + 1]], "zh"))
        firsts, other_block, own_block, spread, cosines, sines, begins, upstream, crossed = after(
            (firsts, other_block, own_block, spread, cosines, sines, begins, upstream, crossed)
        )
    other_set = lax.all_gather(jnp.concatenate(other_block, axis=1), dp, axis=0, tiled=True)
    if even:
        firsts, gots = ([v.reshape((-1,) + v.shape[-2:]) for v in part] for part in firsts)
        out_set, in_set = woven(core.reshape(1), firsts, gots)
    else:
        out_set, in_set = (
            jnp.transpose(
                side, [list(reversed(order)).index(bit) for bit in reversed(bits)] + [-2, -1]
            ).reshape(-1, side.shape[-1])
            for side, order in zip(firsts, gather_orders)
        )
    sets = (own_set, other_set)
    own_quarter = (core == far_half).astype(jnp.int32).reshape(1)

    tokens = layer_in[0, :, 0]
    rot_query, pairs, normed_one, rows_table = project(
        tokens, out_set, in_set, spread, cosines, sines
    )
    kvs = [pairs] + [
        lax.ppermute(pairs, ctx, [(s, s + d) for s in range(parts - d)])
        for d in range(1, reach_parts + 1)
    ]

    kvs, rot_query, upstream = after((kvs, rot_query, upstream))
    crossed.append(other(upstream[0], "zb"))

    begins = begins[:, None, :]
    exchanged = []
    held = ()
    for m in range(micros):
        normed_two, *held = attend(
            m, base, rot_query, kvs, begins, out_set, tokens, rows_table, held
        )
        if m == 0:
            upstream, crossed, normed_two = after((upstream, crossed, normed_two))
        exchanged.append([normed_two, other(normed_two, "core"), other(normed_two, "zb")])
        if m == 0:
            crossed += [other(u, "zb") for u in upstream[1:]]
            upstream_pieces = [[u, other(u, "core"), v] for u, v in zip(upstream, crossed)]
    exchanged[-1].append(corner(normed_two))
    exchanged[:-1], upstream_pieces[0], exchanged[-1][0] = after(
        (exchanged[:-1], upstream_pieces[0], normed_two)
    )
    for early in exchanged[:-1] + upstream_pieces[:1]:
        early.append(other(early[2], "core"))
    mixed, middle, log_sums = held

    backs = []
    before = ()
    for m in range(micros):
        back, before = feed(
            own_quarter, exchanged[m], upstream_pieces[m], sets, m, micros, before
        )
        if m < micros - 1:
            back, upstream_pieces[m + 1] = after((back, upstream_pieces[m + 1]))
            upstream_pieces[m + 1].append(other(upstream_pieces[m + 1][2], "core"))
        backs.append([back[0], other(back[1], "core"), other(back[2], "zb"), corner(back[3])])
    partials = before[:4]
    out_near = other(partials[1], "core")
    out_far = other(partials[3], "core")

    left, pair, act = after(before[4:], backs[0])
    feed_down = weights(left, 1, act, 256)
    backs[-1][1:3], left, pair, feed_down = after((backs[-1][1:3], left, pair, feed_down))
    feed_pair = weights(left, 0, pair, 512)
    backs, feed_pair, out_near, out_far = after((backs, feed_pair, out_near, out_far))
    feed_down = lax.psum_scatter(feed_down, "grp", scatter_dimension=0, tiled=True)
    feed_pair = lax.psum_scatter(feed_pair, "grp", scatter_dimension=0, tiled=True)

    far = []
    ended = ()
    out_beside = []
    for m in range(micros):
        out_sum = (partials[2][m].astype(f32) + out_far[m].astype(f32)).astype(bf16)
        out_beside.append(other(out_sum, "zb"))
        far1, far2, *ended = attend_back(
            m, base, rot_query, kvs, begins, out_set, rows_table, log_sums, middle, cotangent[0, :, 0],
            backs[m], cosines, sines, ended,
        )
        far1, far2, ended, out_beside = after((far1, far2, ended, out_beside))
        far.append(
            [
                lax.ppermute(part, ctx, [(s, s - d) for s in range(d, parts)])
                for d, part in ((1, far1), (2, far2))
            ]
        )
        if m < micros - 1:
            out_far, ended = after((out_far, ended))
    def delivered(half, k):
        part = lax.dynamic_index_in_dim(
            half.reshape((2, -1) + half.shape[1:]), (core + far_half + k) % 2, 0, keepdims=False
        )
        return lax.ppermute(
            part, ("core", "zh"), [(2 * s + a, 2 * (s ^ a ^ k) + s) for s in range(2) for a in range(2)]
        )

    far, feed_down = after((far, feed_down))
    down_parts = [delivered(feed_down, k) for k in range(2)]
    grad_middle, branch_low, query_grad, own_pair, gain_sum = ended
    input_grad, keep, send = finish(
        (group_rank % 2).reshape(1), query_grad, own_pair, far, cosines, sines, in_set,
        rows_table, tokens, normed_one, grad_middle, mixed, branch_low, spread, gain_sum,
        block_rows if even else 0,
    )
    keep, send, down_parts = after((keep, send, down_parts))
    if not even:
        both = jnp.concatenate([keep, send]).reshape(groups // 2, 2, block_rows, -1)
        keep, send = (
            lax.dynamic_index_in_dim(both, v, 1, keepdims=False)
            for v in (group_rank % 2, 1 - group_rank % 2)
        )

    def halved(blocks, order, k):
        bit = order[k]
        size = blocks.shape[0]
        at = sorted(order[k:]).index(bit)
        view = blocks.reshape((size >> (at + 1), 2, 1 << at) + blocks.shape[1:])
        own = (group_rank // bit) % 2
        kept = lax.dynamic_index_in_dim(view, own, 1, keepdims=False)
        sent = lax.dynamic_index_in_dim(view, 1 - own, 1, keepdims=False)
        got = swapped(sent.astype(bf16), bit)
        return (kept.astype(f32) + got.astype(f32)).reshape((size // 2,) + blocks.shape[1:])

    blocks = keep.astype(f32) + swapped(send, 1).astype(f32)
    blocks = blocks.reshape(groups // 2, block_rows, -1)
    cut = QW + 2 * LANES
    sides = [blocks[:, :, :cut], blocks[:, :, cut:]]
    orders = [bits[1:], bits[:0:-1]]
    pair_parts = [delivered(feed_pair, 0)]
    for k in range(len(bits) - 1):
        sides = [halved(side, order, k) for side, order in zip(sides, orders)]
        if k == len(bits) - 3:
            sides, pair_parts, feed_pair = after((sides, pair_parts, feed_pair))
            pair_parts.append(delivered(feed_pair, 1))
    sides, pair_parts = after((sides, pair_parts))
    attention_block = jnp.concatenate([side[0] for side in sides], axis=1).astype(bf16)
    attention_block = attention_block.reshape(parts, weight_rows, -1)

    def block_for(steps):
        return lax.dynamic_index_in_dim(
            attention_block, (rank + steps) % parts, 0, keepdims=False
        )

    sums = block_for(0).astype(f32)
    for d in range(1, parts):
        sums = sums + around(block_for(d), d).astype(f32)

    pair_sum = pair_parts[0].astype(f32) + pair_parts[1].astype(f32)
    down_sum = down_parts[0].astype(f32) + down_parts[1].astype(f32)

    total = middle + partials[0] + out_near.astype(f32) + jnp.stack(out_beside).astype(f32)

    edge = 2 * QW + 2 * KW
    return (
        total.astype(bf16)[None, :, None],
        input_grad[None, :, None],
        sums[:, edge],
        sums[:, QW : 2 * QW],
        sums[:, edge + 2],
        sums[:, 2 * QW : 2 * QW + KW],
        sums[:bias_rows, edge + 3],
        sums[:, 2 * QW + KW : edge],
        sums[:bias_rows, edge + 4],
        sums[:, :QW],
        sums[:, edge + 1],
        pair_sum[:, :hidden],
        pair_sum[:, hidden_pad : hidden_pad + hidden],
        down_sum[:, :hidden].T,
    )


def solution(mesh):
    groups, parts = mesh.devices.shape
    split = jax.sharding.Mesh(
        mesh.devices.reshape(groups // 2, 2, parts // 2, 2), ("grp", "core", "zh", "zb")
    )
    dp = ("grp", "core")
    ctx = ("zh", "zb")
    rows = P(dp + ctx, None)
    line = P(dp + ctx)
    tokens = P(dp, None, None, ctx, None)
    up = P(dp, ctx)
    return jax.shard_map(
        body,
        mesh=split,
        in_specs=(
            tokens, P(dp, None, None, None), tokens, line, rows, line, rows, line, rows, line,
            rows, line, up, up, P(ctx, dp),
        ),
        out_specs=(
            tokens, tokens, line, rows, line, rows, line, rows, line, rows, line,
            up, up, P(ctx, dp),
        ),
        check_vma=False,
    )
```

```python
import functools
import jax, jax.numpy as jnp
from jax import lax
from jax.sharding import PartitionSpec as P
from jax.experimental import pallas as pl
from jax.experimental.pallas import tpu as pltpu
D=896; HEADS=14; KV_HEADS=2; HEAD=64; LANES=128
QW=896; KW=128
epsilon=1e-6
bf16=jnp.bfloat16; f32=jnp.float32
LIMIT=56*1024*1024
COST=pl.CostEstimate(flops=1, bytes_accessed=1, transcendentals=0)

def dot(left, right, left_dim, right_dim):
    return lax.dot_general(left, right, (((left_dim,), (right_dim,)), ((), ())), preferred_element_type=f32)

def half_turn(v, back):
    lane = lax.broadcasted_iota(jnp.int32, v.shape, 1) & (HEAD-1)
    width=v.shape[1]
    up = pltpu.roll(v, width-HEAD//2, 1)
    down = pltpu.roll(v, HEAD//2, 1)
    return jnp.where(lane < HEAD//2, up, down)

def scaled(v):
    return lax.rsqrt(jnp.mean(v*v, axis=-1, keepdims=True)+epsilon)

def pairs_kernel(x_ref, wkv_ref, ws_ref, spread_ref, cos_ref, sin_ref, kv_ref, n1_ref, rows_ref, bias_ref):
    @pl.when(pl.program_id(0)==0)
    def _():
        table = ws_ref[...].astype(f32).T[:8]
        rows_ref[...] = table
        close = dot(table.astype(bf16), spread_ref[...],1,0)
        bias_ref[:, :KW] = close[3:4]
        bias_ref[:, KW:] = close[4:5]
    x = x_ref[...].astype(f32)
    n1 = (x*scaled(x)*rows_ref[0:1]).astype(bf16)
    n1_ref[...] = n1
    kv = dot(n1, wkv_ref[...],1,0) + bias_ref[...]
    v = kv[:, :KW]
    kv_ref[:, :KW] = (v*cos_ref[...] + half_turn(v,False)*sin_ref[...]).astype(bf16)
    kv_ref[:, KW:] = kv[:, KW:].astype(bf16)

def queries_kernel(n1_ref, wq_ref, rows_ref, cos_ref, sin_ref, rq_ref):
    q = dot(n1_ref[...], wq_ref[:, 2*KW:],1,0) + rows_ref[2:3]
    cos = cos_ref[...]; sin = sin_ref[...]
    for b in range(QW//LANES):
        v = q[:, b*LANES:(b+1)*LANES]
        r = (v*cos + half_turn(v,False)*sin).astype(bf16)
        rq_ref[:, b*LANES:(b+1)*LANES] = (r.astype(f32)*HEAD**-0.5).astype(bf16)

def project(x, out_set, in_set, spread, cos, sin):
    m, rows, _ = x.shape
    full=lambda shape,idx: pl.BlockSpec(shape, lambda i: idx)
    blk=lambda w: pl.BlockSpec((None,rows,w), lambda i:(i,0,0))
    sd=jax.ShapeDtypeStruct
    params=dict(compiler_params=pltpu.CompilerParams(vmem_limit_bytes=LIMIT), cost_estimate=COST)
    pair, n1, table = pl.pallas_call(
        pairs_kernel, grid=(m,),
        in_specs=[blk(D), full((D,2*KW),(0,0)), full((D,LANES),(0,QW//LANES)), full((D,LANES),(0,0)), blk(LANES), blk(LANES)],
        out_specs=[blk(2*KW), blk(D), full((8,D),(0,0))],
        out_shape=[sd((m,rows,2*KW),bf16), sd((m,rows,D),bf16), sd((8,D),f32)],
        scratch_shapes=[pltpu.VMEM((1,2*KW),f32)],
        name="pairs", **params,
    )(x, in_set, out_set, spread, cos, sin)
    rq = pl.pallas_call(
        queries_kernel, grid=(m,),
        in_specs=[blk(D), full((D,2*KW+QW),(0,0)), full((8,D),(0,0)), blk(LANES), blk(LANES)],
        out_specs=blk(QW), out_shape=sd((m,rows,QW),bf16),
        name="queries", **params,
    )(n1, in_set, table, cos, sin)
    return rq, pair, n1, table

BLOCK=128
def units():
    group=HEADS//KV_HEADS
    out=[]
    for g in range(KV_HEADS):
        for parity in range(2):
            blocks=[h//2 for h in range(g*group,(g+1)*group) if h%2==parity]
            out.append((g,parity,blocks))
    return out

def padded(v, g, parity, lane):
    if g != parity:
        v = pltpu.roll(v.astype(f32), HEAD, 1).astype(bf16)
    keep = (lane >= HEAD) if parity else (lane < HEAD)
    return jnp.where(keep, v, jnp.zeros_like(v))

def mask_bias(begins, rank_base, q0, window, reach):
    key = lax.broadcasted_iota(jnp.int32,(window,BLOCK),0) + (rank_base + q0 - reach)
    query = lax.broadcasted_iota(jnp.int32,(window,BLOCK),1) + (rank_base + q0)
    ok = (key >= begins) & (key <= query)
    return jnp.where(ok, 0.0, -1e30).astype(f32)

def fill_padded(kv_refs, k_ref, v_ref):
    rows = kv_refs[0].shape[0]
    lane = lax.broadcasted_iota(jnp.int32,(rows,LANES),1)
    for p,ref in enumerate(kv_refs):
        kv=ref[...]
        for g,parity,_ in units():
            u=2*g+parity
            k_ref[u, p*rows:(p+1)*rows] = padded(kv[:, :KW], g, parity, lane)
            v_ref[u, p*rows:(p+1)*rows] = padded(kv[:, KW:], g, parity, lane)

def attend_kernel(base_ref, rq_ref, kv0_ref, kv1_ref, kv2_ref, begin_ref, wo_ref, x_ref, rows_ref, *refs):
    n2_ref, mixed_ref, middle_ref, lse_ref, k_ref, v_ref = refs[-6:]
    qb = pl.program_id(0)
    rows = kv0_ref.shape[0]
    reach=512; window=reach+BLOCK
    @pl.when(qb==0)
    def _():
        fill_padded((kv2_ref,kv1_ref,kv0_ref), k_ref, v_ref)
    q0 = qb*BLOCK
    bias = mask_bias(begin_ref[...], base_ref[0], q0, window, reach)
    parts=[None]*7
    start = pl.multiple_of(q0 + (2*rows - reach), BLOCK)
    for g,parity,blocks in units():
        u=2*g+parity
        qs = jnp.concatenate([rq_ref[:, b*LANES:(b+1)*LANES] for b in blocks], axis=0)
        keys = k_ref[u, pl.ds(start,window)]
        vals = v_ref[u, pl.ds(start,window)]
        s = dot(keys, qs, 1, 1) + jnp.concatenate([bias]*len(blocks),axis=1)
        top = jnp.max(s, axis=0, keepdims=True)
        e = jnp.exp(s-top)
        total = jnp.sum(e, axis=0, keepdims=True)
        p = (e*(1.0/total)).astype(bf16)
        o = dot(vals, p, 0, 0)
        lse = top+jnp.log(total)
        for i,b in enumerate(blocks):
            piece=o[:, i*BLOCK:(i+1)*BLOCK]
            parts[b] = piece if parts[b] is None else parts[b]+piece
            lse_ref[0, 2*b+parity:2*b+parity+1, :] = lse[:, i*BLOCK:(i+1)*BLOCK]
    for b in range(7):
        mixed_ref[:, b*LANES:(b+1)*LANES] = parts[b].T.astype(bf16)
    middle = x_ref[...].astype(f32) + dot(mixed_ref[...], wo_ref[...],1,0)
    middle_ref[...] = middle
    n2_ref[...] = (middle*scaled(middle)*rows_ref[1:2]).astype(bf16)

def attend(m, base, rq, kvs, begins, out_set, x, rows_table, before):
    micros, rows, _ = rq.shape; nq=rows//BLOCK
    full=lambda shape: pl.BlockSpec(shape, lambda i: (0,)*len(shape))
    blk=lambda w: pl.BlockSpec((None,BLOCK,w), lambda i:(m,i,0))
    sd=jax.ShapeDtypeStruct
    return pl.pallas_call(
        attend_kernel, grid=(nq,),
        in_specs=[pl.BlockSpec(memory_space=pltpu.SMEM), blk(QW)]+[pl.BlockSpec((None,rows,2*KW),lambda i:(m,0,0))]*3+[pl.BlockSpec((None,1,BLOCK),lambda i:(m,0,i)), full((D,QW)), blk(D), full((8,D))]+[pl.BlockSpec(memory_space=pl.ANY)]*len(before),
        out_specs=[pl.BlockSpec((BLOCK,D),lambda i:(i,0)), blk(QW), blk(D), pl.BlockSpec((None,1,16,BLOCK),lambda i:(m,i,0,0))],
        out_shape=[sd((rows,D),bf16), sd((micros,rows,QW),bf16), sd((micros,rows,D),f32), sd((micros,nq,16,BLOCK),f32)],
        scratch_shapes=[pltpu.VMEM((4,3*rows,LANES),bf16), pltpu.VMEM((4,3*rows,LANES),bf16)],
        input_output_aliases={9+k:1+k for k in range(len(before))},
        compiler_params=pltpu.CompilerParams(vmem_limit_bytes=LIMIT), cost_estimate=COST,
        name="attend",
    )(base, rq, *kvs, begins, out_set, x, rows_table, *before)

def attend_back_kernel(base_ref, rq_ref, kv0_ref, kv1_ref, kv2_ref, begin_ref, wo_ref, rows_ref, lse_ref, middle_ref, dy_ref, cos_ref, sin_ref, *refs, count):
    gs=refs[:count]
    far1_ref, far2_ref, dmid_ref, dmb_ref, dq_ref, own_ref, gain_ref, k_ref, v_ref, dk_ref, dv_ref = refs[-11:]
    qb = pl.program_id(0); nq=pl.num_programs(0)
    rows = kv0_ref.shape[0]
    reach=512; window=reach+BLOCK
    @pl.when(qb==0)
    def _():
        fill_padded((kv2_ref,kv1_ref,kv0_ref), k_ref, v_ref)
        dk_ref[...] = jnp.zeros_like(dk_ref)
        dv_ref[...] = jnp.zeros_like(dv_ref)
        gain_ref[...] = jnp.zeros_like(gain_ref)
    dn2 = gs[0][...].astype(f32)
    for g_ref in gs[1:]:
        dn2 = dn2+g_ref[...].astype(f32)
    middle = middle_ref[...]
    inv = scaled(middle)
    gain_ref[...] += jnp.broadcast_to(jnp.sum(dn2*(middle*inv),axis=0,keepdims=True), gain_ref.shape)
    w2 = dn2*rows_ref[1:2]
    dmid = dy_ref[...].astype(f32) + inv*w2 - middle*(inv*inv*inv)*jnp.mean(w2*middle,axis=-1,keepdims=True)
    dmid_ref[...] = dmid
    dmb = dmid.astype(bf16)
    dmb_ref[...] = dmb
    dmixed = dot(dmb, wo_ref[...],1,1).astype(bf16)
    q0 = qb*BLOCK
    bias = mask_bias(begin_ref[...], base_ref[0], q0, window, reach)
    start = pl.multiple_of(q0 + (2*rows - reach), BLOCK)
    parts=[None]*7
    for g,parity,blocks in units():
        u=2*g+parity
        n=len(blocks)
        qs = jnp.concatenate([rq_ref[:, b*LANES:(b+1)*LANES] for b in blocks], axis=0)
        ds_ = jnp.concatenate([dmixed[:, b*LANES:(b+1)*LANES] for b in blocks], axis=0)
        keys = k_ref[u, pl.ds(start,window)]
        vals = v_ref[u, pl.ds(start,window)]
        lse = jnp.concatenate([lse_ref[0, 2*b+parity:2*b+parity+1, :] for b in blocks],axis=1)
        p = jnp.exp(dot(keys,qs,1,1) + jnp.concatenate([bias]*n,axis=1) - lse)
        dp = dot(vals, ds_, 1, 1)
        t = p*dp
        ds = (t-p*jnp.sum(t,axis=0,keepdims=True)).astype(bf16)
        pb = p.astype(bf16)
        o = dot(keys, ds, 0, 0)
        for i,b in enumerate(blocks):
            piece=o[:, i*BLOCK:(i+1)*BLOCK]
            parts[b] = piece if parts[b] is None else parts[b]+piece
        dk = dot(ds, qs, 1, 0); dv = dot(pb, ds_, 1, 0)
        keep = lax.broadcasted_iota(jnp.int32,(window,LANES),1)
        keep = (keep>=HEAD) if parity else (keep<HEAD)
        dk = jnp.where(keep, dk, 0.0); dv=jnp.where(keep,dv,0.0)
        if g!=parity:
            dk = pltpu.roll(dk,HEAD,1); dv=pltpu.roll(dv,HEAD,1)
        dk_ref[pl.ds(start,window)] += dk
        dv_ref[pl.ds(start,window)] += dv
    cos=cos_ref[...]; sin=sin_ref[...]
    for b in range(7):
        gq = parts[b].T*HEAD**-0.5
        dq_ref[:, b*LANES:(b+1)*LANES] = (gq*cos + half_turn(gq*sin,True)).astype(bf16)
    @pl.when(qb==nq-1)
    def _():
        own_ref[:, :KW] = dk_ref[2*rows:]; own_ref[:, KW:] = dv_ref[2*rows:]
        far1_ref[:, :KW] = dk_ref[rows:2*rows].astype(bf16); far1_ref[:, KW:] = dv_ref[rows:2*rows].astype(bf16)
        far2_ref[:, :KW] = dk_ref[:rows].astype(bf16); far2_ref[:, KW:] = dv_ref[:rows].astype(bf16)

def attend_back(m, base, rq, kvs, begins, out_set, rows_table, lse, middle, dy, gs, cos, sin, before):
    micros, rows, _ = rq.shape; nq=rows//BLOCK
    full=lambda shape: pl.BlockSpec(shape, lambda i: (0,)*len(shape))
    blk=lambda w: pl.BlockSpec((None,BLOCK,w), lambda i:(m,i,0))
    one=lambda h,w: pl.BlockSpec((None,h,w), lambda i:(m,0,0))
    sd=jax.ShapeDtypeStruct
    at=12+len(gs)
    return pl.pallas_call(
        functools.partial(attend_back_kernel,count=len(gs)), grid=(nq,),
        in_specs=[pl.BlockSpec(memory_space=pltpu.SMEM), blk(QW)]+[pl.BlockSpec((None,rows,2*KW),lambda i:(m,0,0))]*3+[pl.BlockSpec((None,1,BLOCK),lambda i:(m,0,i)), full((D,QW)), full((8,D)),
            pl.BlockSpec((None,1,16,BLOCK),lambda i:(m,i,0,0)), blk(D), blk(D)]+[blk(LANES)]*2+[pl.BlockSpec((BLOCK,D),lambda i:(i,0))]*len(gs)+[pl.BlockSpec(memory_space=pl.ANY)]*len(before),
        out_specs=[full((rows,2*KW)), full((rows,2*KW)), blk(D), blk(D), blk(QW), one(rows,2*KW), one(8,D)],
        out_shape=[sd((rows,2*KW),bf16), sd((rows,2*KW),bf16), sd((micros,rows,D),f32), sd((micros,rows,D),bf16), sd((micros,rows,QW),bf16), sd((micros,rows,2*KW),f32), sd((micros,8,D),f32)],
        scratch_shapes=[pltpu.VMEM((4,3*rows,LANES),bf16)]*2+[pltpu.VMEM((3*rows,LANES),f32)]*2,
        input_output_aliases={at+1+k:2+k for k in range(len(before))},
        compiler_params=pltpu.CompilerParams(vmem_limit_bytes=LIMIT), cost_estimate=COST,
        name="attend_back",
    )(base, rq, *kvs, begins, out_set, rows_table, lse, middle, dy, cos, sin, *gs, *before)

CHUNK=256

def feed_kernel(own_ref, *refs, parts, micro, kept):
    ts=refs[:parts]; gs=refs[parts:2*parts]; sets=refs[2*parts:2*parts+2]
    refs=refs[2*parts+2+kept:]
    backs=refs[:parts]; outs=refs[parts:2*parts]
    left_ref,pair_ref,act_ref,x_ref,y_ref,w_ref,own_buf,far_buf,w_sem,in_sem,out_sem=refs[2*parts:]
    i=pl.program_id(0)
    width=w_ref.shape[1]//3
    chunks=width//CHUNK
    def tokens(k):
        return (pltpu.make_async_copy(ts[k],x_ref.at[k],in_sem.at[0,k]),
                pltpu.make_async_copy(gs[k],y_ref.at[k],in_sem.at[1,k]))
    def columns(which,j,p):
        c=slice(p*width+j*CHUNK,p*width+(j+1)*CHUNK)
        return pltpu.make_async_copy(sets[which].at[:,c],w_ref.at[:,c],w_sem.at[p,j])
    def results(k):
        if k==0:
            return (pltpu.make_async_copy(own_buf.at[0],outs[0].at[micro],out_sem.at[0,0]),
                    pltpu.make_async_copy(own_buf.at[1],backs[0],out_sem.at[1,0]))
        return (pltpu.make_async_copy(far_buf.at[0,k-1],outs[k].at[micro],out_sem.at[0,k]),
                pltpu.make_async_copy(far_buf.at[1,k-1],backs[k],out_sem.at[1,k]))
    @pl.when(i==0)
    def _():
        for copy in tokens(0): copy.start()
        for which in range(2):
            @pl.when(own_ref[0]==1-which)
            def _(which=which):
                for j in range(chunks):
                    for p in range(3): columns(which,j,p).start()
        for k in range(1,parts):
            for copy in tokens(k): copy.start()
    for k in range(parts):
        @pl.when(i==k)
        def _(k=k):
            for copy in tokens(k): copy.wait()
    @pl.when(i==0)
    def _():
        for j in range(chunks):
            for p in range(3): columns(0,j,p).wait()
    x=x_ref[i]; y=y_ref[i]
    left_ref[0]=x.T; left_ref[1]=y.T
    for j in range(chunks):
        c=slice(j*CHUNK,(j+1)*CHUNK); c2=slice(width+j*CHUNK,width+(j+1)*CHUNK); c3=slice(2*width+j*CHUNK,2*width+(j+1)*CHUNK)
        g=dot(x,w_ref[:,c],1,0); u=dot(x,w_ref[:,c2],1,0); da=dot(y,w_ref[:,c3],1,0)
        s=jax.nn.sigmoid(g)
        gs_=g*s
        act_ref[:,c]=(gs_*u).astype(bf16)
        pair_ref[:,c]=(da*u*s*(1.0+g*(1.0-s))).astype(bf16)
        pair_ref[:,c2]=(da*gs_).astype(bf16)
    out=dot(act_ref[...],w_ref[:,2*width:],1,1)
    res=dot(pair_ref[...],w_ref[:,:2*width],1,1)
    for k in range(parts):
        @pl.when(i==k)
        def _(k=k):
            if k==0:
                own_buf[0]=out; own_buf[1]=res
            else:
                far_buf[0,k-1]=out.astype(bf16); far_buf[1,k-1]=res.astype(bf16)
            for copy in results(k): copy.start()
    @pl.when(i==parts-1)
    def _():
        for k in range(parts):
            for copy in results(k): copy.wait()

def feed(own, toks, grads, sets, micro, micros, before):
    parts=len(toks); rows=toks[0].shape[0]; hidden_pad=sets[0].shape[1]//3
    blk=lambda w: pl.BlockSpec((rows,w), lambda i:(micro*parts+i,0))
    sd=jax.ShapeDtypeStruct
    everything=rows*parts*micros
    kept=len(before)
    hold=pl.BlockSpec(memory_space=pl.ANY)
    shapes=[sd((rows,D),f32)]+[sd((rows,D),bf16)]*(parts-1)+[sd((micros,rows,D),f32)]+[sd((micros,rows,D),bf16)]*(parts-1)
    n_in=1+2*parts+2
    dma=pltpu.SemaphoreType.DMA
    out=pl.pallas_call(
        functools.partial(feed_kernel,parts=parts,micro=micro,kept=kept), grid=(parts,),
        in_specs=[pl.BlockSpec(memory_space=pltpu.SMEM)]+[hold]*(2*parts+2+kept),
        out_specs=[hold]*(2*parts)+[pl.BlockSpec((2,None,D,rows), lambda i:(0,micro*parts+i,0,0)),blk(2*hidden_pad),blk(hidden_pad)],
        out_shape=shapes+[sd((2,parts*micros,D,rows),bf16)]+[sd((everything,w),bf16) for w in (2*hidden_pad,hidden_pad)],
        scratch_shapes=[pltpu.VMEM((parts,rows,D),bf16)]*2+[pltpu.VMEM(sets[0].shape,bf16),pltpu.VMEM((2,rows,D),f32),pltpu.VMEM((2,parts-1,rows,D),bf16),
            dma((3,hidden_pad//CHUNK)),dma((2,parts)),dma((2,parts))],
        input_output_aliases={n_in+k:parts+k for k in range(kept)},
        compiler_params=pltpu.CompilerParams(vmem_limit_bytes=LIMIT), cost_estimate=COST,
        name="feed",
    )(own,*toks,*grads,*sets,*before)
    return out[:parts], out[parts:]

def finish_kernel(bit_ref, dq_ref, own_ref, cos_ref, sin_ref, wq_ref, wkv_ref, rows_ref, x_ref, n1_ref, dmid_ref, mixed_ref, dmb_ref, spread_ref, gain2_ref, *refs, near, block):
    far=refs[:-6]
    ig_ref, keep_ref, send_ref, acc_ref, small_ref, sum_ref = refs[-6:]
    i=pl.program_id(0)
    @pl.when(i==0)
    def _():
        acc_ref[...]=jnp.zeros_like(acc_ref)
        small_ref[...]=jnp.zeros_like(small_ref)
    for m in range(len(far)//near):
        @pl.when(i==m)
        def _(m=m):
            own=own_ref[...]
            for ref in far[m*near:(m+1)*near]:
                own=own+ref[...].astype(f32)
            sum_ref[...]=own
    own=sum_ref[...]
    k=own[:, :KW]
    cos=cos_ref[...]; sin=sin_ref[...]
    dk=(k*cos+half_turn(k*sin,True)).astype(bf16)
    dv=own[:, KW:].astype(bf16)
    dkv=jnp.concatenate([dk,dv],axis=1)
    dq=dq_ref[...]
    dn1=dot(dq,wq_ref[:, 2*KW:],1,1)+dot(dkv,wkv_ref[...],1,1)
    x=x_ref[...].astype(f32); inv=scaled(x)
    small_ref[0:1]+=jnp.sum(dn1*(x*inv),axis=0,keepdims=True)
    small_ref[1:2]+=gain2_ref[0:1]
    small_ref[2:3]+=jnp.sum(dq.astype(f32),axis=0,keepdims=True)
    small_ref[3:4,:2*KW]+=jnp.sum(dkv.astype(f32),axis=0,keepdims=True)
    w1=dn1*rows_ref[0:1]
    ig_ref[...]=dmid_ref[...]+inv*w1-x*(inv*inv*inv)*jnp.mean(w1*x,axis=-1,keepdims=True)
    n1=n1_ref[...]
    acc_ref[:, :QW]+=dot(mixed_ref[...],dmb_ref[...],0,0)
    acc_ref[:, QW:2*QW]+=dot(n1,dq,0,0)
    acc_ref[:, 2*QW:2*QW+2*KW]+=dot(n1,dkv,0,0)
    @pl.when(i==pl.num_programs(0)-1)
    def _():
        pair=jnp.concatenate([small_ref[3:4,:KW],small_ref[3:4,KW:2*KW],jnp.zeros((6,KW),f32)],axis=0).astype(bf16)
        table=jnp.concatenate([small_ref[0:3],dot(pair,spread_ref[...],1,1)[0:2],jnp.zeros((LANES-5,D),f32)],axis=0)
        acc_ref[:, 2*QW+2*KW:]=table.T
        if block:
            for j in range(D//block//2):
                at=pl.multiple_of((2*j+bit_ref[0])*block,16)
                keep_ref[j*block:(j+1)*block]=acc_ref[pl.ds(at,block)].astype(bf16)
                at=pl.multiple_of((2*j+1-bit_ref[0])*block,16)
                send_ref[j*block:(j+1)*block]=acc_ref[pl.ds(at,block)].astype(bf16)
        else:
            keep_ref[...]=acc_ref[:D//2].astype(bf16)
            send_ref[...]=acc_ref[D//2:].astype(bf16)

def finish(bit,dq,own,far,cos,sin,in_set,rows_table,x,n1,dmid,mixed,dmb,spread,gain2,block):
    m,rows,_=x.shape
    full=lambda shape,idx=(0,0): pl.BlockSpec(shape, lambda i: idx)
    blk=lambda w,h=rows: pl.BlockSpec((None,h,w), lambda i:(i,0,0))
    sd=jax.ShapeDtypeStruct
    width=2*QW+2*KW+LANES
    near=len(far[0])
    far=[f for pieces in far for f in pieces]
    return pl.pallas_call(
        functools.partial(finish_kernel,near=near,block=block), grid=(m,),
        in_specs=[pl.BlockSpec(memory_space=pltpu.SMEM),blk(QW),blk(2*KW),blk(LANES),blk(LANES),full((D,2*KW+QW)),full((D,2*KW)),full((8,D)),blk(D),blk(D),blk(D),blk(QW),blk(D),full((D,LANES)),blk(D,8)]+[full((rows,2*KW))]*len(far),
        out_specs=[blk(D),full((D//2,width)),full((D//2,width))],
        out_shape=[sd((m,rows,D),f32),sd((D//2,width),bf16),sd((D//2,width),bf16)],
        scratch_shapes=[pltpu.VMEM((D,width),f32),pltpu.VMEM((8,D),f32),pltpu.VMEM((rows,2*KW),f32)],
        compiler_params=pltpu.CompilerParams(vmem_limit_bytes=LIMIT), cost_estimate=COST,
        name="finish",
    )(bit,dq,own,cos,sin,in_set,in_set,rows_table,x,n1,dmid,mixed,dmb,spread,gain2,*far)

def weights_kernel(left_ref, right_ref, out_ref):
    left=jnp.concatenate([left_ref[k] for k in range(left_ref.shape[0])],axis=1)
    out_ref[...]=dot(left,right_ref[...],1,0).astype(bf16)

def weights(left,which,right,chunk):
    rows,width=right.shape
    return pl.pallas_call(
        weights_kernel, grid=(width//chunk,),
        in_specs=[pl.BlockSpec((None,)+left.shape[1:],lambda j:(which,0,0,0),pipeline_mode=pl.Buffered(1)),pl.BlockSpec((rows,chunk),lambda j:(0,j))],
        out_specs=pl.BlockSpec((D,chunk),lambda j:(0,j)), out_shape=jax.ShapeDtypeStruct((D,width),bf16),
        compiler_params=pltpu.CompilerParams(vmem_limit_bytes=LIMIT), cost_estimate=COST,
        name="weights",
    )(left,right)

def woven_kernel(core_ref, *refs):
    n=len(refs)//3
    mine=refs[:n]; got=refs[n:2*n]; outs=refs[2*n:]
    core=core_ref[0]; j=pl.program_id(0)
    for k in range(n):
        rows=mine[k].shape[0]
        outs[k][pl.ds(pl.multiple_of(core*rows,16),rows)]=mine[k][...]
        outs[k][pl.ds(pl.multiple_of((1-core)*rows,16),rows)]=got[k][...]

def woven(core, mine, got):
    n=len(mine); blocks,rows,_=mine[0].shape
    size=blocks.bit_length()-1
    def turned(j):
        return sum(((j>>k)&1)<<(size-1-k) for k in range(size))
    places=[lambda j:(j,0,0), lambda j:(turned(j),0,0)]
    shapes=[jax.ShapeDtypeStruct((2*blocks*rows,v.shape[2]),v.dtype) for v in mine]
    return pl.pallas_call(
        woven_kernel, grid=(blocks,), in_specs=[pl.BlockSpec(memory_space=pltpu.SMEM)]+[pl.BlockSpec((None,)+v.shape[1:],places[k%n]) for k,v in enumerate(mine+got)],
        out_specs=[pl.BlockSpec((2*rows,v.shape[2]),lambda j:(j,0)) for v in mine], out_shape=shapes,
        compiler_params=pltpu.CompilerParams(vmem_limit_bytes=LIMIT), cost_estimate=COST,
        name="woven",
    )(core,*mine,*got)


LONGEST = 512


def after(values_in, *needed):
    return lax.optimization_barrier((values_in, needed))[0]


theta = 10000.0


def body(
    layer_in,
    doc_ids,
    cotangent,
    first_gain,
    query_weight,
    query_bias,
    key_weight,
    key_bias,
    value_weight,
    value_bias,
    out_weight,
    second_gain,
    gate_weight,
    up_weight,
    down_weight,
):
    ctx = ("zh", "zb")
    dp = ("grp", "core")
    parts = lax.axis_size(ctx)
    rank = lax.axis_index(ctx)
    micros = layer_in.shape[1]
    shard_rows = layer_in.shape[3]
    hidden = gate_weight.shape[1]
    hidden_pad = -(-hidden // (2 * LANES)) * 2 * LANES
    weight_rows = query_weight.shape[0]
    bias_rows = key_bias.shape[0]
    reach_parts = -(-LONGEST // shard_rows)
    core = lax.axis_index("core")
    far_half = lax.axis_index("zh")

    group_rank = lax.axis_index(dp)
    groups = lax.axis_size(dp)
    bits = [1 << k for k in range(groups.bit_length() - 1)]
    block_rows = parts * weight_rows
    even = block_rows % 16 == 0

    def swapped(values_in, bit):
        return lax.ppermute(values_in, dp, [(s, s ^ bit) for s in range(groups)])

    def doubled(blocks, order, k):
        bit = order[k]
        got = swapped(blocks, bit)
        low = (group_rank // bit) % 2 == 0
        return jnp.stack([jnp.where(low, blocks, got), jnp.where(low, got, blocks)])

    def around(values_in, steps):
        return lax.ppermute(values_in, ctx, [(s, (s + steps) % parts) for s in range(parts)])

    def other(values_in, axis):
        return lax.ppermute(values_in, axis, [(0, 1), (1, 0)])

    def corner(values_in):
        return lax.ppermute(values_in, ("core", "zb"), [(s, 3 - s) for s in range(4)])

    def shared(values_in):
        beside = other(values_in, "zb")
        return [values_in, other(values_in, "core"), beside, other(beside, "core")]

    def collected(values_in):
        pieces = [values_in] + [around(values_in, d) for d in range(1, parts)]
        ordered = [pieces[d] for d in range(parts - 1, -1, -1)]
        ordered = jnp.stack(ordered + ordered[:-1])
        taken = lax.dynamic_slice_in_dim(ordered, parts - 1 - rank, parts, 0)
        return taken.reshape((-1,) + values_in.shape[1:])

    def column(values_in):
        return jnp.pad(values_in, (0, weight_rows - values_in.shape[0]))[:, None]

    def wide(values_in):
        return jnp.pad(values_in, ((0, 0), (0, hidden_pad - hidden)))

    own_block = jnp.concatenate([wide(gate_weight), wide(up_weight), wide(down_weight.T)], axis=1)
    own_set = lax.all_gather(own_block, dp, axis=0, tiled=True)
    small = jnp.concatenate(
        [column(v) for v in (first_gain, second_gain, query_bias, key_bias, value_bias)], axis=1
    )
    small = jnp.pad(small, ((0, 0), (0, LANES - small.shape[1])))
    own_attention = jnp.concatenate(
        [out_weight, small, key_weight, value_weight, query_weight], axis=1
    )
    first_block = collected(own_attention)
    row = jnp.arange(D, dtype=jnp.int32)[:, None]
    place = row // weight_rows * bias_rows + row % weight_rows
    spread = (
        (place == jnp.arange(LANES, dtype=jnp.int32)[None, :]) & (row % weight_rows < bias_rows)
    ).astype(bf16)

    docs = doc_ids[0, :, 0]
    own_docs = lax.dynamic_slice_in_dim(docs, rank * shard_rows, shard_rows, 1)
    begins = jnp.sum((docs[:, None, :] < own_docs[:, :, None]).astype(jnp.int32), axis=2)
    row_index = rank * shard_rows + jnp.arange(shard_rows, dtype=jnp.int32)
    positions = row_index[None, :] - begins
    frequency = jnp.power(f32(theta), -(jnp.arange(HEAD // 2, dtype=f32) * (2.0 / HEAD)))
    angle = positions.astype(f32)[:, :, None] * frequency
    cosines, sines = jnp.cos(angle), jnp.sin(angle)
    cosines = jnp.concatenate([cosines] * (2 * LANES // HEAD), axis=2)
    sines = jnp.concatenate([-sines, sines] * (LANES // HEAD), axis=2)
    base = (rank * shard_rows).reshape(1)

    own_block, first_block = after((own_block, first_block))
    cut = QW + LANES
    firsts = [first_block[:, :cut], first_block[:, cut:]]
    gather_orders = [bits[1:] + bits[:1], bits[:0:-1] + bits[:1]]
    widths = own_block.shape[1] // LANES // 4 * LANES
    edges = [0, widths, own_block.shape[1] - widths, own_block.shape[1]]
    other_block = []
    upstream = [cotangent[0, m, 0] for m in range(micros)]
    crossed = []
    for k in range(len(bits)):
        if k < len(bits) - 1 or not even:
            firsts = [doubled(side, order, k) for side, order in zip(firsts, gather_orders)]
        else:
            gots = [swapped(side, 1) for side in firsts]
            firsts = [firsts, gots]
        if k < 3:
            other_block.append(other(own_block[:, edges[k] : edges[k + 1]], "zh"))
        firsts, other_block, own_block, spread, cosines, sines, begins, upstream, crossed = after(
            (firsts, other_block, own_block, spread, cosines, sines, begins, upstream, crossed)
        )
    other_set = lax.all_gather(jnp.concatenate(other_block, axis=1), dp, axis=0, tiled=True)
    if even:
        firsts, gots = ([v.reshape((-1,) + v.shape[-2:]) for v in part] for part in firsts)
        out_set, in_set = woven(core.reshape(1), firsts, gots)
    else:
        out_set, in_set = (
            jnp.transpose(
                side, [list(reversed(order)).index(bit) for bit in reversed(bits)] + [-2, -1]
            ).reshape(-1, side.shape[-1])
            for side, order in zip(firsts, gather_orders)
        )
    sets = (own_set, other_set)
    own_quarter = (core == far_half).astype(jnp.int32).reshape(1)

    tokens = layer_in[0, :, 0]
    rot_query, pairs, normed_one, rows_table = project(
        tokens, out_set, in_set, spread, cosines, sines
    )
    kvs = [pairs] + [
        lax.ppermute(pairs, ctx, [(s, s + d) for s in range(parts - d)])
        for d in range(1, reach_parts + 1)
    ]

    kvs, rot_query, upstream = after((kvs, rot_query, upstream))
    crossed.append(other(upstream[0], "zb"))

    begins = begins[:, None, :]
    exchanged = []
    held = ()
    for m in range(micros):
        normed_two, *held = attend(
            m, base, rot_query, kvs, begins, out_set, tokens, rows_table, held
        )
        if m == 0:
            upstream, crossed, normed_two = after((upstream, crossed, normed_two))
        exchanged.append([normed_two, other(normed_two, "core"), other(normed_two, "zb")])
        if m == 0:
            crossed += [other(u, "zb") for u in upstream[1:]]
            upstream_pieces = [[u, other(u, "core"), v] for u, v in zip(upstream, crossed)]
    exchanged[-1].append(corner(normed_two))
    exchanged[:-1], upstream_pieces[0], exchanged[-1][0] = after(
        (exchanged[:-1], upstream_pieces[0], normed_two)
    )
    for early in exchanged[:-1] + upstream_pieces[:1]:
        early.append(other(early[2], "core"))
    mixed, middle, log_sums = held

    backs = []
    before = ()
    for m in range(micros):
        back, before = feed(
            own_quarter, exchanged[m], upstream_pieces[m], sets, m, micros, before
        )
        if m < micros - 1:
            back, upstream_pieces[m + 1] = after((back, upstream_pieces[m + 1]))
            upstream_pieces[m + 1].append(other(upstream_pieces[m + 1][2], "core"))
        backs.append([back[0], other(back[1], "core"), other(back[2], "zb"), corner(back[3])])
    partials = before[:4]
    out_near = other(partials[1], "core")
    out_far = other(partials[3], "core")

    left, pair, act = after(before[4:], backs[0])
    feed_down = weights(left, 1, act, 256)
    backs[-1][1:3], left, pair, feed_down = after((backs[-1][1:3], left, pair, feed_down))
    feed_pair = weights(left, 0, pair, 512)
    backs, feed_pair, out_near, out_far = after((backs, feed_pair, out_near, out_far))
    feed_down = lax.psum_scatter(feed_down, "grp", scatter_dimension=0, tiled=True)
    feed_pair = lax.psum_scatter(feed_pair, "grp", scatter_dimension=0, tiled=True)

    far = []
    ended = ()
    out_beside = []
    for m in range(micros):
        out_sum = (partials[2][m].astype(f32) + out_far[m].astype(f32)).astype(bf16)
        out_beside.append(other(out_sum, "zb"))
        far1, far2, *ended = attend_back(
            m, base, rot_query, kvs, begins, out_set, rows_table, log_sums, middle, cotangent[0, :, 0],
            backs[m], cosines, sines, ended,
        )
        far1, far2, ended, out_beside = after((far1, far2, ended, out_beside))
        far.append(
            [
                lax.ppermute(part, ctx, [(s, s - d) for s in range(d, parts)])
                for d, part in ((1, far1), (2, far2))
            ]
        )
        if m < micros - 1:
            out_far, ended = after((out_far, ended))
    def delivered(half, k):
        part = lax.dynamic_index_in_dim(
            half.reshape((2, -1) + half.shape[1:]), (core + far_half + k) % 2, 0, keepdims=False
        )
        return lax.ppermute(
            part, ("core", "zh"), [(2 * s + a, 2 * (s ^ a ^ k) + s) for s in range(2) for a in range(2)]
        )

    far, feed_down = after((far, feed_down))
    down_parts = [delivered(feed_down, k) for k in range(2)]
    grad_middle, branch_low, query_grad, own_pair, gain_sum = ended
    input_grad, keep, send = finish(
        (group_rank % 2).reshape(1), query_grad, own_pair, far, cosines, sines, in_set,
        rows_table, tokens, normed_one, grad_middle, mixed, branch_low, spread, gain_sum,
        block_rows if even else 0,
    )
    keep, send, down_parts = after((keep, send, down_parts))
    if not even:
        both = jnp.concatenate([keep, send]).reshape(groups // 2, 2, block_rows, -1)
        keep, send = (
            lax.dynamic_index_in_dim(both, v, 1, keepdims=False)
            for v in (group_rank % 2, 1 - group_rank % 2)
        )

    def halved(blocks, order, k):
        bit = order[k]
        size = blocks.shape[0]
        at = sorted(order[k:]).index(bit)
        view = blocks.reshape((size >> (at + 1), 2, 1 << at) + blocks.shape[1:])
        own = (group_rank // bit) % 2
        kept = lax.dynamic_index_in_dim(view, own, 1, keepdims=False)
        sent = lax.dynamic_index_in_dim(view, 1 - own, 1, keepdims=False)
        got = swapped(sent.astype(bf16), bit)
        return (kept.astype(f32) + got.astype(f32)).reshape((size // 2,) + blocks.shape[1:])

    blocks = keep.astype(f32) + swapped(send, 1).astype(f32)
    blocks = blocks.reshape(groups // 2, block_rows, -1)
    cut = QW + 2 * LANES
    sides = [blocks[:, :, :cut], blocks[:, :, cut:]]
    orders = [bits[1:], bits[:0:-1]]
    pair_parts = [delivered(feed_pair, 0)]
    for k in range(len(bits) - 1):
        sides = [halved(side, order, k) for side, order in zip(sides, orders)]
        if k == len(bits) - 3:
            sides, pair_parts, feed_pair = after((sides, pair_parts, feed_pair))
            pair_parts.append(delivered(feed_pair, 1))
    sides, down_parts = after((sides, down_parts))
    attention_block = jnp.concatenate([side[0] for side in sides], axis=1).astype(bf16)
    attention_block = attention_block.reshape(parts, weight_rows, -1)

    def block_for(steps):
        return lax.dynamic_index_in_dim(
            attention_block, (rank + steps) % parts, 0, keepdims=False
        )

    ends = [around(block_for(d), d) for d in range(1, parts)]
    ends, pair_parts = after((ends, pair_parts))
    sums = block_for(0).astype(f32)
    for end in ends:
        sums = sums + end.astype(f32)

    pair_sum = pair_parts[0].astype(f32) + pair_parts[1].astype(f32)
    down_sum = down_parts[0].astype(f32) + down_parts[1].astype(f32)

    total = middle + partials[0] + out_near.astype(f32) + jnp.stack(out_beside).astype(f32)

    edge = 2 * QW + 2 * KW
    return (
        total.astype(bf16)[None, :, None],
        input_grad[None, :, None],
        sums[:, edge],
        sums[:, QW : 2 * QW],
        sums[:, edge + 2],
        sums[:, 2 * QW : 2 * QW + KW],
        sums[:bias_rows, edge + 3],
        sums[:, 2 * QW + KW : edge],
        sums[:bias_rows, edge + 4],
        sums[:, :QW],
        sums[:, edge + 1],
        pair_sum[:, :hidden],
        pair_sum[:, hidden_pad : hidden_pad + hidden],
        down_sum[:, :hidden].T,
    )


def solution(mesh):
    groups, parts = mesh.devices.shape
    split = jax.sharding.Mesh(
        mesh.devices.reshape(groups // 2, 2, parts // 2, 2), ("grp", "core", "zh", "zb")
    )
    dp = ("grp", "core")
    ctx = ("zh", "zb")
    rows = P(dp + ctx, None)
    line = P(dp + ctx)
    tokens = P(dp, None, None, ctx, None)
    up = P(dp, ctx)
    return jax.shard_map(
        body,
        mesh=split,
        in_specs=(
            tokens, P(dp, None, None, None), tokens, line, rows, line, rows, line, rows, line,
            rows, line, up, up, P(ctx, dp),
        ),
        out_specs=(
            tokens, tokens, line, rows, line, rows, line, rows, line, rows, line,
            up, up, P(ctx, dp),
        ),
        check_vma=False,
    )
```

```python
import functools
import jax, jax.numpy as jnp
from jax import lax
from jax.sharding import PartitionSpec as P
from jax.experimental import pallas as pl
from jax.experimental.pallas import tpu as pltpu
D=896; HEADS=14; KV_HEADS=2; HEAD=64; LANES=128
QW=896; KW=128
epsilon=1e-6
bf16=jnp.bfloat16; f32=jnp.float32
LIMIT=56*1024*1024
COST=pl.CostEstimate(flops=1, bytes_accessed=1, transcendentals=0)

def dot(left, right, left_dim, right_dim):
    return lax.dot_general(left, right, (((left_dim,), (right_dim,)), ((), ())), preferred_element_type=f32)

def half_turn(v, back):
    lane = lax.broadcasted_iota(jnp.int32, v.shape, 1) & (HEAD-1)
    width=v.shape[1]
    up = pltpu.roll(v, width-HEAD//2, 1)
    down = pltpu.roll(v, HEAD//2, 1)
    return jnp.where(lane < HEAD//2, up, down)

def scaled(v):
    return lax.rsqrt(jnp.mean(v*v, axis=-1, keepdims=True)+epsilon)

def pairs_kernel(x_ref, wkv_ref, ws_ref, spread_ref, cos_ref, sin_ref, n1_ref, rows_ref, *refs):
    kv_refs=refs[:-1]; bias_ref=refs[-1]
    @pl.when(pl.program_id(0)==0)
    def _():
        table = ws_ref[...].astype(f32).T[:8]
        rows_ref[...] = table
        close = dot(table.astype(bf16), spread_ref[...],1,0)
        bias_ref[:, :KW] = close[3:4]
        bias_ref[:, KW:] = close[4:5]
    x = x_ref[...].astype(f32)
    n1 = (x*scaled(x)*rows_ref[0:1]).astype(bf16)
    n1_ref[...] = n1
    kv = dot(n1, wkv_ref[...],1,0) + bias_ref[...]
    v = kv[:, :KW]
    pair = jnp.concatenate([v*cos_ref[...] + half_turn(v,False)*sin_ref[...], kv[:, KW:]],axis=1).astype(bf16)
    for m,kv_ref in enumerate(kv_refs):
        @pl.when(pl.program_id(0)==m)
        def _(kv_ref=kv_ref): kv_ref[...] = pair

def queries_kernel(n1_ref, wq_ref, rows_ref, cos_ref, sin_ref, rq_ref):
    q = dot(n1_ref[...], wq_ref[:, 2*KW:],1,0) + rows_ref[2:3]
    cos = cos_ref[...]; sin = sin_ref[...]
    for b in range(QW//LANES):
        v = q[:, b*LANES:(b+1)*LANES]
        r = (v*cos + half_turn(v,False)*sin).astype(bf16)
        rq_ref[:, b*LANES:(b+1)*LANES] = (r.astype(f32)*HEAD**-0.5).astype(bf16)

def project(x, out_set, in_set, spread, cos, sin):
    m, rows, _ = x.shape
    full=lambda shape,idx: pl.BlockSpec(shape, lambda i: idx)
    blk=lambda w: pl.BlockSpec((None,rows,w), lambda i:(i,0,0))
    sd=jax.ShapeDtypeStruct
    params=dict(compiler_params=pltpu.CompilerParams(vmem_limit_bytes=LIMIT), cost_estimate=COST)
    n1, table, *pair = pl.pallas_call(
        pairs_kernel, grid=(m,),
        in_specs=[blk(D), full((D,2*KW),(0,0)), full((D,LANES),(0,QW//LANES)), full((D,LANES),(0,0)), blk(LANES), blk(LANES)],
        out_specs=[blk(D), full((8,D),(0,0))]+[full((rows,2*KW),(0,0))]*m,
        out_shape=[sd((m,rows,D),bf16), sd((8,D),f32)]+[sd((rows,2*KW),bf16)]*m,
        scratch_shapes=[pltpu.VMEM((1,2*KW),f32)],
        name="pairs", **params,
    )(x, in_set, out_set, spread, cos, sin)
    rq = pl.pallas_call(
        queries_kernel, grid=(m,),
        in_specs=[blk(D), full((D,2*KW+QW),(0,0)), full((8,D),(0,0)), blk(LANES), blk(LANES)],
        out_specs=blk(QW), out_shape=sd((m,rows,QW),bf16),
        name="queries", **params,
    )(n1, in_set, table, cos, sin)
    return rq, pair, n1, table

BLOCK=128
def units():
    group=HEADS//KV_HEADS
    out=[]
    for g in range(KV_HEADS):
        for parity in range(2):
            blocks=[h//2 for h in range(g*group,(g+1)*group) if h%2==parity]
            out.append((g,parity,blocks))
    return out

def padded(v, g, parity, lane):
    if g != parity:
        v = pltpu.roll(v.astype(f32), HEAD, 1).astype(bf16)
    keep = (lane >= HEAD) if parity else (lane < HEAD)
    return jnp.where(keep, v, jnp.zeros_like(v))

def mask_bias(begins, rank_base, q0, window, reach):
    key = lax.broadcasted_iota(jnp.int32,(window,BLOCK),0) + (rank_base + q0 - reach)
    query = lax.broadcasted_iota(jnp.int32,(window,BLOCK),1) + (rank_base + q0)
    ok = (key >= begins) & (key <= query)
    return jnp.where(ok, 0.0, -1e30).astype(f32)

def fill_padded(kv_refs, k_ref, v_ref):
    rows = kv_refs[0].shape[0]
    lane = lax.broadcasted_iota(jnp.int32,(rows,LANES),1)
    for p,ref in enumerate(kv_refs):
        kv=ref[...]
        for g,parity,_ in units():
            u=2*g+parity
            k_ref[u, p*rows:(p+1)*rows] = padded(kv[:, :KW], g, parity, lane)
            v_ref[u, p*rows:(p+1)*rows] = padded(kv[:, KW:], g, parity, lane)

def attend_kernel(base_ref, rq_ref, kv0_ref, kv1_ref, kv2_ref, begin_ref, wo_ref, x_ref, rows_ref, *refs):
    n2_ref, mixed_ref, middle_ref, lse_ref, k_ref, v_ref = refs[-6:]
    qb = pl.program_id(0)
    rows = kv0_ref.shape[0]
    reach=512; window=reach+BLOCK
    @pl.when(qb==0)
    def _():
        fill_padded((kv2_ref,kv1_ref,kv0_ref), k_ref, v_ref)
    q0 = qb*BLOCK
    bias = mask_bias(begin_ref[...], base_ref[0], q0, window, reach)
    parts=[None]*7
    start = pl.multiple_of(q0 + (2*rows - reach), BLOCK)
    for g,parity,blocks in units():
        u=2*g+parity
        qs = jnp.concatenate([rq_ref[:, b*LANES:(b+1)*LANES] for b in blocks], axis=0)
        keys = k_ref[u, pl.ds(start,window)]
        vals = v_ref[u, pl.ds(start,window)]
        s = dot(keys, qs, 1, 1) + jnp.concatenate([bias]*len(blocks),axis=1)
        top = jnp.max(s, axis=0, keepdims=True)
        e = jnp.exp(s-top)
        total = jnp.sum(e, axis=0, keepdims=True)
        p = (e*(1.0/total)).astype(bf16)
        o = dot(vals, p, 0, 0)
        lse = top+jnp.log(total)
        for i,b in enumerate(blocks):
            piece=o[:, i*BLOCK:(i+1)*BLOCK]
            parts[b] = piece if parts[b] is None else parts[b]+piece
            lse_ref[0, 2*b+parity:2*b+parity+1, :] = lse[:, i*BLOCK:(i+1)*BLOCK]
    for b in range(7):
        mixed_ref[:, b*LANES:(b+1)*LANES] = parts[b].T.astype(bf16)
    middle = x_ref[...].astype(f32) + dot(mixed_ref[...], wo_ref[...],1,0)
    middle_ref[...] = middle
    n2_ref[...] = (middle*scaled(middle)*rows_ref[1:2]).astype(bf16)

def attend(m, base, rq, kvs, begins, out_set, x, rows_table, before):
    micros, rows, _ = rq.shape; nq=rows//BLOCK
    full=lambda shape: pl.BlockSpec(shape, lambda i: (0,)*len(shape))
    blk=lambda w: pl.BlockSpec((None,BLOCK,w), lambda i:(m,i,0))
    sd=jax.ShapeDtypeStruct
    return pl.pallas_call(
        attend_kernel, grid=(nq,),
        in_specs=[pl.BlockSpec(memory_space=pltpu.SMEM), blk(QW)]+[full((rows,2*KW))]*3+[pl.BlockSpec((None,1,BLOCK),lambda i:(m,0,i)), full((D,QW)), blk(D), full((8,D))]+[pl.BlockSpec(memory_space=pl.ANY)]*len(before),
        out_specs=[pl.BlockSpec((BLOCK,D),lambda i:(i,0)), blk(QW), blk(D), pl.BlockSpec((None,1,16,BLOCK),lambda i:(m,i,0,0))],
        out_shape=[sd((rows,D),bf16), sd((micros,rows,QW),bf16), sd((micros,rows,D),f32), sd((micros,nq,16,BLOCK),f32)],
        scratch_shapes=[pltpu.VMEM((4,3*rows,LANES),bf16), pltpu.VMEM((4,3*rows,LANES),bf16)],
        input_output_aliases={9+k:1+k for k in range(len(before))},
        compiler_params=pltpu.CompilerParams(vmem_limit_bytes=LIMIT), cost_estimate=COST,
        name="attend",
    )(base, rq, *kvs, begins, out_set, x, rows_table, *before)

def attend_back_kernel(base_ref, rq_ref, kv0_ref, kv1_ref, kv2_ref, begin_ref, wo_ref, rows_ref, lse_ref, middle_ref, dy_ref, cos_ref, sin_ref, *refs, count):
    gs=refs[:count]
    far1_ref, far2_ref, dmid_ref, dmb_ref, dq_ref, own_ref, gain_ref, k_ref, v_ref, dk_ref, dv_ref = refs[-11:]
    qb = pl.program_id(0); nq=pl.num_programs(0)
    rows = kv0_ref.shape[0]
    reach=512; window=reach+BLOCK
    @pl.when(qb==0)
    def _():
        fill_padded((kv2_ref,kv1_ref,kv0_ref), k_ref, v_ref)
        dk_ref[...] = jnp.zeros_like(dk_ref)
        dv_ref[...] = jnp.zeros_like(dv_ref)
        gain_ref[...] = jnp.zeros_like(gain_ref)
    dn2 = gs[0][...].astype(f32)
    for g_ref in gs[1:]:
        dn2 = dn2+g_ref[...].astype(f32)
    middle = middle_ref[...]
    inv = scaled(middle)
    gain_ref[...] += jnp.broadcast_to(jnp.sum(dn2*(middle*inv),axis=0,keepdims=True), gain_ref.shape)
    w2 = dn2*rows_ref[1:2]
    dmid = dy_ref[...].astype(f32) + inv*w2 - middle*(inv*inv*inv)*jnp.mean(w2*middle,axis=-1,keepdims=True)
    dmid_ref[...] = dmid
    dmb = dmid.astype(bf16)
    dmb_ref[...] = dmb
    dmixed = dot(dmb, wo_ref[...],1,1).astype(bf16)
    q0 = qb*BLOCK
    bias = mask_bias(begin_ref[...], base_ref[0], q0, window, reach)
    start = pl.multiple_of(q0 + (2*rows - reach), BLOCK)
    parts=[None]*7
    for g,parity,blocks in units():
        u=2*g+parity
        n=len(blocks)
        qs = jnp.concatenate([rq_ref[:, b*LANES:(b+1)*LANES] for b in blocks], axis=0)
        ds_ = jnp.concatenate([dmixed[:, b*LANES:(b+1)*LANES] for b in blocks], axis=0)
        keys = k_ref[u, pl.ds(start,window)]
        vals = v_ref[u, pl.ds(start,window)]
        lse = jnp.concatenate([lse_ref[0, 2*b+parity:2*b+parity+1, :] for b in blocks],axis=1)
        p = jnp.exp(dot(keys,qs,1,1) + jnp.concatenate([bias]*n,axis=1) - lse)
        dp = dot(vals, ds_, 1, 1)
        t = p*dp
        ds = (t-p*jnp.sum(t,axis=0,keepdims=True)).astype(bf16)
        pb = p.astype(bf16)
        o = dot(keys, ds, 0, 0)
        for i,b in enumerate(blocks):
            piece=o[:, i*BLOCK:(i+1)*BLOCK]
            parts[b] = piece if parts[b] is None else parts[b]+piece
        dk = dot(ds, qs, 1, 0); dv = dot(pb, ds_, 1, 0)
        keep = lax.broadcasted_iota(jnp.int32,(window,LANES),1)
        keep = (keep>=HEAD) if parity else (keep<HEAD)
        dk = jnp.where(keep, dk, 0.0); dv=jnp.where(keep,dv,0.0)
        if g!=parity:
            dk = pltpu.roll(dk,HEAD,1); dv=pltpu.roll(dv,HEAD,1)
        dk_ref[pl.ds(start,window)] += dk
        dv_ref[pl.ds(start,window)] += dv
    cos=cos_ref[...]; sin=sin_ref[...]
    for b in range(7):
        gq = parts[b].T*HEAD**-0.5
        dq_ref[:, b*LANES:(b+1)*LANES] = (gq*cos + half_turn(gq*sin,True)).astype(bf16)
    @pl.when(qb==nq-1)
    def _():
        own_ref[:, :KW] = dk_ref[2*rows:]; own_ref[:, KW:] = dv_ref[2*rows:]
        far1_ref[:, :KW] = dk_ref[rows:2*rows].astype(bf16); far1_ref[:, KW:] = dv_ref[rows:2*rows].astype(bf16)
        far2_ref[:, :KW] = dk_ref[:rows].astype(bf16); far2_ref[:, KW:] = dv_ref[:rows].astype(bf16)

def attend_back(m, base, rq, kvs, begins, out_set, rows_table, lse, middle, dy, gs, cos, sin, before):
    micros, rows, _ = rq.shape; nq=rows//BLOCK
    full=lambda shape: pl.BlockSpec(shape, lambda i: (0,)*len(shape))
    blk=lambda w: pl.BlockSpec((None,BLOCK,w), lambda i:(m,i,0))
    one=lambda h,w: pl.BlockSpec((None,h,w), lambda i:(m,0,0))
    sd=jax.ShapeDtypeStruct
    at=12+len(gs)
    return pl.pallas_call(
        functools.partial(attend_back_kernel,count=len(gs)), grid=(nq,),
        in_specs=[pl.BlockSpec(memory_space=pltpu.SMEM), blk(QW)]+[full((rows,2*KW))]*3+[pl.BlockSpec((None,1,BLOCK),lambda i:(m,0,i)), full((D,QW)), full((8,D)),
            pl.BlockSpec((None,1,16,BLOCK),lambda i:(m,i,0,0)), blk(D), blk(D)]+[blk(LANES)]*2+[pl.BlockSpec((BLOCK,D),lambda i:(i,0))]*len(gs)+[pl.BlockSpec(memory_space=pl.ANY)]*len(before),
        out_specs=[full((rows,2*KW)), full((rows,2*KW)), blk(D), blk(D), blk(QW), one(rows,2*KW), one(8,D)],
        out_shape=[sd((rows,2*KW),bf16), sd((rows,2*KW),bf16), sd((micros,rows,D),f32), sd((micros,rows,D),bf16), sd((micros,rows,QW),bf16), sd((micros,rows,2*KW),f32), sd((micros,8,D),f32)],
        scratch_shapes=[pltpu.VMEM((4,3*rows,LANES),bf16)]*2+[pltpu.VMEM((3*rows,LANES),f32)]*2,
        input_output_aliases={at+1+k:2+k for k in range(len(before))},
        compiler_params=pltpu.CompilerParams(vmem_limit_bytes=LIMIT), cost_estimate=COST,
        name="attend_back",
    )(base, rq, *kvs, begins, out_set, rows_table, lse, middle, dy, cos, sin, *gs, *before)

CHUNK=256

def feed_kernel(own_ref, *refs, parts, micro, kept):
    ts=refs[:parts]; gs=refs[parts:2*parts]; sets=refs[2*parts:2*parts+2]
    refs=refs[2*parts+2+kept:]
    backs=refs[:parts]; outs=refs[parts:2*parts]
    left_ref,pair_ref,act_ref,x_ref,y_ref,w_ref,own_buf,far_buf,w_sem,in_sem,out_sem=refs[2*parts:]
    i=pl.program_id(0)
    width=w_ref.shape[1]//3
    chunks=width//CHUNK
    def tokens(k):
        return (pltpu.make_async_copy(ts[k],x_ref.at[k],in_sem.at[0,k]),
                pltpu.make_async_copy(gs[k],y_ref.at[k],in_sem.at[1,k]))
    def columns(which,j,p):
        c=slice(p*width+j*CHUNK,p*width+(j+1)*CHUNK)
        return pltpu.make_async_copy(sets[which].at[:,c],w_ref.at[:,c],w_sem.at[p,j])
    def results(k):
        if k==0:
            return (pltpu.make_async_copy(own_buf.at[0],outs[0].at[micro],out_sem.at[0,0]),
                    pltpu.make_async_copy(own_buf.at[1],backs[0],out_sem.at[1,0]))
        return (pltpu.make_async_copy(far_buf.at[0,k-1],outs[k].at[micro],out_sem.at[0,k]),
                pltpu.make_async_copy(far_buf.at[1,k-1],backs[k],out_sem.at[1,k]))
    @pl.when(i==0)
    def _():
        for copy in tokens(0): copy.start()
        for which in range(2):
            @pl.when(own_ref[0]==1-which)
            def _(which=which):
                for j in range(chunks):
                    for p in range(3): columns(which,j,p).start()
        for k in range(1,parts):
            for copy in tokens(k): copy.start()
    for k in range(parts):
        @pl.when(i==k)
        def _(k=k):
            for copy in tokens(k): copy.wait()
    @pl.when(i==0)
    def _():
        for j in range(chunks):
            for p in range(3): columns(0,j,p).wait()
    x=x_ref[i]; y=y_ref[i]
    left_ref[0]=x.T; left_ref[1]=y.T
    for j in range(chunks):
        c=slice(j*CHUNK,(j+1)*CHUNK); c2=slice(width+j*CHUNK,width+(j+1)*CHUNK); c3=slice(2*width+j*CHUNK,2*width+(j+1)*CHUNK)
        g=dot(x,w_ref[:,c],1,0); u=dot(x,w_ref[:,c2],1,0); da=dot(y,w_ref[:,c3],1,0)
        s=jax.nn.sigmoid(g)
        gs_=g*s
        act_ref[:,c]=(gs_*u).astype(bf16)
        pair_ref[:,c]=(da*u*s*(1.0+g*(1.0-s))).astype(bf16)
        pair_ref[:,c2]=(da*gs_).astype(bf16)
    out=dot(act_ref[...],w_ref[:,2*width:],1,1)
    res=dot(pair_ref[...],w_ref[:,:2*width],1,1)
    for k in range(parts):
        @pl.when(i==k)
        def _(k=k):
            if k==0:
                own_buf[0]=out; own_buf[1]=res
            else:
                far_buf[0,k-1]=out.astype(bf16); far_buf[1,k-1]=res.astype(bf16)
            for copy in results(k): copy.start()
    @pl.when(i==parts-1)
    def _():
        for k in range(parts):
            for copy in results(k): copy.wait()

def feed(own, toks, grads, sets, micro, micros, before):
    parts=len(toks); rows=toks[0].shape[0]; hidden_pad=sets[0].shape[1]//3
    blk=lambda w: pl.BlockSpec((rows,w), lambda i:(micro*parts+i,0))
    sd=jax.ShapeDtypeStruct
    everything=rows*parts*micros
    kept=len(before)
    hold=pl.BlockSpec(memory_space=pl.ANY)
    shapes=[sd((rows,D),f32)]+[sd((rows,D),bf16)]*(parts-1)+[sd((micros,rows,D),f32)]+[sd((micros,rows,D),bf16)]*(parts-1)
    n_in=1+2*parts+2
    dma=pltpu.SemaphoreType.DMA
    out=pl.pallas_call(
        functools.partial(feed_kernel,parts=parts,micro=micro,kept=kept), grid=(parts,),
        in_specs=[pl.BlockSpec(memory_space=pltpu.SMEM)]+[hold]*(2*parts+2+kept),
        out_specs=[hold]*(2*parts)+[pl.BlockSpec((2,None,D,rows), lambda i:(0,micro*parts+i,0,0)),blk(2*hidden_pad),blk(hidden_pad)],
        out_shape=shapes+[sd((2,parts*micros,D,rows),bf16)]+[sd((everything,w),bf16) for w in (2*hidden_pad,hidden_pad)],
        scratch_shapes=[pltpu.VMEM((parts,rows,D),bf16)]*2+[pltpu.VMEM(sets[0].shape,bf16),pltpu.VMEM((2,rows,D),f32),pltpu.VMEM((2,parts-1,rows,D),bf16),
            dma((3,hidden_pad//CHUNK)),dma((2,parts)),dma((2,parts))],
        input_output_aliases={n_in+k:parts+k for k in range(kept)},
        compiler_params=pltpu.CompilerParams(vmem_limit_bytes=LIMIT), cost_estimate=COST,
        name="feed",
    )(own,*toks,*grads,*sets,*before)
    return out[:parts], out[parts:]

def finish_kernel(bit_ref, dq_ref, own_ref, cos_ref, sin_ref, wq_ref, wkv_ref, rows_ref, x_ref, n1_ref, dmid_ref, mixed_ref, dmb_ref, spread_ref, gain2_ref, *refs, near, block):
    far=refs[:-6]
    ig_ref, keep_ref, send_ref, acc_ref, small_ref, sum_ref = refs[-6:]
    i=pl.program_id(0)
    @pl.when(i==0)
    def _():
        acc_ref[...]=jnp.zeros_like(acc_ref)
        small_ref[...]=jnp.zeros_like(small_ref)
    for m in range(len(far)//near):
        @pl.when(i==m)
        def _(m=m):
            own=own_ref[...]
            for ref in far[m*near:(m+1)*near]:
                own=own+ref[...].astype(f32)
            sum_ref[...]=own
    own=sum_ref[...]
    k=own[:, :KW]
    cos=cos_ref[...]; sin=sin_ref[...]
    dk=(k*cos+half_turn(k*sin,True)).astype(bf16)
    dv=own[:, KW:].astype(bf16)
    dkv=jnp.concatenate([dk,dv],axis=1)
    dq=dq_ref[...]
    dn1=dot(dq,wq_ref[:, 2*KW:],1,1)+dot(dkv,wkv_ref[...],1,1)
    x=x_ref[...].astype(f32); inv=scaled(x)
    small_ref[0:1]+=jnp.sum(dn1*(x*inv),axis=0,keepdims=True)
    small_ref[1:2]+=gain2_ref[0:1]
    small_ref[2:3]+=jnp.sum(dq.astype(f32),axis=0,keepdims=True)
    small_ref[3:4,:2*KW]+=jnp.sum(dkv.astype(f32),axis=0,keepdims=True)
    w1=dn1*rows_ref[0:1]
    ig_ref[...]=dmid_ref[...]+inv*w1-x*(inv*inv*inv)*jnp.mean(w1*x,axis=-1,keepdims=True)
    n1=n1_ref[...]
    acc_ref[:, :QW]+=dot(mixed_ref[...],dmb_ref[...],0,0)
    acc_ref[:, QW:2*QW]+=dot(n1,dq,0,0)
    acc_ref[:, 2*QW:2*QW+2*KW]+=dot(n1,dkv,0,0)
    @pl.when(i==pl.num_programs(0)-1)
    def _():
        pair=jnp.concatenate([small_ref[3:4,:KW],small_ref[3:4,KW:2*KW],jnp.zeros((6,KW),f32)],axis=0).astype(bf16)
        table=jnp.concatenate([small_ref[0:3],dot(pair,spread_ref[...],1,1)[0:2],jnp.zeros((LANES-5,D),f32)],axis=0)
        acc_ref[:, 2*QW+2*KW:]=table.T
        if block:
            for j in range(D//block//2):
                at=pl.multiple_of((2*j+bit_ref[0])*block,16)
                keep_ref[j*block:(j+1)*block]=acc_ref[pl.ds(at,block)].astype(bf16)
                at=pl.multiple_of((2*j+1-bit_ref[0])*block,16)
                send_ref[j*block:(j+1)*block]=acc_ref[pl.ds(at,block)].astype(bf16)
        else:
            keep_ref[...]=acc_ref[:D//2].astype(bf16)
            send_ref[...]=acc_ref[D//2:].astype(bf16)

def finish(bit,dq,own,far,cos,sin,in_set,rows_table,x,n1,dmid,mixed,dmb,spread,gain2,block):
    m,rows,_=x.shape
    full=lambda shape,idx=(0,0): pl.BlockSpec(shape, lambda i: idx)
    blk=lambda w,h=rows: pl.BlockSpec((None,h,w), lambda i:(i,0,0))
    sd=jax.ShapeDtypeStruct
    width=2*QW+2*KW+LANES
    near=len(far[0])
    far=[f for pieces in far for f in pieces]
    return pl.pallas_call(
        functools.partial(finish_kernel,near=near,block=block), grid=(m,),
        in_specs=[pl.BlockSpec(memory_space=pltpu.SMEM),blk(QW),blk(2*KW),blk(LANES),blk(LANES),full((D,2*KW+QW)),full((D,2*KW)),full((8,D)),blk(D),blk(D),blk(D),blk(QW),blk(D),full((D,LANES)),blk(D,8)]+[full((rows,2*KW))]*len(far),
        out_specs=[blk(D),full((D//2,width)),full((D//2,width))],
        out_shape=[sd((m,rows,D),f32),sd((D//2,width),bf16),sd((D//2,width),bf16)],
        scratch_shapes=[pltpu.VMEM((D,width),f32),pltpu.VMEM((8,D),f32),pltpu.VMEM((rows,2*KW),f32)],
        compiler_params=pltpu.CompilerParams(vmem_limit_bytes=LIMIT), cost_estimate=COST,
        name="finish",
    )(bit,dq,own,cos,sin,in_set,in_set,rows_table,x,n1,dmid,mixed,dmb,spread,gain2,*far)

def weights_kernel(left_ref, right_ref, out_ref):
    left=jnp.concatenate([left_ref[k] for k in range(left_ref.shape[0])],axis=1)
    out_ref[...]=dot(left,right_ref[...],1,0).astype(bf16)

def weights(left,which,right,chunk):
    rows,width=right.shape
    return pl.pallas_call(
        weights_kernel, grid=(width//chunk,),
        in_specs=[pl.BlockSpec((None,)+left.shape[1:],lambda j:(which,0,0,0),pipeline_mode=pl.Buffered(1)),pl.BlockSpec((rows,chunk),lambda j:(0,j))],
        out_specs=pl.BlockSpec((D,chunk),lambda j:(0,j)), out_shape=jax.ShapeDtypeStruct((D,width),bf16),
        compiler_params=pltpu.CompilerParams(vmem_limit_bytes=LIMIT), cost_estimate=COST,
        name="weights",
    )(left,right)

def woven_kernel(core_ref, *refs):
    n=len(refs)//3
    mine=refs[:n]; got=refs[n:2*n]; outs=refs[2*n:]
    core=core_ref[0]; j=pl.program_id(0)
    for k in range(n):
        rows=mine[k].shape[0]
        outs[k][pl.ds(pl.multiple_of(core*rows,16),rows)]=mine[k][...]
        outs[k][pl.ds(pl.multiple_of((1-core)*rows,16),rows)]=got[k][...]

def woven(core, mine, got):
    n=len(mine); blocks,rows,_=mine[0].shape
    size=blocks.bit_length()-1
    def turned(j):
        return sum(((j>>k)&1)<<(size-1-k) for k in range(size))
    places=[lambda j:(j,0,0), lambda j:(turned(j),0,0)]
    shapes=[jax.ShapeDtypeStruct((2*blocks*rows,v.shape[2]),v.dtype) for v in mine]
    return pl.pallas_call(
        woven_kernel, grid=(blocks,), in_specs=[pl.BlockSpec(memory_space=pltpu.SMEM)]+[pl.BlockSpec((None,)+v.shape[1:],places[k%n]) for k,v in enumerate(mine+got)],
        out_specs=[pl.BlockSpec((2*rows,v.shape[2]),lambda j:(j,0)) for v in mine], out_shape=shapes,
        compiler_params=pltpu.CompilerParams(vmem_limit_bytes=LIMIT), cost_estimate=COST,
        name="woven",
    )(core,*mine,*got)


LONGEST = 512


def after(values_in, *needed):
    return lax.optimization_barrier((values_in, needed))[0]


theta = 10000.0


def body(
    layer_in,
    doc_ids,
    cotangent,
    first_gain,
    query_weight,
    query_bias,
    key_weight,
    key_bias,
    value_weight,
    value_bias,
    out_weight,
    second_gain,
    gate_weight,
    up_weight,
    down_weight,
):
    ctx = ("zh", "zb")
    dp = ("grp", "core")
    parts = lax.axis_size(ctx)
    rank = lax.axis_index(ctx)
    micros = layer_in.shape[1]
    shard_rows = layer_in.shape[3]
    hidden = gate_weight.shape[1]
    hidden_pad = -(-hidden // (2 * LANES)) * 2 * LANES
    weight_rows = query_weight.shape[0]
    bias_rows = key_bias.shape[0]
    reach_parts = -(-LONGEST // shard_rows)
    core = lax.axis_index("core")
    far_half = lax.axis_index("zh")

    group_rank = lax.axis_index(dp)
    groups = lax.axis_size(dp)
    bits = [1 << k for k in range(groups.bit_length() - 1)]
    block_rows = parts * weight_rows
    even = block_rows % 16 == 0

    def swapped(values_in, bit):
        return lax.ppermute(values_in, dp, [(s, s ^ bit) for s in range(groups)])

    def doubled(blocks, order, k):
        bit = order[k]
        got = swapped(blocks, bit)
        low = (group_rank // bit) % 2 == 0
        return jnp.stack([jnp.where(low, blocks, got), jnp.where(low, got, blocks)])

    def around(values_in, steps):
        return lax.ppermute(values_in, ctx, [(s, (s + steps) % parts) for s in range(parts)])

    def other(values_in, axis):
        return lax.ppermute(values_in, axis, [(0, 1), (1, 0)])

    def corner(values_in):
        return lax.ppermute(values_in, ("core", "zb"), [(s, 3 - s) for s in range(4)])

    def shared(values_in):
        beside = other(values_in, "zb")
        return [values_in, other(values_in, "core"), beside, other(beside, "core")]

    def collected(values_in):
        pieces = [values_in] + [around(values_in, d) for d in range(1, parts)]
        ordered = [pieces[d] for d in range(parts - 1, -1, -1)]
        ordered = jnp.stack(ordered + ordered[:-1])
        taken = lax.dynamic_slice_in_dim(ordered, parts - 1 - rank, parts, 0)
        return taken.reshape((-1,) + values_in.shape[1:])

    def column(values_in):
        return jnp.pad(values_in, (0, weight_rows - values_in.shape[0]))[:, None]

    def wide(values_in):
        return jnp.pad(values_in, ((0, 0), (0, hidden_pad - hidden)))

    own_block = jnp.concatenate([wide(gate_weight), wide(up_weight), wide(down_weight.T)], axis=1)
    own_set = lax.all_gather(own_block, dp, axis=0, tiled=True)
    small = jnp.concatenate(
        [column(v) for v in (first_gain, second_gain, query_bias, key_bias, value_bias)], axis=1
    )
    small = jnp.pad(small, ((0, 0), (0, LANES - small.shape[1])))
    own_attention = jnp.concatenate(
        [out_weight, small, key_weight, value_weight, query_weight], axis=1
    )
    first_block = collected(own_attention)
    row = jnp.arange(D, dtype=jnp.int32)[:, None]
    place = row // weight_rows * bias_rows + row % weight_rows
    spread = (
        (place == jnp.arange(LANES, dtype=jnp.int32)[None, :]) & (row % weight_rows < bias_rows)
    ).astype(bf16)

    docs = doc_ids[0, :, 0]
    own_docs = lax.dynamic_slice_in_dim(docs, rank * shard_rows, shard_rows, 1)
    begins = jnp.sum((docs[:, None, :] < own_docs[:, :, None]).astype(jnp.int32), axis=2)
    row_index = rank * shard_rows + jnp.arange(shard_rows, dtype=jnp.int32)
    positions = row_index[None, :] - begins
    frequency = jnp.power(f32(theta), -(jnp.arange(HEAD // 2, dtype=f32) * (2.0 / HEAD)))
    angle = positions.astype(f32)[:, :, None] * frequency
    cosines, sines = jnp.cos(angle), jnp.sin(angle)
    cosines = jnp.concatenate([cosines] * (2 * LANES // HEAD), axis=2)
    sines = jnp.concatenate([-sines, sines] * (LANES // HEAD), axis=2)
    base = (rank * shard_rows).reshape(1)

    own_block, first_block = after((own_block, first_block))
    cut = QW + LANES
    firsts = [first_block[:, :cut], first_block[:, cut:]]
    gather_orders = [bits[1:] + bits[:1], bits[:0:-1] + bits[:1]]
    widths = own_block.shape[1] // LANES // 4 * LANES
    edges = [0, widths, own_block.shape[1] - widths, own_block.shape[1]]
    other_block = []
    upstream = [cotangent[0, m, 0] for m in range(micros)]
    crossed = []
    for k in range(len(bits)):
        if k < len(bits) - 1 or not even:
            firsts = [doubled(side, order, k) for side, order in zip(firsts, gather_orders)]
        else:
            gots = [swapped(side, 1) for side in firsts]
            firsts = [firsts, gots]
        if k < 3:
            other_block.append(other(own_block[:, edges[k] : edges[k + 1]], "zh"))
        if k == 1:
            crossed.append(other(upstream[0], "zb"))
        firsts, other_block, own_block, spread, cosines, sines, begins, upstream, crossed = after(
            (firsts, other_block, own_block, spread, cosines, sines, begins, upstream, crossed)
        )
    other_set = lax.all_gather(jnp.concatenate(other_block, axis=1), dp, axis=0, tiled=True)
    if even:
        firsts, gots = ([v.reshape((-1,) + v.shape[-2:]) for v in part] for part in firsts)
        out_set, in_set = woven(core.reshape(1), firsts, gots)
    else:
        out_set, in_set = (
            jnp.transpose(
                side, [list(reversed(order)).index(bit) for bit in reversed(bits)] + [-2, -1]
            ).reshape(-1, side.shape[-1])
            for side, order in zip(firsts, gather_orders)
        )
    sets = (own_set, other_set)
    own_quarter = (core == far_half).astype(jnp.int32).reshape(1)

    tokens = layer_in[0, :, 0]
    rot_query, pairs, normed_one, rows_table = project(
        tokens, out_set, in_set, spread, cosines, sines
    )
    def earlier(pair):
        return [pair] + [
            lax.ppermute(pair, ctx, [(s, s + d) for s in range(parts - d)])
            for d in range(1, reach_parts + 1)
        ]

    kvs = [earlier(pairs[0])]
    rot_query, pairs[1:] = after((rot_query, pairs[1:]))
    kvs += [earlier(pair) for pair in pairs[1:]]

    begins = begins[:, None, :]
    exchanged = []
    held = ()
    for m in range(micros):
        normed_two, *held = attend(
            m, base, rot_query, kvs[m], begins, out_set, tokens, rows_table, held
        )
        if m == 0:
            upstream, crossed, normed_two, kvs[1:] = after((upstream, crossed, normed_two, kvs[1:]))
        exchanged.append([normed_two, other(normed_two, "core"), other(normed_two, "zb")])
        if m == 0:
            crossed += [other(u, "zb") for u in upstream[1:]]
            upstream_pieces = [[u, other(u, "core"), v] for u, v in zip(upstream, crossed)]
    exchanged[-1].append(corner(normed_two))
    exchanged[:-1], upstream_pieces[0], exchanged[-1][0] = after(
        (exchanged[:-1], upstream_pieces[0], normed_two)
    )
    for early in exchanged[:-1] + upstream_pieces[:1]:
        early.append(other(early[2], "core"))
    mixed, middle, log_sums = held

    backs = []
    before = ()
    for m in range(micros):
        back, before = feed(
            own_quarter, exchanged[m], upstream_pieces[m], sets, m, micros, before
        )
        if m < micros - 1:
            back, upstream_pieces[m + 1] = after((back, upstream_pieces[m + 1]))
            upstream_pieces[m + 1].append(other(upstream_pieces[m + 1][2], "core"))
        backs.append([back[0], other(back[1], "core"), other(back[2], "zb"), corner(back[3])])
    partials = before[:4]
    out_near = other(partials[1], "core")
    out_far = other(partials[3], "core")

    left, pair, act = after(before[4:], backs[0])
    feed_down = weights(left, 1, act, 256)
    backs[-1][1:3], left, pair, feed_down = after((backs[-1][1:3], left, pair, feed_down))
    feed_pair = weights(left, 0, pair, 512)
    backs, feed_pair, out_near, out_far = after((backs, feed_pair, out_near, out_far))
    feed_down = lax.psum_scatter(feed_down, "grp", scatter_dimension=0, tiled=True)
    feed_pair = lax.psum_scatter(feed_pair, "grp", scatter_dimension=0, tiled=True)

    far = []
    ended = ()
    out_beside = []
    for m in range(micros):
        out_sum = (partials[2][m].astype(f32) + out_far[m].astype(f32)).astype(bf16)
        out_beside.append(other(out_sum, "zb"))
        far1, far2, *ended = attend_back(
            m, base, rot_query, kvs[m], begins, out_set, rows_table, log_sums, middle, cotangent[0, :, 0],
            backs[m], cosines, sines, ended,
        )
        far1, far2, ended, out_beside = after((far1, far2, ended, out_beside))
        far.append(
            [
                lax.ppermute(part, ctx, [(s, s - d) for s in range(d, parts)])
                for d, part in ((1, far1), (2, far2))
            ]
        )
        if m < micros - 1:
            out_far, ended = after((out_far, ended))
    def delivered(half, k):
        part = lax.dynamic_index_in_dim(
            half.reshape((2, -1) + half.shape[1:]), (core + far_half + k) % 2, 0, keepdims=False
        )
        return lax.ppermute(
            part, ("core", "zh"), [(2 * s + a, 2 * (s ^ a ^ k) + s) for s in range(2) for a in range(2)]
        )

    far, feed_down = after((far, feed_down))
    down_parts = [delivered(feed_down, k) for k in range(2)]
    grad_middle, branch_low, query_grad, own_pair, gain_sum = ended
    input_grad, keep, send = finish(
        (group_rank % 2).reshape(1), query_grad, own_pair, far, cosines, sines, in_set,
        rows_table, tokens, normed_one, grad_middle, mixed, branch_low, spread, gain_sum,
        block_rows if even else 0,
    )
    keep, send, down_parts = after((keep, send, down_parts))
    if not even:
        both = jnp.concatenate([keep, send]).reshape(groups // 2, 2, block_rows, -1)
        keep, send = (
            lax.dynamic_index_in_dim(both, v, 1, keepdims=False)
            for v in (group_rank % 2, 1 - group_rank % 2)
        )

    def halved(blocks, order, k):
        bit = order[k]
        size = blocks.shape[0]
        at = sorted(order[k:]).index(bit)
        view = blocks.reshape((size >> (at + 1), 2, 1 << at) + blocks.shape[1:])
        own = (group_rank // bit) % 2
        kept = lax.dynamic_index_in_dim(view, own, 1, keepdims=False)
        sent = lax.dynamic_index_in_dim(view, 1 - own, 1, keepdims=False)
        got = swapped(sent.astype(bf16), bit)
        return (kept.astype(f32) + got.astype(f32)).reshape((size // 2,) + blocks.shape[1:])

    blocks = keep.astype(f32) + swapped(send, 1).astype(f32)
    blocks = blocks.reshape(groups // 2, block_rows, -1)
    cut = QW + 2 * LANES
    sides = [blocks[:, :, :cut], blocks[:, :, cut:]]
    orders = [bits[1:], bits[:0:-1]]
    pair_parts = [delivered(feed_pair, 0)]
    for k in range(len(bits) - 1):
        sides = [halved(side, order, k) for side, order in zip(sides, orders)]
        if k == len(bits) - 3:
            sides, pair_parts, feed_pair = after((sides, pair_parts, feed_pair))
            pair_parts.append(delivered(feed_pair, 1))
    sides, down_parts = after((sides, down_parts))
    attention_block = jnp.concatenate([side[0] for side in sides], axis=1).astype(bf16)
    attention_block = attention_block.reshape(parts, weight_rows, -1)

    def block_for(steps):
        return lax.dynamic_index_in_dim(
            attention_block, (rank + steps) % parts, 0, keepdims=False
        )

    ends = [around(block_for(d), d) for d in range(1, parts)]
    ends, pair_parts = after((ends, pair_parts))
    sums = block_for(0).astype(f32)
    for end in ends:
        sums = sums + end.astype(f32)

    pair_sum = pair_parts[0].astype(f32) + pair_parts[1].astype(f32)
    down_sum = down_parts[0].astype(f32) + down_parts[1].astype(f32)

    total = middle + partials[0] + out_near.astype(f32) + jnp.stack(out_beside).astype(f32)

    edge = 2 * QW + 2 * KW
    return (
        total.astype(bf16)[None, :, None],
        input_grad[None, :, None],
        sums[:, edge],
        sums[:, QW : 2 * QW],
        sums[:, edge + 2],
        sums[:, 2 * QW : 2 * QW + KW],
        sums[:bias_rows, edge + 3],
        sums[:, 2 * QW + KW : edge],
        sums[:bias_rows, edge + 4],
        sums[:, :QW],
        sums[:, edge + 1],
        pair_sum[:, :hidden],
        pair_sum[:, hidden_pad : hidden_pad + hidden],
        down_sum[:, :hidden].T,
    )


def solution(mesh):
    groups, parts = mesh.devices.shape
    split = jax.sharding.Mesh(
        mesh.devices.reshape(groups // 2, 2, parts // 2, 2), ("grp", "core", "zh", "zb")
    )
    dp = ("grp", "core")
    ctx = ("zh", "zb")
    rows = P(dp + ctx, None)
    line = P(dp + ctx)
    tokens = P(dp, None, None, ctx, None)
    up = P(dp, ctx)
    return jax.shard_map(
        body,
        mesh=split,
        in_specs=(
            tokens, P(dp, None, None, None), tokens, line, rows, line, rows, line, rows, line,
            rows, line, up, up, P(ctx, dp),
        ),
        out_specs=(
            tokens, tokens, line, rows, line, rows, line, rows, line, rows, line,
            up, up, P(ctx, dp),
        ),
        check_vma=False,
    )
```

```python
import functools
import jax, jax.numpy as jnp
from jax import lax
from jax.sharding import PartitionSpec as P
from jax.experimental import pallas as pl
from jax.experimental.pallas import tpu as pltpu
D=896; HEADS=14; KV_HEADS=2; HEAD=64; LANES=128
QW=896; KW=128
epsilon=1e-6
bf16=jnp.bfloat16; f32=jnp.float32
LIMIT=56*1024*1024
COST=pl.CostEstimate(flops=1, bytes_accessed=1, transcendentals=0)

def dot(left, right, left_dim, right_dim):
    return lax.dot_general(left, right, (((left_dim,), (right_dim,)), ((), ())), preferred_element_type=f32)

def half_turn(v, back):
    lane = lax.broadcasted_iota(jnp.int32, v.shape, 1) & (HEAD-1)
    width=v.shape[1]
    up = pltpu.roll(v, width-HEAD//2, 1)
    down = pltpu.roll(v, HEAD//2, 1)
    return jnp.where(lane < HEAD//2, up, down)

def scaled(v):
    return lax.rsqrt(jnp.mean(v*v, axis=-1, keepdims=True)+epsilon)

def pairs_kernel(x_ref, wkv_ref, ws_ref, spread_ref, cos_ref, sin_ref, n1_ref, rows_ref, *refs):
    kv_refs=refs[:-1]; bias_ref=refs[-1]
    @pl.when(pl.program_id(0)==0)
    def _():
        table = ws_ref[...].astype(f32).T[:8]
        rows_ref[...] = table
        close = dot(table.astype(bf16), spread_ref[...],1,0)
        bias_ref[:, :KW] = close[3:4]
        bias_ref[:, KW:] = close[4:5]
    x = x_ref[...].astype(f32)
    n1 = (x*scaled(x)*rows_ref[0:1]).astype(bf16)
    n1_ref[...] = n1
    kv = dot(n1, wkv_ref[...],1,0) + bias_ref[...]
    v = kv[:, :KW]
    pair = jnp.concatenate([v*cos_ref[...] + half_turn(v,False)*sin_ref[...], kv[:, KW:]],axis=1).astype(bf16)
    for m,kv_ref in enumerate(kv_refs):
        @pl.when(pl.program_id(0)==m)
        def _(kv_ref=kv_ref): kv_ref[...] = pair

def queries_kernel(n1_ref, wq_ref, rows_ref, cos_ref, sin_ref, rq_ref):
    q = dot(n1_ref[...], wq_ref[:, 2*KW:],1,0) + rows_ref[2:3]
    cos = cos_ref[...]; sin = sin_ref[...]
    for b in range(QW//LANES):
        v = q[:, b*LANES:(b+1)*LANES]
        r = (v*cos + half_turn(v,False)*sin).astype(bf16)
        rq_ref[:, b*LANES:(b+1)*LANES] = (r.astype(f32)*HEAD**-0.5).astype(bf16)

def project(x, out_set, in_set, spread, cos, sin):
    m, rows, _ = x.shape
    full=lambda shape,idx: pl.BlockSpec(shape, lambda i: idx)
    blk=lambda w: pl.BlockSpec((None,rows,w), lambda i:(i,0,0))
    sd=jax.ShapeDtypeStruct
    params=dict(compiler_params=pltpu.CompilerParams(vmem_limit_bytes=LIMIT), cost_estimate=COST)
    n1, table, *pair = pl.pallas_call(
        pairs_kernel, grid=(m,),
        in_specs=[blk(D), full((D,2*KW),(0,0)), full((D,LANES),(0,QW//LANES)), full((D,LANES),(0,0)), blk(LANES), blk(LANES)],
        out_specs=[blk(D), full((8,D),(0,0))]+[full((rows,2*KW),(0,0))]*m,
        out_shape=[sd((m,rows,D),bf16), sd((8,D),f32)]+[sd((rows,2*KW),bf16)]*m,
        scratch_shapes=[pltpu.VMEM((1,2*KW),f32)],
        name="pairs", **params,
    )(x, in_set, out_set, spread, cos, sin)
    rq = pl.pallas_call(
        queries_kernel, grid=(m,),
        in_specs=[blk(D), full((D,2*KW+QW),(0,0)), full((8,D),(0,0)), blk(LANES), blk(LANES)],
        out_specs=blk(QW), out_shape=sd((m,rows,QW),bf16),
        name="queries", **params,
    )(n1, in_set, table, cos, sin)
    return rq, pair, n1, table

BLOCK=128
def units():
    group=HEADS//KV_HEADS
    out=[]
    for g in range(KV_HEADS):
        for parity in range(2):
            blocks=[h//2 for h in range(g*group,(g+1)*group) if h%2==parity]
            out.append((g,parity,blocks))
    return out

def padded(v, g, parity, lane):
    if g != parity:
        v = pltpu.roll(v.astype(f32), HEAD, 1).astype(bf16)
    keep = (lane >= HEAD) if parity else (lane < HEAD)
    return jnp.where(keep, v, jnp.zeros_like(v))

def mask_bias(begins, rank_base, q0, window, reach):
    key = lax.broadcasted_iota(jnp.int32,(window,BLOCK),0) + (rank_base + q0 - reach)
    query = lax.broadcasted_iota(jnp.int32,(window,BLOCK),1) + (rank_base + q0)
    ok = (key >= begins) & (key <= query)
    return jnp.where(ok, 0.0, -1e30).astype(f32)

def fill_padded(kv_refs, k_ref, v_ref):
    rows = kv_refs[0].shape[0]
    lane = lax.broadcasted_iota(jnp.int32,(rows,LANES),1)
    for p,ref in enumerate(kv_refs):
        kv=ref[...]
        for g,parity,_ in units():
            u=2*g+parity
            k_ref[u, p*rows:(p+1)*rows] = padded(kv[:, :KW], g, parity, lane)
            v_ref[u, p*rows:(p+1)*rows] = padded(kv[:, KW:], g, parity, lane)

def attend_kernel(base_ref, rq_ref, kv0_ref, kv1_ref, kv2_ref, begin_ref, wo_ref, x_ref, rows_ref, *refs):
    n2_ref, mixed_ref, middle_ref, lse_ref, k_ref, v_ref = refs[-6:]
    qb = pl.program_id(0)
    rows = kv0_ref.shape[0]
    reach=512; window=reach+BLOCK
    @pl.when(qb==0)
    def _():
        fill_padded((kv2_ref,kv1_ref,kv0_ref), k_ref, v_ref)
    q0 = qb*BLOCK
    bias = mask_bias(begin_ref[...], base_ref[0], q0, window, reach)
    parts=[None]*7
    start = pl.multiple_of(q0 + (2*rows - reach), BLOCK)
    for g,parity,blocks in units():
        u=2*g+parity
        qs = jnp.concatenate([rq_ref[:, b*LANES:(b+1)*LANES] for b in blocks], axis=0)
        keys = k_ref[u, pl.ds(start,window)]
        vals = v_ref[u, pl.ds(start,window)]
        s = dot(keys, qs, 1, 1) + jnp.concatenate([bias]*len(blocks),axis=1)
        top = jnp.max(s, axis=0, keepdims=True)
        e = jnp.exp(s-top)
        total = jnp.sum(e, axis=0, keepdims=True)
        p = (e*(1.0/total)).astype(bf16)
        o = dot(vals, p, 0, 0)
        lse = top+jnp.log(total)
        for i,b in enumerate(blocks):
            piece=o[:, i*BLOCK:(i+1)*BLOCK]
            parts[b] = piece if parts[b] is None else parts[b]+piece
            lse_ref[0, 2*b+parity:2*b+parity+1, :] = lse[:, i*BLOCK:(i+1)*BLOCK]
    for b in range(7):
        mixed_ref[:, b*LANES:(b+1)*LANES] = parts[b].T.astype(bf16)
    middle = x_ref[...].astype(f32) + dot(mixed_ref[...], wo_ref[...],1,0)
    middle_ref[...] = middle
    n2_ref[...] = (middle*scaled(middle)*rows_ref[1:2]).astype(bf16)

def attend(m, base, rq, kvs, begins, out_set, x, rows_table, before):
    micros, rows, _ = rq.shape; nq=rows//BLOCK
    full=lambda shape: pl.BlockSpec(shape, lambda i: (0,)*len(shape))
    blk=lambda w: pl.BlockSpec((None,BLOCK,w), lambda i:(m,i,0))
    sd=jax.ShapeDtypeStruct
    return pl.pallas_call(
        attend_kernel, grid=(nq,),
        in_specs=[pl.BlockSpec(memory_space=pltpu.SMEM), blk(QW)]+[full((rows,2*KW))]*3+[pl.BlockSpec((None,1,BLOCK),lambda i:(m,0,i)), full((D,QW)), blk(D), full((8,D))]+[pl.BlockSpec(memory_space=pl.ANY)]*len(before),
        out_specs=[pl.BlockSpec((BLOCK,D),lambda i:(i,0)), blk(QW), blk(D), pl.BlockSpec((None,1,16,BLOCK),lambda i:(m,i,0,0))],
        out_shape=[sd((rows,D),bf16), sd((micros,rows,QW),bf16), sd((micros,rows,D),f32), sd((micros,nq,16,BLOCK),f32)],
        scratch_shapes=[pltpu.VMEM((4,3*rows,LANES),bf16), pltpu.VMEM((4,3*rows,LANES),bf16)],
        input_output_aliases={9+k:1+k for k in range(len(before))},
        compiler_params=pltpu.CompilerParams(vmem_limit_bytes=LIMIT), cost_estimate=COST,
        name="attend",
    )(base, rq, *kvs, begins, out_set, x, rows_table, *before)

def attend_back_kernel(base_ref, rq_ref, kv0_ref, kv1_ref, kv2_ref, begin_ref, wo_ref, rows_ref, lse_ref, middle_ref, dy_ref, cos_ref, sin_ref, *refs, count):
    gs=refs[:count]
    far1_ref, far2_ref, dmid_ref, dmb_ref, dq_ref, own_ref, gain_ref, k_ref, v_ref, dk_ref, dv_ref = refs[-11:]
    qb = pl.program_id(0); nq=pl.num_programs(0)
    rows = kv0_ref.shape[0]
    reach=512; window=reach+BLOCK
    @pl.when(qb==0)
    def _():
        fill_padded((kv2_ref,kv1_ref,kv0_ref), k_ref, v_ref)
        dk_ref[...] = jnp.zeros_like(dk_ref)
        dv_ref[...] = jnp.zeros_like(dv_ref)
        gain_ref[...] = jnp.zeros_like(gain_ref)
    dn2 = gs[0][...].astype(f32)
    for g_ref in gs[1:]:
        dn2 = dn2+g_ref[...].astype(f32)
    middle = middle_ref[...]
    inv = scaled(middle)
    gain_ref[...] += jnp.broadcast_to(jnp.sum(dn2*(middle*inv),axis=0,keepdims=True), gain_ref.shape)
    w2 = dn2*rows_ref[1:2]
    dmid = dy_ref[...].astype(f32) + inv*w2 - middle*(inv*inv*inv)*jnp.mean(w2*middle,axis=-1,keepdims=True)
    dmid_ref[...] = dmid
    dmb = dmid.astype(bf16)
    dmb_ref[...] = dmb
    dmixed = dot(dmb, wo_ref[...],1,1).astype(bf16)
    q0 = qb*BLOCK
    bias = mask_bias(begin_ref[...], base_ref[0], q0, window, reach)
    start = pl.multiple_of(q0 + (2*rows - reach), BLOCK)
    parts=[None]*7
    for g,parity,blocks in units():
        u=2*g+parity
        n=len(blocks)
        qs = jnp.concatenate([rq_ref[:, b*LANES:(b+1)*LANES] for b in blocks], axis=0)
        ds_ = jnp.concatenate([dmixed[:, b*LANES:(b+1)*LANES] for b in blocks], axis=0)
        keys = k_ref[u, pl.ds(start,window)]
        vals = v_ref[u, pl.ds(start,window)]
        lse = jnp.concatenate([lse_ref[0, 2*b+parity:2*b+parity+1, :] for b in blocks],axis=1)
        p = jnp.exp(dot(keys,qs,1,1) + jnp.concatenate([bias]*n,axis=1) - lse)
        dp = dot(vals, ds_, 1, 1)
        t = p*dp
        ds = (t-p*jnp.sum(t,axis=0,keepdims=True)).astype(bf16)
        pb = p.astype(bf16)
        o = dot(keys, ds, 0, 0)
        for i,b in enumerate(blocks):
            piece=o[:, i*BLOCK:(i+1)*BLOCK]
            parts[b] = piece if parts[b] is None else parts[b]+piece
        dk = dot(ds, qs, 1, 0); dv = dot(pb, ds_, 1, 0)
        keep = lax.broadcasted_iota(jnp.int32,(window,LANES),1)
        keep = (keep>=HEAD) if parity else (keep<HEAD)
        dk = jnp.where(keep, dk, 0.0); dv=jnp.where(keep,dv,0.0)
        if g!=parity:
            dk = pltpu.roll(dk,HEAD,1); dv=pltpu.roll(dv,HEAD,1)
        dk_ref[pl.ds(start,window)] += dk
        dv_ref[pl.ds(start,window)] += dv
    cos=cos_ref[...]; sin=sin_ref[...]
    for b in range(7):
        gq = parts[b].T*HEAD**-0.5
        dq_ref[:, b*LANES:(b+1)*LANES] = (gq*cos + half_turn(gq*sin,True)).astype(bf16)
    @pl.when(qb==nq-1)
    def _():
        own_ref[:, :KW] = dk_ref[2*rows:]; own_ref[:, KW:] = dv_ref[2*rows:]
        far1_ref[:, :KW] = dk_ref[rows:2*rows].astype(bf16); far1_ref[:, KW:] = dv_ref[rows:2*rows].astype(bf16)
        far2_ref[:, :KW] = dk_ref[:rows].astype(bf16); far2_ref[:, KW:] = dv_ref[:rows].astype(bf16)

def attend_back(m, base, rq, kvs, begins, out_set, rows_table, lse, middle, dy, gs, cos, sin, before):
    micros, rows, _ = rq.shape; nq=rows//BLOCK
    full=lambda shape: pl.BlockSpec(shape, lambda i: (0,)*len(shape))
    blk=lambda w: pl.BlockSpec((None,BLOCK,w), lambda i:(m,i,0))
    one=lambda h,w: pl.BlockSpec((None,h,w), lambda i:(m,0,0))
    sd=jax.ShapeDtypeStruct
    at=12+len(gs)
    return pl.pallas_call(
        functools.partial(attend_back_kernel,count=len(gs)), grid=(nq,),
        in_specs=[pl.BlockSpec(memory_space=pltpu.SMEM), blk(QW)]+[full((rows,2*KW))]*3+[pl.BlockSpec((None,1,BLOCK),lambda i:(m,0,i)), full((D,QW)), full((8,D)),
            pl.BlockSpec((None,1,16,BLOCK),lambda i:(m,i,0,0)), blk(D), blk(D)]+[blk(LANES)]*2+[pl.BlockSpec((BLOCK,D),lambda i:(i,0))]*len(gs)+[pl.BlockSpec(memory_space=pl.ANY)]*len(before),
        out_specs=[full((rows,2*KW)), full((rows,2*KW)), blk(D), blk(D), blk(QW), one(rows,2*KW), one(8,D)],
        out_shape=[sd((rows,2*KW),bf16), sd((rows,2*KW),bf16), sd((micros,rows,D),f32), sd((micros,rows,D),bf16), sd((micros,rows,QW),bf16), sd((micros,rows,2*KW),f32), sd((micros,8,D),f32)],
        scratch_shapes=[pltpu.VMEM((4,3*rows,LANES),bf16)]*2+[pltpu.VMEM((3*rows,LANES),f32)]*2,
        input_output_aliases={at+1+k:2+k for k in range(len(before))},
        compiler_params=pltpu.CompilerParams(vmem_limit_bytes=LIMIT), cost_estimate=COST,
        name="attend_back",
    )(base, rq, *kvs, begins, out_set, rows_table, lse, middle, dy, cos, sin, *gs, *before)

CHUNK=256

def feed_kernel(own_ref, *refs, parts, micro, kept):
    ts=refs[:parts]; gs=refs[parts:2*parts]; sets=refs[2*parts:2*parts+2]
    refs=refs[2*parts+2+kept:]
    backs=refs[:parts]; outs=refs[parts:2*parts]
    left_ref,pair_ref,act_ref,x_ref,y_ref,w_ref,own_buf,far_buf,w_sem,in_sem,out_sem=refs[2*parts:]
    i=pl.program_id(0)
    width=w_ref.shape[1]//3
    chunks=width//CHUNK
    def tokens(k):
        return (pltpu.make_async_copy(ts[k],x_ref.at[k],in_sem.at[0,k]),
                pltpu.make_async_copy(gs[k],y_ref.at[k],in_sem.at[1,k]))
    def columns(which,j,p):
        c=slice(p*width+j*CHUNK,p*width+(j+1)*CHUNK)
        return pltpu.make_async_copy(sets[which].at[:,c],w_ref.at[:,c],w_sem.at[p,j])
    def results(k):
        if k==0:
            return (pltpu.make_async_copy(own_buf.at[0],outs[0].at[micro],out_sem.at[0,0]),
                    pltpu.make_async_copy(own_buf.at[1],backs[0],out_sem.at[1,0]))
        return (pltpu.make_async_copy(far_buf.at[0,k-1],outs[k].at[micro],out_sem.at[0,k]),
                pltpu.make_async_copy(far_buf.at[1,k-1],backs[k],out_sem.at[1,k]))
    @pl.when(i==0)
    def _():
        for copy in tokens(0): copy.start()
        for which in range(2):
            @pl.when(own_ref[0]==1-which)
            def _(which=which):
                for j in range(chunks):
                    for p in range(3): columns(which,j,p).start()
        for k in range(1,parts):
            for copy in tokens(k): copy.start()
    for k in range(parts):
        @pl.when(i==k)
        def _(k=k):
            for copy in tokens(k): copy.wait()
    @pl.when(i==0)
    def _():
        for j in range(chunks):
            for p in range(3): columns(0,j,p).wait()
    x=x_ref[i]; y=y_ref[i]
    left_ref[0]=x.T; left_ref[1]=y.T
    for j in range(chunks):
        c=slice(j*CHUNK,(j+1)*CHUNK); c2=slice(width+j*CHUNK,width+(j+1)*CHUNK); c3=slice(2*width+j*CHUNK,2*width+(j+1)*CHUNK)
        g=dot(x,w_ref[:,c],1,0); u=dot(x,w_ref[:,c2],1,0); da=dot(y,w_ref[:,c3],1,0)
        s=jax.nn.sigmoid(g)
        gs_=g*s
        act_ref[:,c]=(gs_*u).astype(bf16)
        pair_ref[:,c]=(da*u*s*(1.0+g*(1.0-s))).astype(bf16)
        pair_ref[:,c2]=(da*gs_).astype(bf16)
    out=dot(act_ref[...],w_ref[:,2*width:],1,1)
    res=dot(pair_ref[...],w_ref[:,:2*width],1,1)
    for k in range(parts):
        @pl.when(i==k)
        def _(k=k):
            if k==0:
                own_buf[0]=out; own_buf[1]=res
            else:
                far_buf[0,k-1]=out.astype(bf16); far_buf[1,k-1]=res.astype(bf16)
            for copy in results(k): copy.start()
    @pl.when(i==parts-1)
    def _():
        for k in range(parts):
            for copy in results(k): copy.wait()

def feed(own, toks, grads, sets, micro, micros, before):
    parts=len(toks); rows=toks[0].shape[0]; hidden_pad=sets[0].shape[1]//3
    blk=lambda w: pl.BlockSpec((rows,w), lambda i:(micro*parts+i,0))
    sd=jax.ShapeDtypeStruct
    everything=rows*parts*micros
    kept=len(before)
    hold=pl.BlockSpec(memory_space=pl.ANY)
    shapes=[sd((rows,D),f32)]+[sd((rows,D),bf16)]*(parts-1)+[sd((micros,rows,D),f32)]+[sd((micros,rows,D),bf16)]*(parts-1)
    n_in=1+2*parts+2
    dma=pltpu.SemaphoreType.DMA
    out=pl.pallas_call(
        functools.partial(feed_kernel,parts=parts,micro=micro,kept=kept), grid=(parts,),
        in_specs=[pl.BlockSpec(memory_space=pltpu.SMEM)]+[hold]*(2*parts+2+kept),
        out_specs=[hold]*(2*parts)+[pl.BlockSpec((2,None,D,rows), lambda i:(0,micro*parts+i,0,0)),blk(2*hidden_pad),blk(hidden_pad)],
        out_shape=shapes+[sd((2,parts*micros,D,rows),bf16)]+[sd((everything,w),bf16) for w in (2*hidden_pad,hidden_pad)],
        scratch_shapes=[pltpu.VMEM((parts,rows,D),bf16)]*2+[pltpu.VMEM(sets[0].shape,bf16),pltpu.VMEM((2,rows,D),f32),pltpu.VMEM((2,parts-1,rows,D),bf16),
            dma((3,hidden_pad//CHUNK)),dma((2,parts)),dma((2,parts))],
        input_output_aliases={n_in+k:parts+k for k in range(kept)},
        compiler_params=pltpu.CompilerParams(vmem_limit_bytes=LIMIT), cost_estimate=COST,
        name="feed",
    )(own,*toks,*grads,*sets,*before)
    return out[:parts], out[parts:]

def finish_kernel(bit_ref, dq_ref, own_ref, cos_ref, sin_ref, wq_ref, wkv_ref, rows_ref, x_ref, n1_ref, dmid_ref, mixed_ref, dmb_ref, spread_ref, gain2_ref, *refs, near, block):
    far=refs[:-6]
    ig_ref, keep_ref, send_ref, acc_ref, small_ref, sum_ref = refs[-6:]
    i=pl.program_id(0)
    @pl.when(i==0)
    def _():
        acc_ref[...]=jnp.zeros_like(acc_ref)
        small_ref[...]=jnp.zeros_like(small_ref)
    for m in range(len(far)//near):
        @pl.when(i==m)
        def _(m=m):
            own=own_ref[...]
            for ref in far[m*near:(m+1)*near]:
                own=own+ref[...].astype(f32)
            sum_ref[...]=own
    own=sum_ref[...]
    k=own[:, :KW]
    cos=cos_ref[...]; sin=sin_ref[...]
    dk=(k*cos+half_turn(k*sin,True)).astype(bf16)
    dv=own[:, KW:].astype(bf16)
    dkv=jnp.concatenate([dk,dv],axis=1)
    dq=dq_ref[...]
    dn1=dot(dq,wq_ref[:, 2*KW:],1,1)+dot(dkv,wkv_ref[...],1,1)
    x=x_ref[...].astype(f32); inv=scaled(x)
    small_ref[0:1]+=jnp.sum(dn1*(x*inv),axis=0,keepdims=True)
    small_ref[1:2]+=gain2_ref[0:1]
    small_ref[2:3]+=jnp.sum(dq.astype(f32),axis=0,keepdims=True)
    small_ref[3:4,:2*KW]+=jnp.sum(dkv.astype(f32),axis=0,keepdims=True)
    w1=dn1*rows_ref[0:1]
    ig_ref[...]=dmid_ref[...]+inv*w1-x*(inv*inv*inv)*jnp.mean(w1*x,axis=-1,keepdims=True)
    n1=n1_ref[...]
    acc_ref[:, :QW]+=dot(mixed_ref[...],dmb_ref[...],0,0)
    acc_ref[:, QW:2*QW]+=dot(n1,dq,0,0)
    acc_ref[:, 2*QW:2*QW+2*KW]+=dot(n1,dkv,0,0)
    @pl.when(i==pl.num_programs(0)-1)
    def _():
        pair=jnp.concatenate([small_ref[3:4,:KW],small_ref[3:4,KW:2*KW],jnp.zeros((6,KW),f32)],axis=0).astype(bf16)
        table=jnp.concatenate([small_ref[0:3],dot(pair,spread_ref[...],1,1)[0:2],jnp.zeros((LANES-5,D),f32)],axis=0)
        acc_ref[:, 2*QW+2*KW:]=table.T
        if block:
            for j in range(D//block//2):
                at=pl.multiple_of((2*j+bit_ref[0])*block,16)
                keep_ref[j*block:(j+1)*block]=acc_ref[pl.ds(at,block)].astype(bf16)
                at=pl.multiple_of((2*j+1-bit_ref[0])*block,16)
                send_ref[j*block:(j+1)*block]=acc_ref[pl.ds(at,block)].astype(bf16)
        else:
            keep_ref[...]=acc_ref[:D//2].astype(bf16)
            send_ref[...]=acc_ref[D//2:].astype(bf16)

def finish(bit,dq,own,far,cos,sin,in_set,rows_table,x,n1,dmid,mixed,dmb,spread,gain2,block):
    m,rows,_=x.shape
    full=lambda shape,idx=(0,0): pl.BlockSpec(shape, lambda i: idx)
    blk=lambda w,h=rows: pl.BlockSpec((None,h,w), lambda i:(i,0,0))
    sd=jax.ShapeDtypeStruct
    width=2*QW+2*KW+LANES
    near=len(far[0])
    far=[f for pieces in far for f in pieces]
    return pl.pallas_call(
        functools.partial(finish_kernel,near=near,block=block), grid=(m,),
        in_specs=[pl.BlockSpec(memory_space=pltpu.SMEM),blk(QW),blk(2*KW),blk(LANES),blk(LANES),full((D,2*KW+QW)),full((D,2*KW)),full((8,D)),blk(D),blk(D),blk(D),blk(QW),blk(D),full((D,LANES)),blk(D,8)]+[full((rows,2*KW))]*len(far),
        out_specs=[blk(D),full((D//2,width)),full((D//2,width))],
        out_shape=[sd((m,rows,D),f32),sd((D//2,width),bf16),sd((D//2,width),bf16)],
        scratch_shapes=[pltpu.VMEM((D,width),f32),pltpu.VMEM((8,D),f32),pltpu.VMEM((rows,2*KW),f32)],
        compiler_params=pltpu.CompilerParams(vmem_limit_bytes=LIMIT), cost_estimate=COST,
        name="finish",
    )(bit,dq,own,cos,sin,in_set,in_set,rows_table,x,n1,dmid,mixed,dmb,spread,gain2,*far)

def weights_kernel(left_ref, right_ref, out_ref):
    left=jnp.concatenate([left_ref[k] for k in range(left_ref.shape[0])],axis=1)
    out_ref[...]=dot(left,right_ref[...],1,0).astype(bf16)

def weights(left,which,right,chunk):
    rows,width=right.shape
    return pl.pallas_call(
        weights_kernel, grid=(width//chunk,),
        in_specs=[pl.BlockSpec((None,)+left.shape[1:],lambda j:(which,0,0,0),pipeline_mode=pl.Buffered(1)),pl.BlockSpec((rows,chunk),lambda j:(0,j))],
        out_specs=pl.BlockSpec((D,chunk),lambda j:(0,j)), out_shape=jax.ShapeDtypeStruct((D,width),bf16),
        compiler_params=pltpu.CompilerParams(vmem_limit_bytes=LIMIT), cost_estimate=COST,
        name="weights",
    )(left,right)

def woven_kernel(core_ref, *refs):
    n=len(refs)//3
    mine=refs[:n]; got=refs[n:2*n]; outs=refs[2*n:]
    core=core_ref[0]; j=pl.program_id(0)
    for k in range(n):
        rows=mine[k].shape[0]
        outs[k][pl.ds(pl.multiple_of(core*rows,16),rows)]=mine[k][...]
        outs[k][pl.ds(pl.multiple_of((1-core)*rows,16),rows)]=got[k][...]

def woven(core, mine, got):
    n=len(mine); blocks,rows,_=mine[0].shape
    size=blocks.bit_length()-1
    def turned(j):
        return sum(((j>>k)&1)<<(size-1-k) for k in range(size))
    places=[lambda j:(j,0,0), lambda j:(turned(j),0,0)]
    shapes=[jax.ShapeDtypeStruct((2*blocks*rows,v.shape[2]),v.dtype) for v in mine]
    return pl.pallas_call(
        woven_kernel, grid=(blocks,), in_specs=[pl.BlockSpec(memory_space=pltpu.SMEM)]+[pl.BlockSpec((None,)+v.shape[1:],places[k%n]) for k,v in enumerate(mine+got)],
        out_specs=[pl.BlockSpec((2*rows,v.shape[2]),lambda j:(j,0)) for v in mine], out_shape=shapes,
        compiler_params=pltpu.CompilerParams(vmem_limit_bytes=LIMIT), cost_estimate=COST,
        name="woven",
    )(core,*mine,*got)


LONGEST = 512


def after(values_in, *needed):
    return lax.optimization_barrier((values_in, needed))[0]


theta = 10000.0


def body(
    layer_in,
    doc_ids,
    cotangent,
    first_gain,
    query_weight,
    query_bias,
    key_weight,
    key_bias,
    value_weight,
    value_bias,
    out_weight,
    second_gain,
    gate_weight,
    up_weight,
    down_weight,
):
    ctx = ("zh", "zb")
    dp = ("grp", "core")
    parts = lax.axis_size(ctx)
    rank = lax.axis_index(ctx)
    micros = layer_in.shape[1]
    shard_rows = layer_in.shape[3]
    hidden = gate_weight.shape[1]
    hidden_pad = -(-hidden // (2 * LANES)) * 2 * LANES
    weight_rows = query_weight.shape[0]
    bias_rows = key_bias.shape[0]
    reach_parts = -(-LONGEST // shard_rows)
    core = lax.axis_index("core")
    far_half = lax.axis_index("zh")

    group_rank = lax.axis_index(dp)
    groups = lax.axis_size(dp)
    bits = [1 << k for k in range(groups.bit_length() - 1)]
    block_rows = parts * weight_rows
    even = block_rows % 16 == 0

    def swapped(values_in, bit):
        return lax.ppermute(values_in, dp, [(s, s ^ bit) for s in range(groups)])

    def doubled(blocks, order, k):
        bit = order[k]
        got = swapped(blocks, bit)
        low = (group_rank // bit) % 2 == 0
        return jnp.stack([jnp.where(low, blocks, got), jnp.where(low, got, blocks)])

    def around(values_in, steps):
        return lax.ppermute(values_in, ctx, [(s, (s + steps) % parts) for s in range(parts)])

    def other(values_in, axis):
        return lax.ppermute(values_in, axis, [(0, 1), (1, 0)])

    def corner(values_in):
        return lax.ppermute(values_in, ("core", "zb"), [(s, 3 - s) for s in range(4)])

    def shared(values_in):
        beside = other(values_in, "zb")
        return [values_in, other(values_in, "core"), beside, other(beside, "core")]

    def collected(values_in):
        pieces = [values_in] + [around(values_in, d) for d in range(1, parts)]
        ordered = [pieces[d] for d in range(parts - 1, -1, -1)]
        ordered = jnp.stack(ordered + ordered[:-1])
        taken = lax.dynamic_slice_in_dim(ordered, parts - 1 - rank, parts, 0)
        return taken.reshape((-1,) + values_in.shape[1:])

    def column(values_in):
        return jnp.pad(values_in, (0, weight_rows - values_in.shape[0]))[:, None]

    def wide(values_in):
        return jnp.pad(values_in, ((0, 0), (0, hidden_pad - hidden)))

    own_block = jnp.concatenate([wide(gate_weight), wide(up_weight), wide(down_weight.T)], axis=1)
    own_set = lax.all_gather(own_block, dp, axis=0, tiled=True)
    small = jnp.concatenate(
        [column(v) for v in (first_gain, second_gain, query_bias, key_bias, value_bias)], axis=1
    )
    small = jnp.pad(small, ((0, 0), (0, LANES - small.shape[1])))
    own_attention = jnp.concatenate(
        [out_weight, small, key_weight, value_weight, query_weight], axis=1
    )
    first_block = collected(own_attention)
    row = jnp.arange(D, dtype=jnp.int32)[:, None]
    place = row // weight_rows * bias_rows + row % weight_rows
    spread = (
        (place == jnp.arange(LANES, dtype=jnp.int32)[None, :]) & (row % weight_rows < bias_rows)
    ).astype(bf16)

    docs = doc_ids[0, :, 0]
    own_docs = lax.dynamic_slice_in_dim(docs, rank * shard_rows, shard_rows, 1)
    begins = jnp.sum((docs[:, None, :] < own_docs[:, :, None]).astype(jnp.int32), axis=2)
    row_index = rank * shard_rows + jnp.arange(shard_rows, dtype=jnp.int32)
    positions = row_index[None, :] - begins
    frequency = jnp.power(f32(theta), -(jnp.arange(HEAD // 2, dtype=f32) * (2.0 / HEAD)))
    angle = positions.astype(f32)[:, :, None] * frequency
    cosines, sines = jnp.cos(angle), jnp.sin(angle)
    cosines = jnp.concatenate([cosines] * (2 * LANES // HEAD), axis=2)
    sines = jnp.concatenate([-sines, sines] * (LANES // HEAD), axis=2)
    base = (rank * shard_rows).reshape(1)

    own_block, first_block = after((own_block, first_block))
    cut = QW + LANES
    firsts = [first_block[:, :cut], first_block[:, cut:]]
    gather_orders = [bits[1:] + bits[:1], bits[:0:-1] + bits[:1]]
    widths = own_block.shape[1] // LANES // 4 * LANES
    edges = [0, widths, own_block.shape[1] - widths, own_block.shape[1]]
    other_block = []
    upstream = [cotangent[0, m, 0] for m in range(micros)]
    crossed = []
    for k in range(len(bits)):
        if k < len(bits) - 1 or not even:
            firsts = [doubled(side, order, k) for side, order in zip(firsts, gather_orders)]
        else:
            gots = [swapped(side, 1) for side in firsts]
            firsts = [firsts, gots]
        if k < 3:
            other_block.append(other(own_block[:, edges[k] : edges[k + 1]], "zh"))
        if k == 1:
            crossed.append(other(upstream[0], "zb"))
        firsts, other_block, own_block, spread, cosines, sines, begins, upstream, crossed = after(
            (firsts, other_block, own_block, spread, cosines, sines, begins, upstream, crossed)
        )
    other_set = lax.all_gather(jnp.concatenate(other_block, axis=1), dp, axis=0, tiled=True)
    if even:
        firsts, gots = ([v.reshape((-1,) + v.shape[-2:]) for v in part] for part in firsts)
        out_set, in_set = woven(core.reshape(1), firsts, gots)
    else:
        out_set, in_set = (
            jnp.transpose(
                side, [list(reversed(order)).index(bit) for bit in reversed(bits)] + [-2, -1]
            ).reshape(-1, side.shape[-1])
            for side, order in zip(firsts, gather_orders)
        )
    sets = (own_set, other_set)
    own_quarter = (core == far_half).astype(jnp.int32).reshape(1)

    tokens = layer_in[0, :, 0]
    rot_query, pairs, normed_one, rows_table = project(
        tokens, out_set, in_set, spread, cosines, sines
    )
    def earlier(pair):
        return [pair] + [
            lax.ppermute(pair, ctx, [(s, s + d) for s in range(parts - d)])
            for d in range(1, reach_parts + 1)
        ]

    kvs = [earlier(pairs[0])]
    rot_query, pairs[1:] = after((rot_query, pairs[1:]))
    kvs += [earlier(pair) for pair in pairs[1:]]

    begins = begins[:, None, :]
    exchanged = []
    held = ()
    for m in range(micros):
        normed_two, *held = attend(
            m, base, rot_query, kvs[m], begins, out_set, tokens, rows_table, held
        )
        if m == 0:
            upstream, crossed, normed_two, kvs[1:] = after((upstream, crossed, normed_two, kvs[1:]))
        exchanged.append([normed_two, other(normed_two, "core"), other(normed_two, "zb")])
        if m == 0:
            crossed += [other(u, "zb") for u in upstream[1:]]
            upstream_pieces = [[u, other(u, "core"), v] for u, v in zip(upstream, crossed)]
    exchanged[-1].append(corner(normed_two))
    exchanged[:-1], upstream_pieces[0], exchanged[-1][0] = after(
        (exchanged[:-1], upstream_pieces[0], normed_two)
    )
    for early in exchanged[:-1] + upstream_pieces[:1]:
        early.append(other(early[2], "core"))
    mixed, middle, log_sums = held

    backs = []
    before = ()
    for m in range(micros):
        back, before = feed(
            own_quarter, exchanged[m], upstream_pieces[m], sets, m, micros, before
        )
        if m < micros - 1:
            back, upstream_pieces[m + 1] = after((back, upstream_pieces[m + 1]))
            upstream_pieces[m + 1].append(other(upstream_pieces[m + 1][2], "core"))
        backs.append([back[0], other(back[1], "core"), other(back[2], "zb"), corner(back[3])])
    partials = before[:4]
    out_near = other(partials[1], "core")
    out_far = other(partials[3], "core")

    left, pair, act = after(before[4:], backs[0])
    feed_down = weights(left, 1, act, 256)
    backs[-1][1:3], left, pair, feed_down = after((backs[-1][1:3], left, pair, feed_down))
    feed_pair = weights(left, 0, pair, 256)
    backs, feed_pair, out_near, out_far = after((backs, feed_pair, out_near, out_far))
    feed_down = lax.psum_scatter(feed_down, "grp", scatter_dimension=0, tiled=True)
    feed_pair = lax.psum_scatter(feed_pair, "grp", scatter_dimension=0, tiled=True)

    far = []
    ended = ()
    out_beside = []
    for m in range(micros):
        out_sum = (partials[2][m].astype(f32) + out_far[m].astype(f32)).astype(bf16)
        out_beside.append(other(out_sum, "zb"))
        far1, far2, *ended = attend_back(
            m, base, rot_query, kvs[m], begins, out_set, rows_table, log_sums, middle, cotangent[0, :, 0],
            backs[m], cosines, sines, ended,
        )
        far1, far2, ended, out_beside = after((far1, far2, ended, out_beside))
        far.append(
            [
                lax.ppermute(part, ctx, [(s, s - d) for s in range(d, parts)])
                for d, part in ((1, far1), (2, far2))
            ]
        )
        if m < micros - 1:
            out_far, ended = after((out_far, ended))
    def portion(half, k):
        return lax.dynamic_index_in_dim(
            half.reshape((2, -1) + half.shape[1:]), (core + far_half + k) % 2, 0, keepdims=False
        )

    def handed(part, k):
        return lax.ppermute(
            part, ("core", "zh"), [(2 * s + a, 2 * (s ^ a ^ k) + s) for s in range(2) for a in range(2)]
        )

    def delivered(half, k):
        return handed(portion(half, k), k)

    down_parts = [portion(feed_down, k) for k in range(2)]
    far, down_parts = after((far, down_parts))
    down_parts = [handed(part, k) for k, part in enumerate(down_parts)]
    grad_middle, branch_low, query_grad, own_pair, gain_sum = ended
    input_grad, keep, send = finish(
        (group_rank % 2).reshape(1), query_grad, own_pair, far, cosines, sines, in_set,
        rows_table, tokens, normed_one, grad_middle, mixed, branch_low, spread, gain_sum,
        block_rows if even else 0,
    )
    keep, send, down_parts = after((keep, send, down_parts))
    if not even:
        both = jnp.concatenate([keep, send]).reshape(groups // 2, 2, block_rows, -1)
        keep, send = (
            lax.dynamic_index_in_dim(both, v, 1, keepdims=False)
            for v in (group_rank % 2, 1 - group_rank % 2)
        )

    def halved(blocks, order, k):
        bit = order[k]
        size = blocks.shape[0]
        at = sorted(order[k:]).index(bit)
        view = blocks.reshape((size >> (at + 1), 2, 1 << at) + blocks.shape[1:])
        own = (group_rank // bit) % 2
        kept = lax.dynamic_index_in_dim(view, own, 1, keepdims=False)
        sent = lax.dynamic_index_in_dim(view, 1 - own, 1, keepdims=False)
        got = swapped(sent.astype(bf16), bit)
        return (kept.astype(f32) + got.astype(f32)).reshape((size // 2,) + blocks.shape[1:])

    blocks = keep.astype(f32) + swapped(send, 1).astype(f32)
    blocks = blocks.reshape(groups // 2, block_rows, -1)
    cut = QW + 2 * LANES
    sides = [blocks[:, :, :cut], blocks[:, :, cut:]]
    orders = [bits[1:], bits[:0:-1]]
    pair_parts = [delivered(feed_pair, 0)]
    for k in range(len(bits) - 1):
        sides = [halved(side, order, k) for side, order in zip(sides, orders)]
        if k == len(bits) - 3:
            sides, pair_parts, feed_pair = after((sides, pair_parts, feed_pair))
            pair_parts.append(delivered(feed_pair, 1))
    sides, down_parts = after((sides, down_parts))
    attention_block = jnp.concatenate([side[0] for side in sides], axis=1).astype(bf16)
    attention_block = attention_block.reshape(parts, weight_rows, -1)

    def block_for(steps):
        return lax.dynamic_index_in_dim(
            attention_block, (rank + steps) % parts, 0, keepdims=False
        )

    ends = [around(block_for(d), d) for d in range(1, parts)]
    ends, pair_parts = after((ends, pair_parts))
    sums = block_for(0).astype(f32)
    for end in ends:
        sums = sums + end.astype(f32)

    pair_sum = pair_parts[0].astype(f32) + pair_parts[1].astype(f32)
    down_sum = down_parts[0].astype(f32) + down_parts[1].astype(f32)

    total = middle + partials[0] + out_near.astype(f32) + jnp.stack(out_beside).astype(f32)

    edge = 2 * QW + 2 * KW
    return (
        total.astype(bf16)[None, :, None],
        input_grad[None, :, None],
        sums[:, edge],
        sums[:, QW : 2 * QW],
        sums[:, edge + 2],
        sums[:, 2 * QW : 2 * QW + KW],
        sums[:bias_rows, edge + 3],
        sums[:, 2 * QW + KW : edge],
        sums[:bias_rows, edge + 4],
        sums[:, :QW],
        sums[:, edge + 1],
        pair_sum[:, :hidden],
        pair_sum[:, hidden_pad : hidden_pad + hidden],
        down_sum[:, :hidden].T,
    )


def solution(mesh):
    groups, parts = mesh.devices.shape
    split = jax.sharding.Mesh(
        mesh.devices.reshape(groups // 2, 2, parts // 2, 2), ("grp", "core", "zh", "zb")
    )
    dp = ("grp", "core")
    ctx = ("zh", "zb")
    rows = P(dp + ctx, None)
    line = P(dp + ctx)
    tokens = P(dp, None, None, ctx, None)
    up = P(dp, ctx)
    return jax.shard_map(
        body,
        mesh=split,
        in_specs=(
            tokens, P(dp, None, None, None), tokens, line, rows, line, rows, line, rows, line,
            rows, line, up, up, P(ctx, dp),
        ),
        out_specs=(
            tokens, tokens, line, rows, line, rows, line, rows, line, rows, line,
            up, up, P(ctx, dp),
        ),
        check_vma=False,
    )
```
